256 devices in a mesh: outer: 8 (over x, y_lo), inner: 8 (over z), tensor: 4 (over y_hi, core).
Axes of the slice: x: 4, y: 4 (y_hi: 2, y_lo: 2; y = y_hi * 2 + y_lo), z: 8, core: 2. Of those that a mesh axis runs over, the one named last changes fastest.
Arguments:
- queries: bfloat16 [16384, 16, 128], P(('outer', 'inner'), 'tensor'), may hold values from -5 to 5
- keys: bfloat16 [16384, 4, 128], P(('outer', 'inner'), 'tensor'), may hold values from -5 to 5
- values: bfloat16 [16384, 4, 128], P(('outer', 'inner'), 'tensor'), may hold values from -6 to 6
- w_out: bfloat16 [16, 128, 4096], P('tensor'), may hold values from -0.125 to 0.125
- d_out: bfloat16 [16384, 4096], P(('outer', 'inner', 'tensor')), may hold values from -6 to 6
- lengths: int32 [16], replicated, may hold values from 1 to 10240, 16384 in all
Outputs:
- mixed: bfloat16 [16384, 4096], P(('outer', 'inner', 'tensor'))
- d_queries: bfloat16 [16384, 16, 128], P(('outer', 'inner'), 'tensor')
- d_keys: bfloat16 [16384, 4, 128], P(('outer', 'inner'), 'tensor')
- d_values: bfloat16 [16384, 4, 128], P(('outer', 'inner'), 'tensor')
The draws below stay inside these ranges and needn't reach their ends.
Inputs may be any that keep to these rules, and one draw needn't show every extreme that they name: `lengths`: the 16 documents fill the sequence of 16384 tokens exactly, and the longest has exactly 10240 tokens.
All inputs are finite; a program needn't handle non-finite values.
Results may differ from the reference program's by a relative error of at most 0.04.
Values may be sent and summed in bfloat16 or wider, within the bound.
A program may use at most 128 MiB of HBM per device.

```python
import math
import jax
import jax.numpy as jnp
import numpy as np
from jax import lax

D = 4096
HD = 128
HEADS = 16
KV_HEADS = 4
DOCS = 16
TOKENS = 16384
MOST_DOC = 10240


def drawn_pair(key):
    base_q = jnp.clip(jax.random.normal(jax.random.fold_in(key, 11), (TOKENS, HEADS, HD), jnp.float32), -5.0, 5.0)
    base_k = jnp.clip(jax.random.normal(jax.random.fold_in(key, 12), (TOKENS, KV_HEADS, HD), jnp.float32), -5.0, 5.0)
    return (base_q, base_k)


def draw_queries(key, part):
    return drawn_pair(key)[0].astype(jnp.bfloat16)


def draw_keys(key, part):
    return drawn_pair(key)[1].astype(jnp.bfloat16)


def levels(rng, shape, cuts, smallest, largest):
    def one(dim, shards_of):
        draws = jax.random.uniform(jax.random.fold_in(jax.random.fold_in(rng, 6), dim), (shards_of,), jnp.float32, smallest / len(cuts), largest / len(cuts))
        return jnp.repeat(jnp.exp(draws), shape[dim] // shards_of).reshape((-1,) + (1,) * (len(shape) - dim - 1))

    level = one(*cuts[0])
    for cut in cuts[1:]:
        level = level * one(*cut)
    return level


def length_profile(number_of, total, limit, lean):
    loads = [(1 << 20) // math.isqrt(standing ** lean) + 1 for standing in range(2, number_of + 1)]
    surplus, given = total - limit - (number_of - 1), [1] * (number_of - 1)
    while surplus > 0:
        free = [i for i in range(number_of - 1) if given[i] < limit]
        pool, remaining = sum([loads[i] for i in free]), surplus
        for i in free:
            more = min(limit - given[i], max(1, remaining * loads[i] // pool), surplus)
            given[i] = given[i] + more
            surplus = surplus - more
    return np.array([limit] + given)


def ragged_sizes(stream_key, number_of, total, most, slope):
    if number_of == 2:
        one = jax.random.randint(stream_key, (), max(1, total - most), min(most, total - 1) + 1)
        return jnp.stack([one, total - one])
    sizes = jnp.asarray(length_profile(number_of, total, most, slope), jnp.int32)
    couples = (number_of - 1) // 2
    source_of, taker = sizes[1:1 + 2 * couples:2], sizes[2:2 + 2 * couples:2]
    slack = jnp.minimum(source_of - 1, most - taker)
    shifted = jax.random.randint(jax.random.fold_in(stream_key, 1), (couples,), 0, 1 << 20) % (slack + 1)
    sizes = sizes.at[1:1 + 2 * couples:2].set(source_of - shifted).at[2:2 + 2 * couples:2].set(taker + shifted)
    return sizes[jax.random.permutation(jax.random.fold_in(stream_key, 2), number_of)]


def scatter_about(rng, dims, scale, reach, pieces=(), held_as=jnp.bfloat16):
    values = scale * jax.random.normal(rng, dims, jnp.float32)
    if pieces:
        values = values * levels(rng, dims, pieces, -0.22, 0.18)
    return jnp.clip(values, -reach, reach).astype(held_as)


def setup_inputs(seed: int = 0) -> dict:
    key_list = jax.random.split(jax.random.key(seed), 7)
    queries = draw_queries(jax.random.fold_in(key_list[6], 71), 0)
    keys = draw_keys(jax.random.fold_in(key_list[6], 71), 0)
    values = scatter_about(key_list[2], (TOKENS, KV_HEADS, HD), 1.0, 6.0, ((0, 64), (1, 4)))
    w_out = scatter_about(key_list[3], (HEADS, HD, D), (HEADS * HD) ** -0.5, 0.125, ((0, 4),))
    d_out = scatter_about(key_list[4], (TOKENS, D), 1.0, 6.0, ((0, 256),))
    lengths = ragged_sizes(key_list[5], DOCS, TOKENS, MOST_DOC, 2).astype(jnp.int32)
    return dict(queries=queries, keys=keys, values=values, w_out=w_out, d_out=d_out, lengths=lengths)


NEG_FILL = -1e30


def segment_of(positions, ends):
    return jnp.sum((positions[:, None] >= ends[None, :]).astype(jnp.int32), axis=1)


def doc_begin(position, ends):
    return jnp.max(jnp.where(ends <= position, ends, jnp.zeros_like(ends)))


def masked_scores(q_rows, k_block, q_pos, q_seg, k_start, ends, scale):
    width = k_block.shape[0]
    k_pos = k_start + jnp.arange(width, dtype=jnp.int32)
    k_seg = segment_of(k_pos, ends)
    s = lax.dot_general(q_rows, k_block, (((1,), (1,)), ((), ())), preferred_element_type=jnp.float32) * scale
    mask = (k_pos[None, :] <= q_pos[:, None]) & (k_seg[None, :] == q_seg[:, None])
    return jnp.where(mask, s, NEG_FILL), mask


def reference(queries, keys, values, w_out, d_out, lengths):
    group = HEADS // KV_HEADS
    scale = HD ** -0.5
    ends = jnp.cumsum(lengths).astype(jnp.int32)
    w_flat = w_out.reshape(HEADS * HD, D)
    d_attn = lax.dot_general(d_out, w_flat, (((1,), (1,)), ((), ())), preferred_element_type=jnp.float32).astype(jnp.bfloat16)
    span = math.gcd(512, TOKENS)
    n_blocks = TOKENS // span
    rows = span * group
    q_heads = queries.reshape(TOKENS, KV_HEADS, group, HD).transpose(1, 0, 2, 3).reshape(KV_HEADS, TOKENS * group, HD)
    g_heads = d_attn.reshape(TOKENS, KV_HEADS, group, HD).transpose(1, 0, 2, 3).reshape(KV_HEADS, TOKENS * group, HD)
    k_heads = keys.transpose(1, 0, 2)
    v_heads = values.transpose(1, 0, 2)

    def one_head(operands):
        q_all, g_all, k_all, v_all = operands

        def query_block(carry, index):
            dk_acc, dv_acc = carry
            q_start = (index * span).astype(jnp.int32)
            q_rows = lax.dynamic_slice_in_dim(q_all, q_start * group, rows, 0)
            g_rows = lax.dynamic_slice_in_dim(g_all, q_start * group, rows, 0)
            q_pos = q_start + jnp.arange(rows, dtype=jnp.int32) // group
            q_seg = segment_of(q_pos, ends)
            first = doc_begin(q_start, ends)
            last = q_start + span - 1

            def needed(b):
                k_start = b * span
                return (k_start <= last) & (k_start + span - 1 >= first)

            def scores_at(b):
                k_start = (b * span).astype(jnp.int32)
                k_block = lax.dynamic_slice_in_dim(k_all, k_start, span, 0)
                return masked_scores(q_rows, k_block, q_pos, q_seg, k_start, ends, scale)

            def stats(b, state):
                def work(st):
                    top, denom = st
                    s, mask = scores_at(b)
                    new_top = jnp.maximum(top, jnp.max(s, axis=1))
                    weights = jnp.where(mask, jnp.exp(s - new_top[:, None]), jnp.float32(0.0))
                    return new_top, denom * jnp.exp(top - new_top) + jnp.sum(weights, axis=1)
                return lax.cond(needed(b), work, lambda st: st, state)

            top, denom = lax.fori_loop(0, n_blocks, stats, (jnp.full((rows,), NEG_FILL, jnp.float32), jnp.zeros((rows,), jnp.float32)))
            lse = top + jnp.log(denom)

            def probs_at(b):
                s, mask = scores_at(b)
                return jnp.where(mask, jnp.exp(s - lse[:, None]), jnp.float32(0.0))

            def outputs(b, acc):
                def work(a):
                    v_block = lax.dynamic_slice_in_dim(v_all, (b * span).astype(jnp.int32), span, 0)
                    return a + jnp.dot(probs_at(b).astype(jnp.bfloat16), v_block, preferred_element_type=jnp.float32)
                return lax.cond(needed(b), work, lambda a: a, acc)

            out = lax.fori_loop(0, n_blocks, outputs, jnp.zeros((rows, HD), jnp.float32)).astype(jnp.bfloat16)
            delta = jnp.sum(g_rows.astype(jnp.float32) * out.astype(jnp.float32), axis=1)

            def grads(b, state):
                def work(st):
                    dq, dka, dva = st
                    k_start = (b * span).astype(jnp.int32)
                    k_block = lax.dynamic_slice_in_dim(k_all, k_start, span, 0)
                    v_block = lax.dynamic_slice_in_dim(v_all, k_start, span, 0)
                    probs = probs_at(b)
                    dv = lax.dot_general(probs.astype(jnp.bfloat16), g_rows, (((0,), (0,)), ((), ())), preferred_element_type=jnp.float32)
                    dp = lax.dot_general(g_rows, v_block, (((1,), (1,)), ((), ())), preferred_element_type=jnp.float32)
                    ds = (probs * (dp - delta[:, None])).astype(jnp.bfloat16)
                    dq = dq + jnp.dot(ds, k_block, preferred_element_type=jnp.float32) * scale
                    dk = lax.dot_general(ds, q_rows, (((0,), (0,)), ((), ())), preferred_element_type=jnp.float32) * scale
                    zero = jnp.zeros((), jnp.int32)
                    dka = lax.dynamic_update_slice(dka, lax.dynamic_slice_in_dim(dka, k_start, span, 0) + dk, (k_start, zero))
                    dva = lax.dynamic_update_slice(dva, lax.dynamic_slice_in_dim(dva, k_start, span, 0) + dv, (k_start, zero))
                    return dq, dka, dva
                return lax.cond(needed(b), work, lambda st: st, state)

            dq, dk_acc, dv_acc = lax.fori_loop(0, n_blocks, grads, (jnp.zeros((rows, HD), jnp.float32), dk_acc, dv_acc))
            return (dk_acc, dv_acc), (out, dq)

        init = (jnp.zeros((TOKENS, HD), jnp.float32), jnp.zeros((TOKENS, HD), jnp.float32))
        (dk_acc, dv_acc), (outs, dqs) = lax.scan(query_block, init, jnp.arange(n_blocks, dtype=jnp.int32))
        return outs.reshape(TOKENS * group, HD), dqs.reshape(TOKENS * group, HD), dk_acc, dv_acc

    outs, dqs, dks, dvs = lax.map(one_head, (q_heads, g_heads, k_heads, v_heads))
    attn = outs.reshape(KV_HEADS, TOKENS, group, HD).transpose(1, 0, 2, 3).reshape(TOKENS, HEADS * HD)
    mixed = jnp.dot(attn, w_flat, preferred_element_type=jnp.float32).astype(jnp.bfloat16)
    d_queries = dqs.reshape(KV_HEADS, TOKENS, group, HD).transpose(1, 0, 2, 3).reshape(TOKENS, HEADS, HD).astype(jnp.bfloat16)
    d_keys = dks.transpose(1, 0, 2).astype(jnp.bfloat16)
    d_values = dvs.transpose(1, 0, 2).astype(jnp.bfloat16)
    return (mixed, d_queries, d_keys, d_values)
```

```python
import jax
import jax.numpy as jnp
from jax import lax
from jax.experimental import pallas as pl
from jax.experimental.pallas import tpu as pltpu
from jax.sharding import PartitionSpec as P

MESH = pl.DeviceIdType.MESH
NT = (((1,), (1,)), ((), ()))
NN = (((1,), (0,)), ((), ()))
TN = (((0,), (0,)), ((), ()))
F32, BF16 = jnp.float32, jnp.bfloat16
LOG2E = 1.4426950408889634
LOW, FLOOR = -1e30, -1e20
VMEM, ANY, SMEM = pltpu.VMEM, pl.ANY, pltpu.SMEM

NX, NY, NZ = 4, 2, 8
TOK = 256
SUB = TOK // NX
GROUP = 4
ROWS = TOK * GROUP
HD = 128
SHARDS = NX * NY * NZ
TILE = 256
RUNS = TILE // SUB
CHUNK = 256
SCALE = HD**-0.5


def place():
    outer, z, t = lax.axis_index("outer"), lax.axis_index("inner"), lax.axis_index("tensor")
    return outer // NY, outer % NY, z, t


def at(x, y, z, t):
    return {"outer": x * NY + y, "inner": z, "tensor": t}


def remote(src, dst, send, recv, device):
    return pltpu.make_async_remote_copy(
        src_ref=src, dst_ref=dst, send_sem=send, recv_sem=recv, device_id=device, device_id_type=MESH
    )


def meet(devices):
    barrier = pltpu.get_barrier_semaphore()
    for device in devices:
        pl.semaphore_signal(barrier, inc=1, device_id=device, device_id_type=MESH)
    pl.semaphore_wait(barrier, len(devices))


PLANE = [(dx, dy) for dy in range(NY) for dx in range(NX) if (dx, dy) != (0, 0)]


def gather_kernel(q, kv, do, qa, kva, doa, qs, qr, ks, kr, zs, zr, ds, dr, ls):
    x, y, z, t = place()
    right, left = (x + 1) % NX, (x + NX - 1) % NX
    up, down = (z + 1) % NZ, (z + NZ - 1) % NZ
    partner, far = t + 1 - 2 * (t % 2), (t + 2) % 4
    meet(
        [at((x + dx) % NX, (y + dy) % NY, z, t) for dx, dy in PLANE]
        + [at(x, y, up, t), at(x, y, down, t), at(x, y, z, partner), at(x, y, z, far)]
    )
    plane, landed = [], []
    for i, (dx, dy) in enumerate(PLANE):
        tx, ty = (x + dx) % NX, (y + dy) % NY
        fx, fy = (x + NX - dx) % NX, (y + NY - dy) % NY
        copy = remote(kv.at[:, tx], kva.at[:, x, y, z], ks.at[i], kr.at[i], at(tx, ty, z, t))
        copy.start()
        plane.append(copy)
        landed.append(remote(kv.at[:, tx], kva.at[:, fx, fy, z], ks.at[i], kr.at[i], at(tx, ty, z, t)))
    own_kv = pltpu.make_async_copy(kv.at[:, x], kva.at[:, x, y, z], ls.at[0])
    own_kv.start()
    far_do = remote(do, doa.at[t], ds.at[0], dr.at[0], at(x, y, z, far))
    near_do = remote(do, doa.at[t], ds.at[1], dr.at[1], at(x, y, z, partner))
    far_do.start()
    near_do.start()
    to_right = remote(q, qa.at[1], qs.at[0], qr.at[0], at(right, y, z, t))
    to_left = remote(q, qa.at[3], qs.at[1], qr.at[1], at(left, y, z, t))
    to_right.start()
    to_left.start()
    own_do = pltpu.make_async_copy(do, doa.at[t], ls.at[1])
    own_do.start()
    own_q = pltpu.make_async_copy(q, qa.at[0], ls.at[2])
    own_q.start()
    own_kv.wait()
    for copy in landed:
        copy.wait_recv()
    streams = [(0, 0, 4), (1, 1, 4), (0, 1, 3), (1, 0, 3)]
    sent = []

    def hop(step):
        for i, (half, way, hops) in enumerate(streams):
            if step < hops:
                block = (z + NZ - step) % NZ if way == 0 else (z + step) % NZ
                part = kva.at[half, :, :, block]
                copy = remote(part, part, zs.at[i, step], zr.at[i, step], at(x, y, up if way == 0 else down, t))
                copy.start()
                sent.append(copy)

    def arrive(step):
        for i, (half, way, hops) in enumerate(streams):
            if step < hops:
                block = (z + NZ - step - 1) % NZ if way == 0 else (z + step + 1) % NZ
                part = kva.at[half, :, :, block]
                remote(
                    part, part, zs.at[i, step], zr.at[i, step], at(x, y, up if way == 0 else down, t)
                ).wait_recv()

    hop(0)
    half = ROWS // 2
    to_right.wait_recv()
    on_right = remote(
        qa.at[1, 0:half], qa.at[2, 0:half], qs.at[2], qr.at[2], at(right, y, z, t)
    )
    on_right.start()
    to_left.wait_recv()
    on_left = remote(
        qa.at[3, half:ROWS], qa.at[2, half:ROWS], qs.at[3], qr.at[3], at(left, y, z, t)
    )
    on_left.start()
    for step in range(3):
        arrive(step)
        hop(step + 1)
    remote(do, doa.at[far], ds.at[0], dr.at[0], at(x, y, z, far)).wait_recv()
    on_do = remote(doa.at[far], doa.at[far], ds.at[2], dr.at[2], at(x, y, z, partner))
    on_do.start()
    arrive(3)
    on_right.wait_recv()
    on_left.wait_recv()
    remote(do, doa.at[partner], ds.at[1], dr.at[1], at(x, y, z, partner)).wait_recv()
    other = (partner + 2) % 4
    remote(doa.at[other], doa.at[other], ds.at[2], dr.at[2], at(x, y, z, partner)).wait_recv()
    for copy in plane + sent + [far_do, near_do, to_right, to_left, on_right, on_left, on_do]:
        copy.wait_send()
    own_do.wait()
    own_q.wait()


def gather(q, kv, do):
    dma = pltpu.SemaphoreType.DMA
    return pl.pallas_call(
        gather_kernel,
        out_shape=(
            jax.ShapeDtypeStruct((NX, ROWS, HD), BF16),
            jax.ShapeDtypeStruct((2, NX, NY, NZ, SUB, HD), BF16),
            jax.ShapeDtypeStruct((4, *do.shape), BF16),
        ),
        in_specs=[pl.BlockSpec(memory_space=VMEM)] * 3,
        out_specs=(pl.BlockSpec(memory_space=ANY),) * 3,
        scratch_shapes=[
            dma((4,)), dma((4,)), dma((7,)), dma((7,)), dma((4, 4)), dma((4, 4)), dma((3,)), dma((3,)), dma((3,)),
        ],
        compiler_params=pltpu.CompilerParams(collective_id=0, has_side_effects=True),
        name="gather",
    )(q, kv, do)


def swap_kernel(st, ox, sta, oxa, ss, sr, os_, or_):
    x, y, z, t = place()
    meet([at((x + dx) % NX, y, z, t) for dx in range(1, NX)])
    copies = []
    for e in range(1, NX):
        to = at((x + NX - e) % NX, y, z, t)
        copies.append(remote(st, sta.at[e], ss.at[e], sr.at[e], to))
        copies.append(remote(ox.at[e], oxa.at[e], os_.at[e], or_.at[e], to))
    for copy in copies:
        copy.start()
    for copy in copies:
        copy.wait_recv()
    for copy in copies:
        copy.wait_send()


def swap(st, ox):
    dma = pltpu.SemaphoreType.DMA
    return pl.pallas_call(
        swap_kernel,
        out_shape=(jax.ShapeDtypeStruct((NX, *st.shape), st.dtype), jax.ShapeDtypeStruct(ox.shape, BF16)),
        in_specs=[pl.BlockSpec(memory_space=VMEM), pl.BlockSpec(memory_space=ANY)],
        out_specs=(pl.BlockSpec(memory_space=ANY),) * 2,
        scratch_shapes=[dma((4,))] * 4,
        compiler_params=pltpu.CompilerParams(collective_id=1, has_side_effects=True),
        name="swap",
    )(st, ox)


def reduce_kernel(dq, g, mix, dqa, kvp, m_near, m_far, b0, b1, b2, b3, total, m_sum,
                  qs, qr, zs, zr, ks, kr, ms, mr, ls):
    x, y, z, t = place()
    up, down = (z + 1) % NZ, (z + NZ - 1) % NZ
    partner, far = t + 1 - 2 * (t % 2), (t + 2) % 4
    meet(
        [at((x + dx) % NX, (y + dy) % NY, z, t) for dx, dy in PLANE]
        + [at(x, y, up, t), at(x, y, down, t), at(x, y, z, partner), at(x, y, z, far)]
    )
    sent = []

    def send(copy):
        copy.start()
        sent.append(copy)
        return copy

    streams = [(0, 0, 4, b0), (1, 1, 4, b1), (0, 1, 3, b2), (1, 0, 3, b3)]

    def hop(step):
        for i, (half, way, hops, buf) in enumerate(streams):
            if step < hops:
                away = hops - step
                block = (z + away) % NZ if way == 0 else (z + NZ - away) % NZ
                src = g.at[half, :, :, block]
                if step > 0:
                    remote(buf.at[step - 1], buf.at[step - 1], zs.at[i, step - 1], zr.at[i, step - 1],
                           at(x, y, up if way == 0 else down, t)).wait_recv()
                    buf[step - 1] = (buf[step - 1].astype(F32) + g[half, :, :, block].astype(F32)).astype(BF16)
                    src = buf.at[step - 1]
                send(remote(src, buf.at[step], zs.at[i, step], zr.at[i, step],
                            at(x, y, up if way == 0 else down, t)))

    hop(0)
    other = (partner + 2) % 4
    near = [
        send(remote(mix.at[partner], m_near.at[0], ms.at[0], mr.at[0], at(x, y, z, partner))),
        send(remote(mix.at[other], m_near.at[1], ms.at[1], mr.at[1], at(x, y, z, partner))),
    ]
    queries = [
        send(remote(dq.at[e], dqa.at[e], qs.at[e], qr.at[e], at((x + NX - e) % NX, y, z, t)))
        for e in range(1, NX)
    ]
    near[1].wait_recv()
    m_sum[...] = (mix[far].astype(F32) + m_near[1].astype(F32)).astype(BF16)
    away = send(remote(m_sum, m_far, ms.at[2], mr.at[2], at(x, y, z, far)))
    for step in range(1, 4):
        hop(step)
    for i, (half, way, hops, buf) in enumerate(streams):
        remote(buf.at[hops - 1], buf.at[hops - 1], zs.at[i, hops - 1], zr.at[i, hops - 1],
               at(x, y, up if way == 0 else down, t)).wait_recv()
    total[0] = (b0[3].astype(F32) + b2[2].astype(F32) + g[0, :, :, z].astype(F32)).astype(BF16)
    total[1] = (b1[3].astype(F32) + b3[2].astype(F32) + g[1, :, :, z].astype(F32)).astype(BF16)
    landed = []
    for i, (dx, dy) in enumerate(PLANE):
        tx, ty = (x + dx) % NX, (y + dy) % NY
        fx, fy = (x + NX - dx) % NX, (y + NY - dy) % NY
        send(remote(total.at[:, tx, ty], kvp.at[:, x, y], ks.at[i], kr.at[i], at(tx, ty, z, t)))
        landed.append(remote(total.at[:, tx, ty], kvp.at[:, fx, fy], ks.at[i], kr.at[i], at(tx, ty, z, t)))
    own = pltpu.make_async_copy(total.at[:, x, y], kvp.at[:, x, y], ls.at[0])
    own.start()
    for copy in queries + [near[0], away] + landed:
        copy.wait_recv()
    for copy in sent:
        copy.wait_send()
    own.wait()


def reduce(dq, g, mix):
    dma = pltpu.SemaphoreType.DMA
    width = mix.shape[2]
    block = (NX, NY, SUB, HD)
    return pl.pallas_call(
        reduce_kernel,
        out_shape=(
            jax.ShapeDtypeStruct(dq.shape, BF16),
            jax.ShapeDtypeStruct((2, *block), BF16),
            jax.ShapeDtypeStruct((2, 64, width), BF16),
            jax.ShapeDtypeStruct((64, width), BF16),
        ),
        in_specs=[pl.BlockSpec(memory_space=ANY)] + [pl.BlockSpec(memory_space=VMEM)] * 2,
        out_specs=(
            pl.BlockSpec(memory_space=ANY), pl.BlockSpec(memory_space=ANY),
            pl.BlockSpec(memory_space=VMEM), pl.BlockSpec(memory_space=ANY),
        ),
        scratch_shapes=[
            pltpu.VMEM((4, *block), BF16), pltpu.VMEM((4, *block), BF16),
            pltpu.VMEM((3, *block), BF16), pltpu.VMEM((3, *block), BF16),
            pltpu.VMEM((2, *block), BF16), pltpu.VMEM((64, width), BF16),
            dma((4,)), dma((4,)), dma((4, 4)), dma((4, 4)), dma((7,)), dma((7,)), dma((3,)), dma((3,)), dma((1,)),
        ],
        compiler_params=pltpu.CompilerParams(
            collective_id=2, has_side_effects=True, vmem_limit_bytes=60 << 20
        ),
        name="reduce",
    )(dq, g, mix)


def begin_of(position, lengths):
    end, first = jnp.int32(0), jnp.zeros_like(position)
    for j in range(lengths.shape[0]):
        end = end + lengths[j]
        first = jnp.where(position >= end, end, first)
    return first


def tiles_of(r, x, y, z, lengths):
    s = ((x + NX - r) % NX) * (NY * NZ) + y * NZ + z
    start = s * TOK
    f = begin_of(start, lengths) // TOK
    q_pos = start + lax.broadcasted_iota(jnp.int32, (1, ROWS), 1) // GROUP
    low = begin_of(q_pos, lengths)
    low_most = begin_of(start + TOK - 1, lengths)
    count = (s - f) // RUNS + 1

    def tile(i):
        want = f + RUNS * i
        a = jnp.minimum(want, SHARDS - RUNS)
        base = a * TOK + x * SUB
        whole = (a == want) & (base >= low_most) & (base + (RUNS - 1) * TOK + SUB - 1 <= start)
        return a, base, want * TOK, whole

    return count, tile, q_pos, low


def seen(base, floor, q_pos, low, cols):
    i = lax.broadcasted_iota(jnp.int32, (TILE, CHUNK), 0)
    k_pos = base + i + (i // SUB) * (TOK - SUB)
    return (k_pos >= jnp.maximum(low[:, cols], floor)) & (k_pos <= q_pos[:, cols])


def forward_kernel(lengths, q, kv, out, ml, m, l, acc):
    x, y, z, _ = place()

    def shard(r, _):
        count, tile, q_pos, low = tiles_of(r, x, y, z, lengths)
        m[...] = jnp.full(m.shape, FLOOR, F32)
        l[...] = jnp.zeros(l.shape, F32)
        acc[...] = jnp.zeros(acc.shape, F32)

        def step(i, _):
            a, base, floor, whole = tile(i)
            rows = pl.ds(pl.multiple_of(a * SUB, SUB), TILE)

            def work(masked):
                k, v = kv[0, rows, :], kv[1, rows, :]
                for c in range(ROWS // CHUNK):
                    cols = slice(c * CHUNK, (c + 1) * CHUNK)
                    s = lax.dot_general(k, q[r, cols, :], NT, preferred_element_type=F32) * (SCALE * LOG2E)
                    if masked:
                        s = jnp.where(seen(base, floor, q_pos, low, cols), s, LOW)
                    old = m[:, cols]
                    new = jnp.maximum(old, jnp.max(s, axis=0, keepdims=True))
                    p = jnp.exp2(s - new)
                    shrink = jnp.exp2(old - new)
                    m[:, cols] = new
                    l[:, cols] = l[:, cols] * shrink + jnp.sum(p, axis=0, keepdims=True)
                    acc[:, cols] = acc[:, cols] * shrink + lax.dot_general(
                        v, p.astype(BF16), TN, preferred_element_type=F32
                    )

            pl.when(whole)(lambda: work(False))
            pl.when(jnp.logical_not(whole))(lambda: work(True))
            return 0

        lax.fori_loop(0, count, step, 0)
        total = l[...]
        out[r] = (acc[...] / jnp.where(total > 0, total, 1.0)).T.astype(BF16)
        ml[pl.ds(r, 1), :] = m[...]
        ml[pl.ds(r + NX, 1), :] = total
        return 0

    lax.fori_loop(0, NX, shard, 0)


def forward(lengths, q, kv):
    return pl.pallas_call(
        forward_kernel,
        out_shape=(jax.ShapeDtypeStruct((NX, ROWS, HD), BF16), jax.ShapeDtypeStruct((2 * NX, ROWS), F32)),
        in_specs=[pl.BlockSpec(memory_space=SMEM)] + [pl.BlockSpec(memory_space=VMEM)] * 2,
        out_specs=(pl.BlockSpec(memory_space=VMEM),) * 2,
        scratch_shapes=[pltpu.VMEM((1, ROWS), F32), pltpu.VMEM((1, ROWS), F32), pltpu.VMEM((HD, ROWS), F32)],
        compiler_params=pltpu.CompilerParams(vmem_limit_bytes=60 << 20),
        cost_estimate=pl.CostEstimate(flops=4 * 12 * TILE * ROWS * HD, transcendentals=12 * TILE * ROWS, bytes_accessed=8 << 20),
        name="forward",
    )(lengths, q, kv)


def backward_kernel(lengths, q, g, kv, st, sta, dq, dkv, acc, dqt, lse, delta):
    x, y, z, _ = place()
    for r in range(NX):
        tops, sums, parts = [], [], []
        for e in range(NX):
            k = (r + e) % NX
            rows = st if e == 0 else sta.at[e]
            tops.append(rows[k : k + 1, :])
            sums.append(rows[NX + k : NX + k + 1, :])
            parts.append(rows[2 * NX + k : 2 * NX + k + 1, :])
        top = jnp.maximum(jnp.maximum(tops[0], tops[1]), jnp.maximum(tops[2], tops[3]))
        weights = [jnp.exp2(a - top) * b for a, b in zip(tops, sums)]
        total = (weights[0] + weights[1]) + (weights[2] + weights[3])
        lse[r : r + 1, :] = top + jnp.log2(total)
        delta[r : r + 1, :] = sum(w * b for w, b in zip(weights, parts)) / total
    acc[...] = jnp.zeros(acc.shape, F32)

    def shard(r, _):
        count, tile, q_pos, low = tiles_of(r, x, y, z, lengths)
        dqt[...] = jnp.zeros(dqt.shape, F32)

        def step(i, _):
            a, base, floor, whole = tile(i)
            rows = pl.ds(pl.multiple_of(a * SUB, SUB), TILE)

            def work(masked):
                k, v = kv[0, rows, :], kv[1, rows, :]
                dk, dv = acc[0, rows, :], acc[1, rows, :]
                for c in range(ROWS // CHUNK):
                    cols = slice(c * CHUNK, (c + 1) * CHUNK)
                    qc, gc = q[r, cols, :], g[r, cols, :]
                    s = lax.dot_general(k, qc, NT, preferred_element_type=F32) * (SCALE * LOG2E)
                    p = jnp.exp2(s - lse[pl.ds(r, 1), cols])
                    if masked:
                        p = jnp.where(seen(base, floor, q_pos, low, cols), p, 0.0)
                    dp = lax.dot_general(v, gc, NT, preferred_element_type=F32)
                    ds = (p * (dp - delta[pl.ds(r, 1), cols])).astype(BF16)
                    dv = dv + lax.dot_general(p.astype(BF16), gc, NN, preferred_element_type=F32)
                    dk = dk + lax.dot_general(ds, qc, NN, preferred_element_type=F32)
                    dqt[:, cols] = dqt[:, cols] + lax.dot_general(k, ds, TN, preferred_element_type=F32)
                acc[0, rows, :] = dk
                acc[1, rows, :] = dv

            pl.when(whole)(lambda: work(False))
            pl.when(jnp.logical_not(whole))(lambda: work(True))
            return 0

        lax.fori_loop(0, count, step, 0)
        dq[r] = (dqt[...] * SCALE).T.astype(BF16)
        return 0

    lax.fori_loop(0, NX, shard, 0)
    dkv[0] = (acc[0] * SCALE).astype(BF16)
    dkv[1] = acc[1].astype(BF16)


def backward(lengths, q, g, kv, st, sta):
    return pl.pallas_call(
        backward_kernel,
        out_shape=(jax.ShapeDtypeStruct(q.shape, BF16), jax.ShapeDtypeStruct(kv.shape, BF16)),
        in_specs=[pl.BlockSpec(memory_space=SMEM)] + [pl.BlockSpec(memory_space=VMEM)] * 5,
        out_specs=(pl.BlockSpec(memory_space=VMEM),) * 2,
        scratch_shapes=[
            pltpu.VMEM(kv.shape, F32), pltpu.VMEM((HD, ROWS), F32),
            pltpu.VMEM((NX, ROWS), F32), pltpu.VMEM((NX, ROWS), F32),
        ],
        compiler_params=pltpu.CompilerParams(vmem_limit_bytes=60 << 20),
        cost_estimate=pl.CostEstimate(flops=10 * 12 * TILE * ROWS * HD, transcendentals=12 * TILE * ROWS, bytes_accessed=10 << 20),
        name="backward",
    )(lengths, q, g, kv, st, sta)


def local(queries, keys, values, w_out, d_out, lengths):
    width = w_out.shape[2]
    kv = jnp.stack([keys.reshape(NX, SUB, HD), values.reshape(NX, SUB, HD)])
    qa, kva, doa = gather(queries.reshape(ROWS, HD), kv, d_out)
    w_flat = w_out.reshape(GROUP * HD, width)
    g = lax.dot_general(doa.reshape(TOK, width), w_flat, NT, preferred_element_type=F32)
    g = g.astype(BF16).reshape(ROWS, HD)
    outer = NX * NY
    ga = [g] + [
        lax.ppermute(g, "outer", [(i, (i + NY * e) % outer) for i in range(outer)]) for e in range(1, NX)
    ]
    ga = jnp.stack(ga)
    kva = kva.reshape(2, SHARDS * SUB, HD)
    ox, ml = forward(lengths, qa, kva)
    parts = jnp.sum(ga.astype(F32) * ox.astype(F32), axis=2)
    st = jnp.concatenate([ml, parts, jnp.zeros_like(parts)], axis=0)
    sta, oxa = swap(st, ox)
    tops = jnp.stack([st[0]] + [sta[e, e] for e in range(1, NX)])
    sums = jnp.stack([st[NX]] + [sta[e, NX + e] for e in range(1, NX)])
    weights = jnp.exp2(tops - jnp.max(tops, axis=0, keepdims=True)) * sums
    weights = weights / jnp.sum(weights, axis=0, keepdims=True)
    attn = weights[0][:, None] * ox[0].astype(F32)
    for e in range(1, NX):
        attn = attn + weights[e][:, None] * oxa[e].astype(F32)
    attn = attn.astype(BF16).reshape(TOK, GROUP * HD)
    mix = jnp.dot(attn, w_flat, preferred_element_type=F32).astype(BF16).reshape(4, TOK // 4, width)
    dq, dkv = backward(lengths, qa, ga, kva, st, sta)
    dqa, kvp, m_near, m_far = reduce(dq, dkv.reshape(2, NX, NY, NZ, SUB, HD), mix)
    mine = lax.dynamic_index_in_dim(mix, lax.axis_index("tensor"), 0, keepdims=False)
    mixed = (mine.astype(F32) + m_near[0].astype(F32) + m_far.astype(F32)).astype(BF16)
    d_queries = dq[0].astype(F32)
    for e in range(1, NX):
        d_queries = d_queries + dqa[e].astype(F32)
    d_queries = d_queries.astype(BF16).reshape(TOK, GROUP, HD)
    d_kv = (kvp[:, :, 0].astype(F32) + kvp[:, :, 1].astype(F32)).astype(BF16)
    return (mixed, d_queries, d_kv[0].reshape(TOK, 1, HD), d_kv[1].reshape(TOK, 1, HD))


def solution(mesh):
    tokens = P(("outer", "inner"), "tensor", None)
    rows = P(("outer", "inner", "tensor"), None)
    return jax.shard_map(
        local,
        mesh=mesh,
        in_specs=(tokens, tokens, tokens, P("tensor", None, None), rows, P()),
        out_specs=(rows, tokens, tokens, tokens),
        check_vma=False,
    )
```

```python
import jax
import jax.numpy as jnp
from jax import lax
from jax.experimental import pallas as pl
from jax.experimental.pallas import tpu as pltpu
from jax.sharding import PartitionSpec as P

MESH = pl.DeviceIdType.MESH
NT = (((1,), (1,)), ((), ()))
NN = (((1,), (0,)), ((), ()))
TN = (((0,), (0,)), ((), ()))
F32, BF16 = jnp.float32, jnp.bfloat16
LOG2E = 1.4426950408889634
LOW, FLOOR = -1e30, -1e20
VMEM, ANY, SMEM = pltpu.VMEM, pl.ANY, pltpu.SMEM

NX, NY, NZ = 4, 2, 8
TOK = 256
SUB = TOK // NX
GROUP = 4
ROWS = TOK * GROUP
HD = 128
SHARDS = NX * NY * NZ
TILE = 256
RUNS = TILE // SUB
CHUNK = 256
BCHUNK = 512
SCALE = HD**-0.5


def place():
    outer, z, t = lax.axis_index("outer"), lax.axis_index("inner"), lax.axis_index("tensor")
    return outer // NY, outer % NY, z, t


def at(x, y, z, t):
    return {"outer": x * NY + y, "inner": z, "tensor": t}


def remote(src, dst, send, recv, device):
    return pltpu.make_async_remote_copy(
        src_ref=src, dst_ref=dst, send_sem=send, recv_sem=recv, device_id=device, device_id_type=MESH
    )


def meet(devices):
    barrier = pltpu.get_barrier_semaphore()
    for device in devices:
        pl.semaphore_signal(barrier, inc=1, device_id=device, device_id_type=MESH)
    pl.semaphore_wait(barrier, len(devices))


PLANE = [(dx, dy) for dy in range(NY) for dx in range(NX) if (dx, dy) != (0, 0)]


def gather_kernel(q, k, v, do, w, qa, ga, kva, doa, wv, gs, gb,
                  qs, qr, ks, kr, zs, zr, ds, dr, gss, gr, ls):
    x, y, z, t = place()
    right, left = (x + 1) % NX, (x + NX - 1) % NX
    up, down = (z + 1) % NZ, (z + NZ - 1) % NZ
    partner, far = t + 1 - 2 * (t % 2), (t + 2) % 4
    other = (partner + 2) % 4
    near_half, far_half = t // 2, 1 - t // 2
    to_r, to_l = at(right, y, z, t), at(left, y, z, t)
    meet(
        [at((x + dx) % NX, (y + dy) % NY, z, t) for dx, dy in PLANE]
        + [at(x, y, up, t), at(x, y, down, t), at(x, y, z, partner), at(x, y, z, far)]
    )
    sent = []

    def send(src, dst, out, into, device):
        copy = remote(src, dst, out, into, device)
        copy.start()
        sent.append(copy)

    def landed(dst, out, into):
        remote(dst, dst, out, into, to_r).wait_recv()

    for i, (dx, dy) in enumerate(PLANE):
        tx, ty = (x + dx) % NX, (y + dy) % NY
        for half, run in enumerate((k, v)):
            send(run.at[tx], kva.at[half, x, y, z], ks.at[i, half], kr.at[i, half], at(tx, ty, z, t))
    own = [
        pltpu.make_async_copy(k.at[x], kva.at[0, x, y, z], ls.at[0]),
        pltpu.make_async_copy(v.at[x], kva.at[1, x, y, z], ls.at[1]),
        pltpu.make_async_copy(q, qa.at[0], ls.at[2]),
        pltpu.make_async_copy(w, wv, ls.at[3]),
    ]
    for copy in own:
        copy.start()
    send(do, doa.at[t], ds.at[0], dr.at[0], at(x, y, z, partner))
    for i in range(2):
        rows = slice(32 * i, 32 * i + 32)
        send(do.at[rows], doa.at[t, rows], ds.at[1 + i], dr.at[1 + i], at(x, y, z, far))
    send(q, qa.at[1], qs.at[0], qr.at[0], to_r)
    send(q, qa.at[3], qs.at[1], qr.at[1], to_l)
    streams = [(0, 0, 4), (1, 1, 4), (0, 1, 3), (1, 0, 3)]

    def hop(step):
        for i, (half, way, hops) in enumerate(streams):
            if step < hops:
                block = (z + NZ - step) % NZ if way == 0 else (z + step) % NZ
                part = kva.at[half, :, :, block]
                send(part, part, zs.at[i, step], zr.at[i, step], at(x, y, up if way == 0 else down, t))

    def arrive(step):
        for i, (half, way, hops) in enumerate(streams):
            if step < hops:
                block = (z + NZ - step - 1) % NZ if way == 0 else (z + step + 1) % NZ
                landed(kva.at[half, :, :, block], zs.at[i, step], zr.at[i, step])

    def project(first, second, slots, half):
        both = jnp.concatenate([first, second], axis=0)
        res = lax.dot_general(both, wv[...], NT, preferred_element_type=F32)
        for i, slot in enumerate(slots):
            for h in range(GROUP):
                gs[i, pl.ds(h, 64, stride=GROUP), :] = res[64 * i : 64 * i + 64, HD * h : HD * h + HD]
            gb[slot] = gs[i].astype(BF16)
        rows = pl.ds(2 * half, 2)
        i = 0 if half is near_half else 2
        send(gb.at[rows], ga.at[1, rows], gss.at[i], gr.at[i], to_r)
        send(gb.at[rows], ga.at[3, rows], gss.at[i + 1], gr.at[i + 1], to_l)

    own[0].wait()
    own[1].wait()
    for i, (dx, dy) in enumerate(PLANE):
        fx, fy = (x + NX - dx) % NX, (y + NY - dy) % NY
        for half in range(2):
            landed(kva.at[half, fx, fy, z], ks.at[i, half], kr.at[i, half])
    hop(0)
    landed(doa.at[partner], ds.at[0], dr.at[0])
    own[3].wait()
    project(do[...], doa[partner], (t, partner), near_half)
    half = ROWS // 2
    landed(qa.at[1], qs.at[0], qr.at[0])
    send(qa.at[1, 0:half], qa.at[2, 0:half], qs.at[2], qr.at[2], to_r)
    landed(qa.at[3], qs.at[1], qr.at[1])
    send(qa.at[3, half:ROWS], qa.at[2, half:ROWS], qs.at[3], qr.at[3], to_l)
    arrive(0)
    hop(1)
    for i in range(2):
        rows = slice(32 * i, 32 * i + 32)
        landed(doa.at[far, rows], ds.at[1 + i], dr.at[1 + i])
        send(doa.at[far, rows], doa.at[far, rows], ds.at[3 + i], dr.at[3 + i], at(x, y, z, partner))
    arrive(1)
    hop(2)
    for i in range(2):
        landed(doa.at[other, 32 * i : 32 * i + 32], ds.at[3 + i], dr.at[3 + i])
    project(doa[far], doa[other], (far, other), far_half)
    arrive(2)
    hop(3)
    near_rows, far_rows = pl.ds(2 * near_half, 2), pl.ds(2 * far_half, 2)
    landed(ga.at[1, near_rows], gss.at[0], gr.at[0])
    send(ga.at[1, near_rows], ga.at[2, near_rows], gss.at[4], gr.at[4], to_r)
    landed(ga.at[3, near_rows], gss.at[1], gr.at[1])
    landed(ga.at[3, far_rows], gss.at[3], gr.at[3])
    send(ga.at[3, far_rows], ga.at[2, far_rows], gss.at[5], gr.at[5], to_l)
    landed(ga.at[1, far_rows], gss.at[2], gr.at[2])
    own_g = pltpu.make_async_copy(gb, ga.at[0], ls.at[4])
    own_g.start()
    arrive(3)
    landed(qa.at[2, 0:half], qs.at[2], qr.at[2])
    landed(qa.at[2, half:ROWS], qs.at[3], qr.at[3])
    landed(ga.at[2, near_rows], gss.at[4], gr.at[4])
    landed(ga.at[2, far_rows], gss.at[5], gr.at[5])
    for copy in sent:
        copy.wait_send()
    own[2].wait()
    own_g.wait()


def gather(q, k, v, do, w):
    dma = pltpu.SemaphoreType.DMA
    return pl.pallas_call(
        gather_kernel,
        out_shape=(
            jax.ShapeDtypeStruct((NX, ROWS, HD), BF16),
            jax.ShapeDtypeStruct((NX, 4, ROWS // 4, HD), BF16),
            jax.ShapeDtypeStruct((2, NX, NY, NZ, SUB, HD), BF16),
        ),
        in_specs=[pl.BlockSpec(memory_space=VMEM)] * 4 + [pl.BlockSpec(memory_space=pltpu.HBM)],
        out_specs=(pl.BlockSpec(memory_space=ANY),) * 3,
        scratch_shapes=[
            pltpu.VMEM((4, *do.shape), BF16), pltpu.VMEM(w.shape, BF16),
            pltpu.VMEM((2, ROWS // 4, HD), F32), pltpu.VMEM((4, ROWS // 4, HD), BF16),
            dma((4,)), dma((4,)), dma((7, 2)), dma((7, 2)), dma((4, 4)), dma((4, 4)),
            dma((5,)), dma((5,)), dma((6,)), dma((6,)), dma((5,)),
        ],
        compiler_params=pltpu.CompilerParams(
            collective_id=0, has_side_effects=True, vmem_limit_bytes=24 << 20
        ),
        name="gather",
    )(q, k, v, do, w)


def swap_kernel(st, sta, ss, sr):
    x, y, z, t = place()
    meet([at((x + dx) % NX, y, z, t) for dx in range(1, NX)])
    copies = [
        remote(st, sta.at[e], ss.at[e], sr.at[e], at((x + NX - e) % NX, y, z, t)) for e in range(1, NX)
    ]
    for copy in copies:
        copy.start()
    for copy in copies:
        copy.wait_recv()
    for copy in copies:
        copy.wait_send()


def swap(st):
    dma = pltpu.SemaphoreType.DMA
    return pl.pallas_call(
        swap_kernel,
        out_shape=jax.ShapeDtypeStruct((NX, *st.shape), st.dtype),
        in_specs=[pl.BlockSpec(memory_space=VMEM)],
        out_specs=pl.BlockSpec(memory_space=ANY),
        scratch_shapes=[dma((4,))] * 2,
        compiler_params=pltpu.CompilerParams(collective_id=1, has_side_effects=True, vmem_limit_bytes=24 << 20),
        name="swap",
    )(st)


def reduce_kernel(dq, g, attn, wv, dqa, kvp, m_own, m_far, b0, b1, b2, b3, total, mix, m32, m_near, m_sum,
                  qs, qr, zs, zr, ks, kr, ms, mr, ls):
    x, y, z, t = place()
    up, down = (z + 1) % NZ, (z + NZ - 1) % NZ
    partner, far = t + 1 - 2 * (t % 2), (t + 2) % 4
    other = (partner + 2) % 4
    meet(
        [at((x + dx) % NX, (y + dy) % NY, z, t) for dx, dy in PLANE]
        + [at(x, y, up, t), at(x, y, down, t), at(x, y, z, partner), at(x, y, z, far)]
    )
    sent = []

    def send(src, dst, out, into, device):
        copy = remote(src, dst, out, into, device)
        copy.start()
        sent.append(copy)

    def landed(dst, out, into):
        remote(dst, dst, out, into, at(x, y, up, t)).wait_recv()

    streams = [(0, 0, 4, b0), (1, 1, 4, b1), (0, 1, 3, b2), (1, 0, 3, b3)]

    def hop(step):
        for i, (half, way, hops, buf) in enumerate(streams):
            if step < hops:
                away = hops - step
                block = (z + away) % NZ if way == 0 else (z + NZ - away) % NZ
                src = g.at[half, :, :, block]
                if step > 0:
                    landed(buf.at[step - 1], zs.at[i, step - 1], zr.at[i, step - 1])
                    buf[step - 1] = (buf[step - 1].astype(F32) + g[half, :, :, block].astype(F32)).astype(BF16)
                    src = buf.at[step - 1]
                send(src, buf.at[step], zs.at[i, step], zr.at[i, step], at(x, y, up if way == 0 else down, t))

    hop(0)
    for e in range(1, NX):
        send(dq.at[e], dqa.at[e], qs.at[e], qr.at[e], at((x + NX - e) % NX, y, z, t))
    width = mix.shape[2]
    both = jnp.concatenate([attn[partner], attn[other]], axis=0)
    for c in range(0, width, 512):
        res = jnp.dot(both, wv[:, c : c + 512], preferred_element_type=F32).astype(BF16)
        mix[0, :, c : c + 512] = res[0:64]
        mix[1, :, c : c + 512] = res[64:128]
    send(mix.at[1], m_near.at[1], ms.at[1], mr.at[1], at(x, y, z, partner))
    send(mix.at[0], m_near.at[0], ms.at[0], mr.at[0], at(x, y, z, partner))
    both = jnp.concatenate([attn[t], attn[far]], axis=0)
    for c in range(0, width, 512):
        m32[:, c : c + 512] = jnp.dot(both, wv[:, c : c + 512], preferred_element_type=F32)
    landed(m_near.at[1], ms.at[1], mr.at[1])
    m_sum[...] = (m32[64:128, :] + m_near[1].astype(F32)).astype(BF16)
    send(m_sum, m_far, ms.at[2], mr.at[2], at(x, y, z, far))
    hop(1)
    landed(m_near.at[0], ms.at[0], mr.at[0])
    m_own[...] = (m32[0:64, :] + m_near[0].astype(F32)).astype(BF16)
    hop(2)
    hop(3)
    for i, (half, way, hops, buf) in enumerate(streams):
        landed(buf.at[hops - 1], zs.at[i, hops - 1], zr.at[i, hops - 1])
    total[0] = (b0[3].astype(F32) + b2[2].astype(F32) + g[0, :, :, z].astype(F32)).astype(BF16)
    total[1] = (b1[3].astype(F32) + b3[2].astype(F32) + g[1, :, :, z].astype(F32)).astype(BF16)
    for i, (dx, dy) in enumerate(PLANE):
        tx, ty = (x + dx) % NX, (y + dy) % NY
        send(total.at[:, tx, ty], kvp.at[:, x, y], ks.at[i], kr.at[i], at(tx, ty, z, t))
    own = pltpu.make_async_copy(total.at[:, x, y], kvp.at[:, x, y], ls.at[0])
    own.start()
    for e in range(1, NX):
        landed(dqa.at[e], qs.at[e], qr.at[e])
    landed(m_far, ms.at[2], mr.at[2])
    for i, (dx, dy) in enumerate(PLANE):
        fx, fy = (x + NX - dx) % NX, (y + NY - dy) % NY
        landed(kvp.at[:, fx, fy], ks.at[i], kr.at[i])
    for copy in sent:
        copy.wait_send()
    own.wait()


def reduce(dq, g, attn, w):
    dma = pltpu.SemaphoreType.DMA
    width = w.shape[1]
    block = (NX, NY, SUB, HD)
    return pl.pallas_call(
        reduce_kernel,
        out_shape=(
            jax.ShapeDtypeStruct(dq.shape, BF16),
            jax.ShapeDtypeStruct((2, *block), BF16),
            jax.ShapeDtypeStruct((64, width), BF16),
            jax.ShapeDtypeStruct((64, width), BF16),
        ),
        in_specs=[
            pl.BlockSpec(memory_space=ANY), pl.BlockSpec(memory_space=VMEM),
            pl.BlockSpec(memory_space=VMEM), pl.BlockSpec(memory_space=VMEM),
        ],
        out_specs=(
            pl.BlockSpec(memory_space=ANY), pl.BlockSpec(memory_space=ANY),
            pl.BlockSpec(memory_space=VMEM), pl.BlockSpec(memory_space=ANY),
        ),
        scratch_shapes=[
            pltpu.VMEM((4, *block), BF16), pltpu.VMEM((4, *block), BF16),
            pltpu.VMEM((3, *block), BF16), pltpu.VMEM((3, *block), BF16),
            pltpu.VMEM((2, *block), BF16),
            pltpu.VMEM((2, 64, width), BF16), pltpu.VMEM((128, width), F32),
            pltpu.VMEM((2, 64, width), BF16), pltpu.VMEM((64, width), BF16),
            dma((4,)), dma((4,)), dma((4, 4)), dma((4, 4)), dma((7,)), dma((7,)), dma((3,)), dma((3,)), dma((1,)),
        ],
        compiler_params=pltpu.CompilerParams(
            collective_id=2, has_side_effects=True, vmem_limit_bytes=24 << 20
        ),
        name="reduce",
    )(dq, g, attn, w)


def begin_of(position, lengths):
    end, first = jnp.int32(0), jnp.zeros_like(position)
    for j in range(lengths.shape[0]):
        end = end + lengths[j]
        first = jnp.where(position >= end, end, first)
    return first


def tiles_of(r, x, y, z, lengths):
    s = ((x + NX - r) % NX) * (NY * NZ) + y * NZ + z
    start = s * TOK
    f = begin_of(start, lengths) // TOK
    q_pos = start + lax.broadcasted_iota(jnp.int32, (1, ROWS), 1) // GROUP
    low = begin_of(q_pos, lengths)
    low_most = begin_of(start + TOK - 1, lengths)
    count = (s - f) // RUNS + 1

    def tile(i):
        want = f + RUNS * i
        a = jnp.minimum(want, SHARDS - RUNS)
        base = a * TOK + x * SUB
        whole = (a == want) & (base >= low_most) & (base + (RUNS - 1) * TOK + SUB - 1 <= start)
        return a, base, want * TOK, whole

    return count, tile, q_pos, low


def seen(base, floor, q_pos, low, cols):
    low, high = jnp.maximum(low[:, cols], floor) - base, q_pos[:, cols] - base
    i = lax.broadcasted_iota(jnp.int32, (TILE, low.shape[1]), 0)
    k_rel = i + (i // SUB) * (TOK - SUB)
    return (k_rel >= low) & (k_rel <= high)


def forward_kernel(lengths, q, g, kv, o0, o1, o2, o3, st, out, m, part, acc, buf, top):
    x, y, z, _ = place()

    def shard(r, _):
        count, tile, q_pos, low = tiles_of(r, x, y, z, lengths)
        m[...] = jnp.full(m.shape, FLOOR, F32)
        part[...] = jnp.zeros(part.shape, F32)
        acc[...] = jnp.zeros(acc.shape, F32)

        def step(i, _):
            a, base, floor, whole = tile(i)
            rows = pl.ds(pl.multiple_of(a * SUB, SUB), TILE)

            def work(masked):
                k, v = kv[0, rows, :], kv[1, rows, :]
                span = [slice(c * CHUNK, (c + 1) * CHUNK) for c in range(ROWS // CHUNK)]
                for cols in span:
                    s = lax.dot_general(k, q[r, cols, :], NT, preferred_element_type=F32) * (SCALE * LOG2E)
                    if masked:
                        s = jnp.where(seen(base, floor, q_pos, low, cols), s, LOW)
                    buf[:, cols] = s
                    top[:, cols] = jnp.max(s.reshape(TILE // 8, 8, CHUNK), axis=0)
                old = m[...]
                new = jnp.maximum(old, jnp.max(top[...], axis=0, keepdims=True))
                m[...] = new
                shrink = jnp.exp2(old - new)
                for cols in span:
                    p = jnp.exp2(buf[:, cols] - new[:, cols])
                    part[:, cols] = part[:, cols] * shrink[:, cols] + jnp.sum(
                        p.reshape(TILE // 8, 8, CHUNK), axis=0
                    )
                    acc[:, cols] = acc[:, cols] * shrink[:, cols] + lax.dot_general(
                        v, p.astype(BF16), TN, preferred_element_type=F32
                    )

            pl.when(whole)(lambda: work(False))
            pl.when(jnp.logical_not(whole))(lambda: work(True))
            return 0

        lax.fori_loop(0, count, step, 0)
        total = jnp.sum(part[...], axis=0, keepdims=True)
        o = (acc[...] / jnp.where(total > 0, total, 1.0)).T
        out[r] = o.astype(BF16)
        prod = o * g[r].astype(F32)
        high = prod.astype(BF16)
        rest = (prod - high.astype(F32)).astype(BF16)
        ones = jnp.ones((8, HD), BF16)
        sums = lax.dot_general(ones, high, NT, preferred_element_type=F32) + lax.dot_general(
            ones, rest, NT, preferred_element_type=F32
        )
        st[pl.ds(r, 1), :] = m[...]
        st[pl.ds(r + NX, 1), :] = total
        st[pl.ds(r + 2 * NX, 1), :] = sums[0:1, :]
        return 0

    lax.fori_loop(0, NX, shard, 0)
    for e, ref in enumerate((o0, o1, o2, o3)):
        ref[...] = out[e]
    st[3 * NX : 4 * NX, :] = jnp.zeros((NX, ROWS), F32)


def forward(lengths, q, g, kv):
    return pl.pallas_call(
        forward_kernel,
        out_shape=(jax.ShapeDtypeStruct((ROWS, HD), BF16),) * NX + (jax.ShapeDtypeStruct((4 * NX, ROWS), F32),),
        in_specs=[pl.BlockSpec(memory_space=SMEM)] + [pl.BlockSpec(memory_space=VMEM)] * 3,
        out_specs=(pl.BlockSpec(memory_space=VMEM),) * 5,
        scratch_shapes=[
            pltpu.VMEM((NX, ROWS, HD), BF16),
            pltpu.VMEM((1, ROWS), F32), pltpu.VMEM((8, ROWS), F32), pltpu.VMEM((HD, ROWS), F32),
            pltpu.VMEM((TILE, ROWS), F32), pltpu.VMEM((8, ROWS), F32),
        ],
        compiler_params=pltpu.CompilerParams(vmem_limit_bytes=24 << 20),
        cost_estimate=pl.CostEstimate(flops=4 * 12 * TILE * ROWS * HD, transcendentals=12 * TILE * ROWS, bytes_accessed=8 << 20),
        name="forward",
    )(lengths, q, g, kv)


def backward_kernel(lengths, q, g, kv, st, sta, dq, dkv, acc, dqt, lse, delta):
    x, y, z, _ = place()
    for r in range(NX):
        tops, sums, parts = [], [], []
        for e in range(NX):
            k = (r + e) % NX
            rows = st if e == 0 else sta.at[e]
            tops.append(rows[k : k + 1, :])
            sums.append(rows[NX + k : NX + k + 1, :])
            parts.append(rows[2 * NX + k : 2 * NX + k + 1, :])
        top = jnp.maximum(jnp.maximum(tops[0], tops[1]), jnp.maximum(tops[2], tops[3]))
        weights = [jnp.exp2(a - top) * b for a, b in zip(tops, sums)]
        total = (weights[0] + weights[1]) + (weights[2] + weights[3])
        lse[r : r + 1, :] = top + jnp.log2(total)
        delta[r : r + 1, :] = sum(w * b for w, b in zip(weights, parts)) / total
    acc[...] = jnp.zeros(acc.shape, F32)

    def shard(r, _):
        count, tile, q_pos, low = tiles_of(r, x, y, z, lengths)
        dqt[...] = jnp.zeros(dqt.shape, F32)

        def step(i, _):
            a, base, floor, whole = tile(i)
            rows = pl.ds(pl.multiple_of(a * SUB, SUB), TILE)

            def work(masked):
                k, v = kv[0, rows, :], kv[1, rows, :]
                dk, dv = acc[0, rows, :], acc[1, rows, :]
                for c in range(ROWS // BCHUNK):
                    cols = slice(c * BCHUNK, (c + 1) * BCHUNK)
                    qc, gc = q[r, cols, :], g[r, cols, :]
                    s = lax.dot_general(k, qc, NT, preferred_element_type=F32) * (SCALE * LOG2E)
                    p = jnp.exp2(s - lse[pl.ds(r, 1), cols])
                    if masked:
                        p = jnp.where(seen(base, floor, q_pos, low, cols), p, 0.0)
                    dp = lax.dot_general(v, gc, NT, preferred_element_type=F32)
                    ds = (p * (dp - delta[pl.ds(r, 1), cols])).astype(BF16)
                    dv = dv + lax.dot_general(p.astype(BF16), gc, NN, preferred_element_type=F32)
                    dk = dk + lax.dot_general(ds, qc, NN, preferred_element_type=F32)
                    dqt[:, cols] = dqt[:, cols] + lax.dot_general(k, ds, TN, preferred_element_type=F32)
                acc[0, rows, :] = dk
                acc[1, rows, :] = dv

            pl.when(whole)(lambda: work(False))
            pl.when(jnp.logical_not(whole))(lambda: work(True))
            return 0

        lax.fori_loop(0, count, step, 0)
        dq[r] = (dqt[...] * SCALE).T.astype(BF16)
        return 0

    lax.fori_loop(0, NX, shard, 0)

    def finish(i, _):
        rows = pl.ds(pl.multiple_of(i * TILE, TILE), TILE)
        dkv[0, rows, :] = (acc[0, rows, :] * SCALE).astype(BF16)
        dkv[1, rows, :] = acc[1, rows, :].astype(BF16)
        return 0

    lax.fori_loop(0, SHARDS * SUB // TILE, finish, 0)


def backward(lengths, q, g, kv, st, sta):
    return pl.pallas_call(
        backward_kernel,
        out_shape=(jax.ShapeDtypeStruct(q.shape, BF16), jax.ShapeDtypeStruct(kv.shape, BF16)),
        in_specs=[pl.BlockSpec(memory_space=SMEM)] + [pl.BlockSpec(memory_space=VMEM)] * 5,
        out_specs=(pl.BlockSpec(memory_space=VMEM),) * 2,
        scratch_shapes=[
            pltpu.VMEM(kv.shape, F32), pltpu.VMEM((HD, ROWS), F32),
            pltpu.VMEM((NX, ROWS), F32), pltpu.VMEM((NX, ROWS), F32),
        ],
        compiler_params=pltpu.CompilerParams(vmem_limit_bytes=24 << 20),
        cost_estimate=pl.CostEstimate(flops=10 * 12 * TILE * ROWS * HD, transcendentals=12 * TILE * ROWS, bytes_accessed=10 << 20),
        name="backward",
    )(lengths, q, g, kv, st, sta)


def blend_kernel(st, sta, o0, o1, o2, o3, attn, rows):
    tops = [st[0:1, :]] + [sta[e, e : e + 1, :] for e in range(1, NX)]
    sums = [st[NX : NX + 1, :]] + [sta[e, NX + e : NX + e + 1, :] for e in range(1, NX)]
    top = jnp.maximum(jnp.maximum(tops[0], tops[1]), jnp.maximum(tops[2], tops[3]))
    weights = [jnp.exp2(m - top) * l for m, l in zip(tops, sums)]
    total = (weights[0] + weights[1]) + (weights[2] + weights[3])
    share = jnp.concatenate([w / total for w in weights] + [jnp.zeros((4, ROWS), F32)], axis=0).T
    rows[...] = sum(share[:, e : e + 1] * o[...].astype(F32) for e, o in enumerate((o0, o1, o2, o3)))
    for slot in range(4):
        for h in range(GROUP):
            part = rows[pl.ds(slot * (ROWS // 4) + h, TOK // 4, stride=GROUP), :]
            attn[slot, :, HD * h : HD * h + HD] = part.astype(BF16)


def blend(st, sta, ox):
    return pl.pallas_call(
        blend_kernel,
        out_shape=jax.ShapeDtypeStruct((4, TOK // 4, GROUP * HD), BF16),
        in_specs=[pl.BlockSpec(memory_space=VMEM)] * 6,
        out_specs=pl.BlockSpec(memory_space=VMEM),
        scratch_shapes=[pltpu.VMEM((ROWS, HD), F32)],
        compiler_params=pltpu.CompilerParams(vmem_limit_bytes=24 << 20),
        cost_estimate=pl.CostEstimate(flops=8 * ROWS * HD, transcendentals=4 * ROWS, bytes_accessed=2 << 20),
        name="blend",
    )(st, sta, *ox)


def finish_kernel(dq, dqa, kvp, m_own, m_far, mixed, d_queries, d_keys, d_values):
    mixed[...] = (m_own[...].astype(F32) + m_far[...].astype(F32)).astype(BF16)
    total = dq[0].astype(F32)
    for e in range(1, NX):
        total = total + dqa[e].astype(F32)
    d_queries[...] = total.astype(BF16)
    for half, out in enumerate((d_keys, d_values)):
        for e in range(NX):
            out[SUB * e : SUB * e + SUB, :] = (
                kvp[half, e, 0].astype(F32) + kvp[half, e, 1].astype(F32)
            ).astype(BF16)


def finish(dq, dqa, kvp, m_own, m_far):
    return pl.pallas_call(
        finish_kernel,
        grid=(1,),
        out_shape=(
            jax.ShapeDtypeStruct(m_own.shape, BF16),
            jax.ShapeDtypeStruct((ROWS, HD), BF16),
            jax.ShapeDtypeStruct((TOK, HD), BF16),
            jax.ShapeDtypeStruct((TOK, HD), BF16),
        ),
        in_specs=[pl.BlockSpec((1, ROWS, HD), lambda i: (0, 0, 0))] + [pl.BlockSpec(memory_space=VMEM)] * 4,
        out_specs=(pl.BlockSpec(memory_space=VMEM),) * 4,
        compiler_params=pltpu.CompilerParams(vmem_limit_bytes=24 << 20),
        cost_estimate=pl.CostEstimate(flops=1 << 20, transcendentals=0, bytes_accessed=4 << 20),
        name="finish",
    )(dq, dqa, kvp, m_own, m_far)


def local(queries, keys, values, w_out, d_out, lengths):
    width = w_out.shape[2]
    w_flat = w_out.reshape(GROUP * HD, width)
    qa, ga, kva = gather(
        queries.reshape(ROWS, HD), keys.reshape(NX, SUB, HD), values.reshape(NX, SUB, HD), d_out, w_flat
    )
    ga = ga.reshape(NX, ROWS, HD)
    kva = kva.reshape(2, SHARDS * SUB, HD)
    *ox, st = forward(lengths, qa, ga, kva)
    sta = swap(st)
    ox[1], ox[2], ox[3], _ = lax.optimization_barrier((ox[1], ox[2], ox[3], sta))
    outer = NX * NY
    oxa = [ox[0]] + [
        lax.ppermute(ox[e], "outer", [(i, (i + outer - NY * e) % outer) for i in range(outer)])
        for e in range(1, NX)
    ]
    dq, dkv = backward(lengths, qa, ga, kva, st, sta)
    attn = blend(st, sta, oxa)
    dqa, kvp, m_own, m_far = reduce(dq, dkv.reshape(2, NX, NY, NZ, SUB, HD), attn, w_flat)
    mixed, d_queries, d_keys, d_values = finish(dq, dqa, kvp, m_own, m_far)
    return (
        mixed,
        d_queries.reshape(TOK, GROUP, HD),
        d_keys.reshape(TOK, 1, HD),
        d_values.reshape(TOK, 1, HD),
    )


def solution(mesh):
    tokens = P(("outer", "inner"), "tensor", None)
    rows = P(("outer", "inner", "tensor"), None)
    return jax.shard_map(
        local,
        mesh=mesh,
        in_specs=(tokens, tokens, tokens, P("tensor", None, None), rows, P()),
        out_specs=(rows, tokens, tokens, tokens),
        check_vma=False,
    )
```

```python
import jax
import jax.numpy as jnp
from jax import lax
from jax.experimental import pallas as pl
from jax.experimental.pallas import tpu as pltpu
from jax.sharding import PartitionSpec as P

MESH = pl.DeviceIdType.MESH
NT = (((1,), (1,)), ((), ()))
NN = (((1,), (0,)), ((), ()))
TN = (((0,), (0,)), ((), ()))
F32, BF16 = jnp.float32, jnp.bfloat16
LOG2E = 1.4426950408889634
LOW, FLOOR = -1e30, -1e20
VMEM, ANY, SMEM = pltpu.VMEM, pl.ANY, pltpu.SMEM

NX, NY, NZ = 4, 2, 8
TOK = 256
SUB = TOK // NX
GROUP = 4
ROWS = TOK * GROUP
HD = 128
SHARDS = NX * NY * NZ
TILE = 256
RUNS = TILE // SUB
CHUNK = 256
BCHUNK = 512
SCALE = HD**-0.5


def place():
    outer, z, t = lax.axis_index("outer"), lax.axis_index("inner"), lax.axis_index("tensor")
    return outer // NY, outer % NY, z, t


def at(x, y, z, t):
    return {"outer": x * NY + y, "inner": z, "tensor": t}


def remote(src, dst, send, recv, device):
    return pltpu.make_async_remote_copy(
        src_ref=src, dst_ref=dst, send_sem=send, recv_sem=recv, device_id=device, device_id_type=MESH
    )


def meet(devices):
    barrier = pltpu.get_barrier_semaphore()
    for device in devices:
        pl.semaphore_signal(barrier, inc=1, device_id=device, device_id_type=MESH)
    pl.semaphore_wait(barrier, len(devices))


PLANE = [(dx, dy) for dy in range(NY) for dx in range(NX) if (dx, dy) != (0, 0)]


def gather_kernel(q, k, v, do, w, qa, ga, kva, doa, wv, gs, gb,
                  qs, qr, ks, kr, zs, zr, ds, dr, gss, gr, ls):
    x, y, z, t = place()
    right, left = (x + 1) % NX, (x + NX - 1) % NX
    up, down = (z + 1) % NZ, (z + NZ - 1) % NZ
    partner, far = t + 1 - 2 * (t % 2), (t + 2) % 4
    other = (partner + 2) % 4
    near_half, far_half = t // 2, 1 - t // 2
    to_r, to_l = at(right, y, z, t), at(left, y, z, t)
    own = [
        pltpu.make_async_copy(k.at[x], kva.at[0, x, y, z], ls.at[0]),
        pltpu.make_async_copy(v.at[x], kva.at[1, x, y, z], ls.at[1]),
        pltpu.make_async_copy(q, qa.at[0], ls.at[2]),
        pltpu.make_async_copy(w, wv, ls.at[3]),
        pltpu.make_async_copy(do, doa.at[t], ls.at[5]),
    ]
    for copy in own:
        copy.start()
    meet(
        [at((x + dx) % NX, (y + dy) % NY, z, t) for dx, dy in PLANE]
        + [at(x, y, up, t), at(x, y, down, t), at(x, y, z, partner), at(x, y, z, far)]
    )
    sent = []

    def send(src, dst, out, into, device):
        copy = remote(src, dst, out, into, device)
        copy.start()
        sent.append(copy)

    def landed(dst, out, into):
        remote(dst, dst, out, into, to_r).wait_recv()

    for i, (dx, dy) in enumerate(PLANE):
        tx, ty = (x + dx) % NX, (y + dy) % NY
        for half, run in enumerate((k, v)):
            send(run.at[tx], kva.at[half, x, y, z], ks.at[i, half], kr.at[i, half], at(tx, ty, z, t))
    send(do, doa.at[t], ds.at[0], dr.at[0], at(x, y, z, partner))
    for i in range(2):
        rows = slice(32 * i, 32 * i + 32)
        send(do.at[rows], doa.at[t, rows], ds.at[1 + i], dr.at[1 + i], at(x, y, z, far))
    send(q, qa.at[1], qs.at[0], qr.at[0], to_r)
    send(q, qa.at[3], qs.at[1], qr.at[1], to_l)
    streams = [(0, 0, 4), (1, 1, 4), (0, 1, 3), (1, 0, 3)]

    def hop(i, step):
        half, way, hops = streams[i]
        if step < hops:
            block = (z + NZ - step) % NZ if way == 0 else (z + step) % NZ
            part = kva.at[half, :, :, block]
            send(part, part, zs.at[i, step], zr.at[i, step], at(x, y, up if way == 0 else down, t))

    def turn(step):
        for i, (half, way, hops) in enumerate(streams):
            if step < hops:
                block = (z + NZ - step - 1) % NZ if way == 0 else (z + step + 1) % NZ
                landed(kva.at[half, :, :, block], zs.at[i, step], zr.at[i, step])
                hop(i, step + 1)

    def project(first, second, slots, half):
        both = jnp.concatenate([first, second], axis=0)
        res = lax.dot_general(both, wv[...], NT, preferred_element_type=F32)
        for i, slot in enumerate(slots):
            for h in range(GROUP):
                gs[i, pl.ds(h, 64, stride=GROUP), :] = res[64 * i : 64 * i + 64, HD * h : HD * h + HD]
            gb[slot] = gs[i].astype(BF16)
        rows = pl.ds(2 * half, 2)
        i = 0 if half is near_half else 2
        send(gb.at[rows], ga.at[1, rows], gss.at[i], gr.at[i], to_r)
        send(gb.at[rows], ga.at[3, rows], gss.at[i + 1], gr.at[i + 1], to_l)

    own[0].wait()
    own[1].wait()
    for i, (dx, dy) in enumerate(PLANE):
        fx, fy = (x + NX - dx) % NX, (y + NY - dy) % NY
        for half in range(2):
            landed(kva.at[half, fx, fy, z], ks.at[i, half], kr.at[i, half])
    for i in range(4):
        hop(i, 0)
    landed(doa.at[partner], ds.at[0], dr.at[0])
    own[3].wait()
    own[4].wait()
    project(doa[t], doa[partner], (t, partner), near_half)
    half = ROWS // 2
    landed(qa.at[1], qs.at[0], qr.at[0])
    send(qa.at[1, 0:half], qa.at[2, 0:half], qs.at[2], qr.at[2], to_r)
    landed(qa.at[3], qs.at[1], qr.at[1])
    send(qa.at[3, half:ROWS], qa.at[2, half:ROWS], qs.at[3], qr.at[3], to_l)
    turn(0)
    for i in range(2):
        rows = slice(32 * i, 32 * i + 32)
        landed(doa.at[far, rows], ds.at[1 + i], dr.at[1 + i])
        send(doa.at[far, rows], doa.at[far, rows], ds.at[3 + i], dr.at[3 + i], at(x, y, z, partner))
    turn(1)
    for i in range(2):
        landed(doa.at[other, 32 * i : 32 * i + 32], ds.at[3 + i], dr.at[3 + i])
    project(doa[far], doa[other], (far, other), far_half)
    turn(2)
    near_rows, far_rows = pl.ds(2 * near_half, 2), pl.ds(2 * far_half, 2)
    landed(ga.at[1, near_rows], gss.at[0], gr.at[0])
    send(ga.at[1, near_rows], ga.at[2, near_rows], gss.at[4], gr.at[4], to_r)
    landed(ga.at[3, near_rows], gss.at[1], gr.at[1])
    landed(ga.at[3, far_rows], gss.at[3], gr.at[3])
    send(ga.at[3, far_rows], ga.at[2, far_rows], gss.at[5], gr.at[5], to_l)
    landed(ga.at[1, far_rows], gss.at[2], gr.at[2])
    own_g = pltpu.make_async_copy(gb, ga.at[0], ls.at[4])
    own_g.start()
    turn(3)
    landed(qa.at[2, 0:half], qs.at[2], qr.at[2])
    landed(qa.at[2, half:ROWS], qs.at[3], qr.at[3])
    landed(ga.at[2, near_rows], gss.at[4], gr.at[4])
    landed(ga.at[2, far_rows], gss.at[5], gr.at[5])
    for copy in sent:
        copy.wait_send()
    own[2].wait()
    own_g.wait()


def gather(q, k, v, do, w):
    dma = pltpu.SemaphoreType.DMA
    return pl.pallas_call(
        gather_kernel,
        out_shape=(
            jax.ShapeDtypeStruct((NX, ROWS, HD), BF16),
            jax.ShapeDtypeStruct((NX, 4, ROWS // 4, HD), BF16),
            jax.ShapeDtypeStruct((2, NX, NY, NZ, SUB, HD), BF16),
        ),
        in_specs=[pl.BlockSpec(memory_space=ANY)] * 5,
        out_specs=(pl.BlockSpec(memory_space=ANY),) * 3,
        scratch_shapes=[
            pltpu.VMEM((4, *do.shape), BF16), pltpu.VMEM(w.shape, BF16),
            pltpu.VMEM((2, ROWS // 4, HD), F32), pltpu.VMEM((4, ROWS // 4, HD), BF16),
            dma((4,)), dma((4,)), dma((7, 2)), dma((7, 2)), dma((4, 4)), dma((4, 4)),
            dma((5,)), dma((5,)), dma((6,)), dma((6,)), dma((6,)),
        ],
        compiler_params=pltpu.CompilerParams(
            collective_id=0, has_side_effects=True, vmem_limit_bytes=24 << 20
        ),
        name="gather",
    )(*(pltpu.with_memory_space_constraint(a, pltpu.HBM) for a in (q, k, v, do, w)))


def swap_kernel(st, sta, ss, sr):
    x, y, z, t = place()
    meet([at((x + dx) % NX, y, z, t) for dx in range(1, NX)])
    copies = [
        remote(st, sta.at[e], ss.at[e], sr.at[e], at((x + NX - e) % NX, y, z, t)) for e in range(1, NX)
    ]
    for copy in copies:
        copy.start()
    for copy in copies:
        copy.wait_recv()
    for copy in copies:
        copy.wait_send()


def swap(st):
    dma = pltpu.SemaphoreType.DMA
    return pl.pallas_call(
        swap_kernel,
        out_shape=jax.ShapeDtypeStruct((NX, *st.shape), st.dtype),
        in_specs=[pl.BlockSpec(memory_space=VMEM)],
        out_specs=pl.BlockSpec(memory_space=ANY),
        scratch_shapes=[dma((4,))] * 2,
        compiler_params=pltpu.CompilerParams(collective_id=1, has_side_effects=True, vmem_limit_bytes=24 << 20),
        name="swap",
    )(st)


def reduce_kernel(dq, g, attn, wv, dqa, kvp, m_own, m_far, b0, b1, b2, b3, total, mix, m32, m_near, m_sum,
                  qs, qr, zs, zr, ks, kr, ms, mr, ls):
    x, y, z, t = place()
    up, down = (z + 1) % NZ, (z + NZ - 1) % NZ
    partner, far = t + 1 - 2 * (t % 2), (t + 2) % 4
    other = (partner + 2) % 4
    meet(
        [at((x + dx) % NX, (y + dy) % NY, z, t) for dx, dy in PLANE]
        + [at(x, y, up, t), at(x, y, down, t), at(x, y, z, partner), at(x, y, z, far)]
    )
    sent = []

    def send(src, dst, out, into, device):
        copy = remote(src, dst, out, into, device)
        copy.start()
        sent.append(copy)

    def landed(dst, out, into):
        remote(dst, dst, out, into, at(x, y, up, t)).wait_recv()

    streams = [(0, 0, 4, b0), (1, 1, 4, b1), (0, 1, 3, b2), (1, 0, 3, b3)]

    def hop(step):
        for i, (half, way, hops, buf) in enumerate(streams):
            if step < hops:
                away = hops - step
                block = (z + away) % NZ if way == 0 else (z + NZ - away) % NZ
                src = g.at[half, :, :, block]
                if step > 0:
                    landed(buf.at[step - 1], zs.at[i, step - 1], zr.at[i, step - 1])
                    buf[step - 1] = (buf[step - 1].astype(F32) + g[half, :, :, block].astype(F32)).astype(BF16)
                    src = buf.at[step - 1]
                send(src, buf.at[step], zs.at[i, step], zr.at[i, step], at(x, y, up if way == 0 else down, t))

    hop(0)
    for e in range(1, NX):
        send(dq.at[e], dqa.at[e], qs.at[e], qr.at[e], at((x + NX - e) % NX, y, z, t))
    width = mix.shape[2]
    both = jnp.concatenate([attn[partner], attn[other]], axis=0)
    for c in range(0, width, 512):
        res = jnp.dot(both, wv[:, c : c + 512], preferred_element_type=F32).astype(BF16)
        mix[0, :, c : c + 512] = res[0:64]
        mix[1, :, c : c + 512] = res[64:128]
    send(mix.at[1], m_near.at[1], ms.at[1], mr.at[1], at(x, y, z, partner))
    send(mix.at[0], m_near.at[0], ms.at[0], mr.at[0], at(x, y, z, partner))
    both = jnp.concatenate([attn[t], attn[far]], axis=0)
    for c in range(0, width, 512):
        m32[:, c : c + 512] = jnp.dot(both, wv[:, c : c + 512], preferred_element_type=F32)
    landed(m_near.at[1], ms.at[1], mr.at[1])
    m_sum[...] = (m32[64:128, :] + m_near[1].astype(F32)).astype(BF16)
    send(m_sum, m_far, ms.at[2], mr.at[2], at(x, y, z, far))
    hop(1)
    landed(m_near.at[0], ms.at[0], mr.at[0])
    m_own[...] = (m32[0:64, :] + m_near[0].astype(F32)).astype(BF16)
    hop(2)
    hop(3)
    for i, (half, way, hops, buf) in enumerate(streams):
        landed(buf.at[hops - 1], zs.at[i, hops - 1], zr.at[i, hops - 1])
    total[0] = (b0[3].astype(F32) + b2[2].astype(F32) + g[0, :, :, z].astype(F32)).astype(BF16)
    total[1] = (b1[3].astype(F32) + b3[2].astype(F32) + g[1, :, :, z].astype(F32)).astype(BF16)
    for i, (dx, dy) in enumerate(PLANE):
        tx, ty = (x + dx) % NX, (y + dy) % NY
        send(total.at[:, tx, ty], kvp.at[:, x, y], ks.at[i], kr.at[i], at(tx, ty, z, t))
    own = pltpu.make_async_copy(total.at[:, x, y], kvp.at[:, x, y], ls.at[0])
    own.start()
    for e in range(1, NX):
        landed(dqa.at[e], qs.at[e], qr.at[e])
    landed(m_far, ms.at[2], mr.at[2])
    for i, (dx, dy) in enumerate(PLANE):
        fx, fy = (x + NX - dx) % NX, (y + NY - dy) % NY
        landed(kvp.at[:, fx, fy], ks.at[i], kr.at[i])
    for copy in sent:
        copy.wait_send()
    own.wait()


def reduce(dq, g, attn, w):
    dma = pltpu.SemaphoreType.DMA
    width = w.shape[1]
    block = (NX, NY, SUB, HD)
    return pl.pallas_call(
        reduce_kernel,
        out_shape=(
            jax.ShapeDtypeStruct(dq.shape, BF16),
            jax.ShapeDtypeStruct((2, *block), BF16),
            jax.ShapeDtypeStruct((64, width), BF16),
            jax.ShapeDtypeStruct((64, width), BF16),
        ),
        in_specs=[
            pl.BlockSpec(memory_space=ANY), pl.BlockSpec(memory_space=VMEM),
            pl.BlockSpec(memory_space=VMEM), pl.BlockSpec(memory_space=VMEM),
        ],
        out_specs=(
            pl.BlockSpec(memory_space=ANY), pl.BlockSpec(memory_space=ANY),
            pl.BlockSpec(memory_space=VMEM), pl.BlockSpec(memory_space=ANY),
        ),
        scratch_shapes=[
            pltpu.VMEM((4, *block), BF16), pltpu.VMEM((4, *block), BF16),
            pltpu.VMEM((3, *block), BF16), pltpu.VMEM((3, *block), BF16),
            pltpu.VMEM((2, *block), BF16),
            pltpu.VMEM((2, 64, width), BF16), pltpu.VMEM((128, width), F32),
            pltpu.VMEM((2, 64, width), BF16), pltpu.VMEM((64, width), BF16),
            dma((4,)), dma((4,)), dma((4, 4)), dma((4, 4)), dma((7,)), dma((7,)), dma((3,)), dma((3,)), dma((1,)),
        ],
        compiler_params=pltpu.CompilerParams(
            collective_id=2, has_side_effects=True, vmem_limit_bytes=24 << 20
        ),
        name="reduce",
    )(dq, g, attn, w)


def begin_of(position, lengths):
    end, first = jnp.int32(0), jnp.zeros_like(position)
    for j in range(lengths.shape[0]):
        end = end + lengths[j]
        first = jnp.where(position >= end, end, first)
    return first


def tiles_of(r, x, y, z, lengths):
    s = ((x + NX - r) % NX) * (NY * NZ) + y * NZ + z
    start = s * TOK
    f = begin_of(start, lengths) // TOK
    q_pos = start + lax.broadcasted_iota(jnp.int32, (1, ROWS), 1) // GROUP
    low = begin_of(q_pos, lengths)
    low_most = begin_of(start + TOK - 1, lengths)
    count = (s - f) // RUNS + 1

    def tile(i):
        want = f + RUNS * i
        a = jnp.minimum(want, SHARDS - RUNS)
        base = a * TOK + x * SUB
        whole = (a == want) & (base >= low_most) & (base + (RUNS - 1) * TOK + SUB - 1 <= start)
        return a, base, want * TOK, whole

    return count, tile, q_pos, low


def seen(base, floor, q_pos, low, cols):
    low, high = jnp.maximum(low[:, cols], floor) - base, q_pos[:, cols] - base
    i = lax.broadcasted_iota(jnp.int32, (TILE, low.shape[1]), 0)
    k_rel = i + (i // SUB) * (TOK - SUB)
    return (k_rel >= low) & (k_rel <= high)


def forward_kernel(lengths, q, g, kv, o0, o1, o2, o3, st, out, m, part, acc, buf, top):
    x, y, z, _ = place()

    def shard(r, _):
        count, tile, q_pos, low = tiles_of(r, x, y, z, lengths)
        m[...] = jnp.full(m.shape, FLOOR, F32)
        part[...] = jnp.zeros(part.shape, F32)
        acc[...] = jnp.zeros(acc.shape, F32)

        def step(i, _):
            a, base, floor, whole = tile(i)
            rows = pl.ds(pl.multiple_of(a * SUB, SUB), TILE)

            def work(masked):
                k, v = kv[0, rows, :], kv[1, rows, :]
                span = [slice(c * CHUNK, (c + 1) * CHUNK) for c in range(ROWS // CHUNK)]
                for cols in span:
                    s = lax.dot_general(k, q[r, cols, :], NT, preferred_element_type=F32) * (SCALE * LOG2E)
                    if masked:
                        s = jnp.where(seen(base, floor, q_pos, low, cols), s, LOW)
                    buf[:, cols] = s
                    top[:, cols] = jnp.max(s.reshape(TILE // 8, 8, CHUNK), axis=0)
                old = m[...]
                new = jnp.maximum(old, jnp.max(top[...], axis=0, keepdims=True))
                m[...] = new
                shrink = jnp.exp2(old - new)
                for cols in span:
                    p = jnp.exp2(buf[:, cols] - new[:, cols])
                    part[:, cols] = part[:, cols] * shrink[:, cols] + jnp.sum(
                        p.reshape(TILE // 8, 8, CHUNK), axis=0
                    )
                    acc[:, cols] = acc[:, cols] * shrink[:, cols] + lax.dot_general(
                        v, p.astype(BF16), TN, preferred_element_type=F32
                    )

            pl.when(whole)(lambda: work(False))
            pl.when(jnp.logical_not(whole))(lambda: work(True))
            return 0

        lax.fori_loop(0, count, step, 0)
        total = jnp.sum(part[...], axis=0, keepdims=True)
        o = (acc[...] / jnp.where(total > 0, total, 1.0)).T
        out[r] = o.astype(BF16)
        prod = o * g[r].astype(F32)
        high = prod.astype(BF16)
        rest = (prod - high.astype(F32)).astype(BF16)
        ones = jnp.ones((8, HD), BF16)
        sums = lax.dot_general(ones, high, NT, preferred_element_type=F32) + lax.dot_general(
            ones, rest, NT, preferred_element_type=F32
        )
        st[pl.ds(r, 1), :] = m[...]
        st[pl.ds(r + NX, 1), :] = total
        st[pl.ds(r + 2 * NX, 1), :] = sums[0:1, :]
        return 0

    lax.fori_loop(0, NX, shard, 0)
    for e, ref in enumerate((o0, o1, o2, o3)):
        ref[...] = out[e]
    st[3 * NX : 4 * NX, :] = jnp.zeros((NX, ROWS), F32)


def forward(lengths, q, g, kv):
    return pl.pallas_call(
        forward_kernel,
        out_shape=(jax.ShapeDtypeStruct((ROWS, HD), BF16),) * NX + (jax.ShapeDtypeStruct((4 * NX, ROWS), F32),),
        in_specs=[pl.BlockSpec(memory_space=SMEM)] + [pl.BlockSpec(memory_space=VMEM)] * 3,
        out_specs=(pl.BlockSpec(memory_space=VMEM),) * 5,
        scratch_shapes=[
            pltpu.VMEM((NX, ROWS, HD), BF16),
            pltpu.VMEM((1, ROWS), F32), pltpu.VMEM((8, ROWS), F32), pltpu.VMEM((HD, ROWS), F32),
            pltpu.VMEM((TILE, ROWS), F32), pltpu.VMEM((8, ROWS), F32),
        ],
        compiler_params=pltpu.CompilerParams(vmem_limit_bytes=24 << 20),
        cost_estimate=pl.CostEstimate(flops=4 * 12 * TILE * ROWS * HD, transcendentals=12 * TILE * ROWS, bytes_accessed=8 << 20),
        name="forward",
    )(lengths, q, g, kv)


def backward_kernel(lengths, q, g, kv, st, sta, dq, dkv, acc, dqt, lse, delta):
    x, y, z, _ = place()
    for r in range(NX):
        tops, sums, parts = [], [], []
        for e in range(NX):
            k = (r + e) % NX
            rows = st if e == 0 else sta.at[e]
            tops.append(rows[k : k + 1, :])
            sums.append(rows[NX + k : NX + k + 1, :])
            parts.append(rows[2 * NX + k : 2 * NX + k + 1, :])
        top = jnp.maximum(jnp.maximum(tops[0], tops[1]), jnp.maximum(tops[2], tops[3]))
        weights = [jnp.exp2(a - top) * b for a, b in zip(tops, sums)]
        total = (weights[0] + weights[1]) + (weights[2] + weights[3])
        lse[r : r + 1, :] = top + jnp.log2(total)
        delta[r : r + 1, :] = sum(w * b for w, b in zip(weights, parts)) / total
    acc[...] = jnp.zeros(acc.shape, F32)

    def shard(r, _):
        count, tile, q_pos, low = tiles_of(r, x, y, z, lengths)
        dqt[...] = jnp.zeros(dqt.shape, F32)

        def step(i, _):
            a, base, floor, whole = tile(i)
            rows = pl.ds(pl.multiple_of(a * SUB, SUB), TILE)

            def work(masked):
                k, v = kv[0, rows, :], kv[1, rows, :]
                dk, dv = acc[0, rows, :], acc[1, rows, :]
                for c in range(ROWS // BCHUNK):
                    cols = slice(c * BCHUNK, (c + 1) * BCHUNK)
                    qc, gc = q[r, cols, :], g[r, cols, :]
                    s = lax.dot_general(k, qc, NT, preferred_element_type=F32) * (SCALE * LOG2E)
                    p = jnp.exp2(s - lse[pl.ds(r, 1), cols])
                    if masked:
                        p = jnp.where(seen(base, floor, q_pos, low, cols), p, 0.0)
                    dp = lax.dot_general(v, gc, NT, preferred_element_type=F32)
                    ds = (p * (dp - delta[pl.ds(r, 1), cols])).astype(BF16)
                    dv = dv + lax.dot_general(p.astype(BF16), gc, NN, preferred_element_type=F32)
                    dk = dk + lax.dot_general(ds, qc, NN, preferred_element_type=F32)
                    dqt[:, cols] = dqt[:, cols] + lax.dot_general(k, ds, TN, preferred_element_type=F32)
                acc[0, rows, :] = dk
                acc[1, rows, :] = dv

            pl.when(whole)(lambda: work(False))
            pl.when(jnp.logical_not(whole))(lambda: work(True))
            return 0

        lax.fori_loop(0, count, step, 0)
        dq[r] = (dqt[...] * SCALE).T.astype(BF16)
        return 0

    lax.fori_loop(0, NX, shard, 0)

    def finish(i, _):
        rows = pl.ds(pl.multiple_of(i * TILE, TILE), TILE)
        dkv[0, rows, :] = (acc[0, rows, :] * SCALE).astype(BF16)
        dkv[1, rows, :] = acc[1, rows, :].astype(BF16)
        return 0

    lax.fori_loop(0, SHARDS * SUB // TILE, finish, 0)


def backward(lengths, q, g, kv, st, sta):
    return pl.pallas_call(
        backward_kernel,
        out_shape=(jax.ShapeDtypeStruct(q.shape, BF16), jax.ShapeDtypeStruct(kv.shape, BF16)),
        in_specs=[pl.BlockSpec(memory_space=SMEM)] + [pl.BlockSpec(memory_space=VMEM)] * 5,
        out_specs=(pl.BlockSpec(memory_space=VMEM),) * 2,
        scratch_shapes=[
            pltpu.VMEM(kv.shape, F32), pltpu.VMEM((HD, ROWS), F32),
            pltpu.VMEM((NX, ROWS), F32), pltpu.VMEM((NX, ROWS), F32),
        ],
        compiler_params=pltpu.CompilerParams(vmem_limit_bytes=24 << 20),
        cost_estimate=pl.CostEstimate(flops=10 * 12 * TILE * ROWS * HD, transcendentals=12 * TILE * ROWS, bytes_accessed=10 << 20),
        name="backward",
    )(lengths, q, g, kv, st, sta)


def blend_kernel(st, sta, o0, o1, o2, o3, attn, rows):
    tops = [st[0:1, :]] + [sta[e, e : e + 1, :] for e in range(1, NX)]
    sums = [st[NX : NX + 1, :]] + [sta[e, NX + e : NX + e + 1, :] for e in range(1, NX)]
    top = jnp.maximum(jnp.maximum(tops[0], tops[1]), jnp.maximum(tops[2], tops[3]))
    weights = [jnp.exp2(m - top) * l for m, l in zip(tops, sums)]
    total = (weights[0] + weights[1]) + (weights[2] + weights[3])
    share = jnp.concatenate([w / total for w in weights] + [jnp.zeros((4, ROWS), F32)], axis=0).T
    rows[...] = sum(share[:, e : e + 1] * o[...].astype(F32) for e, o in enumerate((o0, o1, o2, o3)))
    for slot in range(4):
        for h in range(GROUP):
            part = rows[pl.ds(slot * (ROWS // 4) + h, TOK // 4, stride=GROUP), :]
            attn[slot, :, HD * h : HD * h + HD] = part.astype(BF16)


def blend(st, sta, ox):
    return pl.pallas_call(
        blend_kernel,
        out_shape=jax.ShapeDtypeStruct((4, TOK // 4, GROUP * HD), BF16),
        in_specs=[pl.BlockSpec(memory_space=VMEM)] * 6,
        out_specs=pl.BlockSpec(memory_space=VMEM),
        scratch_shapes=[pltpu.VMEM((ROWS, HD), F32)],
        compiler_params=pltpu.CompilerParams(vmem_limit_bytes=24 << 20),
        cost_estimate=pl.CostEstimate(flops=8 * ROWS * HD, transcendentals=4 * ROWS, bytes_accessed=2 << 20),
        name="blend",
    )(st, sta, *ox)


def finish_kernel(dq, dqa, kvp, m_own, m_far, mixed, d_queries, d_keys, d_values):
    mixed[...] = (m_own[...].astype(F32) + m_far[...].astype(F32)).astype(BF16)
    total = dq[0].astype(F32)
    for e in range(1, NX):
        total = total + dqa[e].astype(F32)
    d_queries[...] = total.astype(BF16)
    for half, out in enumerate((d_keys, d_values)):
        for e in range(NX):
            out[SUB * e : SUB * e + SUB, :] = (
                kvp[half, e, 0].astype(F32) + kvp[half, e, 1].astype(F32)
            ).astype(BF16)


def finish(dq, dqa, kvp, m_own, m_far):
    return pl.pallas_call(
        finish_kernel,
        grid=(1,),
        out_shape=(
            jax.ShapeDtypeStruct(m_own.shape, BF16),
            jax.ShapeDtypeStruct((ROWS, HD), BF16),
            jax.ShapeDtypeStruct((TOK, HD), BF16),
            jax.ShapeDtypeStruct((TOK, HD), BF16),
        ),
        in_specs=[pl.BlockSpec((1, ROWS, HD), lambda i: (0, 0, 0))] + [pl.BlockSpec(memory_space=VMEM)] * 4,
        out_specs=(pl.BlockSpec(memory_space=VMEM),) * 4,
        compiler_params=pltpu.CompilerParams(vmem_limit_bytes=24 << 20),
        cost_estimate=pl.CostEstimate(flops=1 << 20, transcendentals=0, bytes_accessed=4 << 20),
        name="finish",
    )(dq, dqa, kvp, m_own, m_far)


def local(queries, keys, values, w_out, d_out, lengths):
    width = w_out.shape[2]
    w_flat = w_out.reshape(GROUP * HD, width)
    qa, ga, kva = gather(
        queries.reshape(ROWS, HD), keys.reshape(NX, SUB, HD), values.reshape(NX, SUB, HD), d_out, w_flat
    )
    ga = ga.reshape(NX, ROWS, HD)
    kva = kva.reshape(2, SHARDS * SUB, HD)
    *ox, st = forward(lengths, qa, ga, kva)
    sta = swap(st)
    ox[1], ox[2], ox[3], _ = lax.optimization_barrier((ox[1], ox[2], ox[3], sta))
    outer = NX * NY
    oxa = [ox[0]] + [
        lax.ppermute(ox[e], "outer", [(i, (i + outer - NY * e) % outer) for i in range(outer)])
        for e in range(1, NX)
    ]
    dq, dkv = backward(lengths, qa, ga, kva, st, sta)
    attn = blend(st, sta, oxa)
    dqa, kvp, m_own, m_far = reduce(dq, dkv.reshape(2, NX, NY, NZ, SUB, HD), attn, w_flat)
    mixed, d_queries, d_keys, d_values = finish(dq, dqa, kvp, m_own, m_far)
    return (
        mixed,
        d_queries.reshape(TOK, GROUP, HD),
        d_keys.reshape(TOK, 1, HD),
        d_values.reshape(TOK, 1, HD),
    )


def solution(mesh):
    tokens = P(("outer", "inner"), "tensor", None)
    rows = P(("outer", "inner", "tensor"), None)
    return jax.shard_map(
        local,
        mesh=mesh,
        in_specs=(tokens, tokens, tokens, P("tensor", None, None), rows, P()),
        out_specs=(rows, tokens, tokens, tokens),
        check_vma=False,
    )
```

```python
import jax
import jax.numpy as jnp
from jax import lax
from jax.experimental import pallas as pl
from jax.experimental.pallas import tpu as pltpu
from jax.sharding import PartitionSpec as P

MESH = pl.DeviceIdType.MESH
NT = (((1,), (1,)), ((), ()))
NN = (((1,), (0,)), ((), ()))
TN = (((0,), (0,)), ((), ()))
F32, BF16 = jnp.float32, jnp.bfloat16
LOG2E = 1.4426950408889634
LOW, FLOOR = -1e30, -1e20
VMEM, ANY, SMEM = pltpu.VMEM, pl.ANY, pltpu.SMEM

NX, NY, NZ = 4, 2, 8
TOK = 256
SUB = TOK // NX
GROUP = 4
ROWS = TOK * GROUP
HD = 128
SHARDS = NX * NY * NZ
WIDE = 8
CHUNK = 256
BCHUNK = 512
SCALE = HD**-0.5


def place():
    outer, z, t = lax.axis_index("outer"), lax.axis_index("inner"), lax.axis_index("tensor")
    return outer // NY, outer % NY, z, t


def at(x, y, z, t):
    return {"outer": x * NY + y, "inner": z, "tensor": t}


def remote(src, dst, send, recv, device):
    return pltpu.make_async_remote_copy(
        src_ref=src, dst_ref=dst, send_sem=send, recv_sem=recv, device_id=device, device_id_type=MESH
    )


def meet(devices):
    barrier = pltpu.get_barrier_semaphore()
    for device in devices:
        pl.semaphore_signal(barrier, inc=1, device_id=device, device_id_type=MESH)
    pl.semaphore_wait(barrier, len(devices))


PLANE = [(dx, dy) for dy in range(NY) for dx in range(NX) if (dx, dy) != (0, 0)]


def gather_kernel(q, k, v, do, w, qa, ga, kva, doa, wv, gs, gb,
                  qs, qr, ks, kr, zs, zr, ds, dr, gss, gr, ls):
    x, y, z, t = place()
    right, left = (x + 1) % NX, (x + NX - 1) % NX
    up, down = (z + 1) % NZ, (z + NZ - 1) % NZ
    partner, far = t + 1 - 2 * (t % 2), (t + 2) % 4
    other = (partner + 2) % 4
    near_half, far_half = t // 2, 1 - t // 2
    to_r, to_l = at(right, y, z, t), at(left, y, z, t)
    own = [
        pltpu.make_async_copy(k.at[x], kva.at[0, x, y, z], ls.at[0]),
        pltpu.make_async_copy(v.at[x], kva.at[1, x, y, z], ls.at[1]),
        pltpu.make_async_copy(q, qa.at[0], ls.at[2]),
        pltpu.make_async_copy(w, wv, ls.at[3]),
        pltpu.make_async_copy(do, doa.at[t], ls.at[5]),
    ]
    for copy in own:
        copy.start()
    meet(
        [at((x + dx) % NX, (y + dy) % NY, z, t) for dx, dy in PLANE]
        + [at(x, y, up, t), at(x, y, down, t), at(x, y, z, partner), at(x, y, z, far)]
    )
    sent = []

    def send(src, dst, out, into, device):
        copy = remote(src, dst, out, into, device)
        copy.start()
        sent.append(copy)

    def landed(dst, out, into):
        remote(dst, dst, out, into, to_r).wait_recv()

    for i, (dx, dy) in enumerate(PLANE):
        tx, ty = (x + dx) % NX, (y + dy) % NY
        for half, run in enumerate((k, v)):
            send(run.at[tx], kva.at[half, x, y, z], ks.at[i, half], kr.at[i, half], at(tx, ty, z, t))
    send(do, doa.at[t], ds.at[0], dr.at[0], at(x, y, z, partner))
    for i in range(2):
        rows = slice(32 * i, 32 * i + 32)
        send(do.at[rows], doa.at[t, rows], ds.at[1 + i], dr.at[1 + i], at(x, y, z, far))
    send(q, qa.at[1], qs.at[0], qr.at[0], to_r)
    send(q, qa.at[3], qs.at[1], qr.at[1], to_l)
    streams = [(0, 0, 4), (1, 1, 4), (0, 1, 3), (1, 0, 3)]

    def hop(i, step):
        half, way, hops = streams[i]
        if step < hops:
            block = (z + NZ - step) % NZ if way == 0 else (z + step) % NZ
            part = kva.at[half, :, :, block]
            send(part, part, zs.at[i, step], zr.at[i, step], at(x, y, up if way == 0 else down, t))

    def turn(step):
        for i, (half, way, hops) in enumerate(streams):
            if step < hops:
                block = (z + NZ - step - 1) % NZ if way == 0 else (z + step + 1) % NZ
                landed(kva.at[half, :, :, block], zs.at[i, step], zr.at[i, step])
                hop(i, step + 1)

    def project(first, second, slots, half):
        both = jnp.concatenate([first, second], axis=0)
        res = lax.dot_general(both, wv[...], NT, preferred_element_type=F32)
        for i, slot in enumerate(slots):
            for h in range(GROUP):
                gs[i, pl.ds(h, 64, stride=GROUP), :] = res[64 * i : 64 * i + 64, HD * h : HD * h + HD]
            gb[slot] = gs[i].astype(BF16)
        rows = pl.ds(2 * half, 2)
        i = 0 if half is near_half else 2
        send(gb.at[rows], ga.at[1, rows], gss.at[i], gr.at[i], to_r)
        send(gb.at[rows], ga.at[3, rows], gss.at[i + 1], gr.at[i + 1], to_l)

    own[0].wait()
    own[1].wait()
    for i, (dx, dy) in enumerate(PLANE):
        fx, fy = (x + NX - dx) % NX, (y + NY - dy) % NY
        for half in range(2):
            landed(kva.at[half, fx, fy, z], ks.at[i, half], kr.at[i, half])
    for i in range(4):
        hop(i, 0)
    landed(doa.at[partner], ds.at[0], dr.at[0])
    own[3].wait()
    own[4].wait()
    project(doa[t], doa[partner], (t, partner), near_half)
    half = ROWS // 2
    landed(qa.at[1], qs.at[0], qr.at[0])
    send(qa.at[1, 0:half], qa.at[2, 0:half], qs.at[2], qr.at[2], to_r)
    landed(qa.at[3], qs.at[1], qr.at[1])
    send(qa.at[3, half:ROWS], qa.at[2, half:ROWS], qs.at[3], qr.at[3], to_l)
    turn(0)
    for i in range(2):
        rows = slice(32 * i, 32 * i + 32)
        landed(doa.at[far, rows], ds.at[1 + i], dr.at[1 + i])
        send(doa.at[far, rows], doa.at[far, rows], ds.at[3 + i], dr.at[3 + i], at(x, y, z, partner))
    turn(1)
    for i in range(2):
        landed(doa.at[other, 32 * i : 32 * i + 32], ds.at[3 + i], dr.at[3 + i])
    project(doa[far], doa[other], (far, other), far_half)
    turn(2)
    near_rows, far_rows = pl.ds(2 * near_half, 2), pl.ds(2 * far_half, 2)
    landed(ga.at[1, near_rows], gss.at[0], gr.at[0])
    send(ga.at[1, near_rows], ga.at[2, near_rows], gss.at[4], gr.at[4], to_r)
    landed(ga.at[3, near_rows], gss.at[1], gr.at[1])
    landed(ga.at[3, far_rows], gss.at[3], gr.at[3])
    send(ga.at[3, far_rows], ga.at[2, far_rows], gss.at[5], gr.at[5], to_l)
    landed(ga.at[1, far_rows], gss.at[2], gr.at[2])
    own_g = pltpu.make_async_copy(gb, ga.at[0], ls.at[4])
    own_g.start()
    turn(3)
    landed(qa.at[2, 0:half], qs.at[2], qr.at[2])
    landed(qa.at[2, half:ROWS], qs.at[3], qr.at[3])
    landed(ga.at[2, near_rows], gss.at[4], gr.at[4])
    landed(ga.at[2, far_rows], gss.at[5], gr.at[5])
    for copy in sent:
        copy.wait_send()
    own[2].wait()
    own_g.wait()


def gather(q, k, v, do, w):
    dma = pltpu.SemaphoreType.DMA
    return pl.pallas_call(
        gather_kernel,
        out_shape=(
            jax.ShapeDtypeStruct((NX, ROWS, HD), BF16),
            jax.ShapeDtypeStruct((NX, 4, ROWS // 4, HD), BF16),
            jax.ShapeDtypeStruct((2, NX, NY, NZ, SUB, HD), BF16),
        ),
        in_specs=[pl.BlockSpec(memory_space=ANY)] * 5,
        out_specs=(pl.BlockSpec(memory_space=ANY),) * 3,
        scratch_shapes=[
            pltpu.VMEM((4, *do.shape), BF16), pltpu.VMEM(w.shape, BF16),
            pltpu.VMEM((2, ROWS // 4, HD), F32), pltpu.VMEM((4, ROWS // 4, HD), BF16),
            dma((4,)), dma((4,)), dma((7, 2)), dma((7, 2)), dma((4, 4)), dma((4, 4)),
            dma((5,)), dma((5,)), dma((6,)), dma((6,)), dma((6,)),
        ],
        compiler_params=pltpu.CompilerParams(
            collective_id=0, has_side_effects=True, vmem_limit_bytes=24 << 20
        ),
        name="gather",
    )(*(pltpu.with_memory_space_constraint(a, pltpu.HBM) for a in (q, k, v, do, w)))


def swap_kernel(st, sta, ss, sr):
    x, y, z, t = place()
    meet([at((x + dx) % NX, y, z, t) for dx in range(1, NX)])
    copies = [
        remote(st, sta.at[e], ss.at[e], sr.at[e], at((x + NX - e) % NX, y, z, t)) for e in range(1, NX)
    ]
    for copy in copies:
        copy.start()
    for copy in copies:
        copy.wait_recv()
    for copy in copies:
        copy.wait_send()


def swap(st):
    dma = pltpu.SemaphoreType.DMA
    return pl.pallas_call(
        swap_kernel,
        out_shape=jax.ShapeDtypeStruct((NX, *st.shape), st.dtype),
        in_specs=[pl.BlockSpec(memory_space=VMEM)],
        out_specs=pl.BlockSpec(memory_space=ANY),
        scratch_shapes=[dma((4,))] * 2,
        compiler_params=pltpu.CompilerParams(collective_id=1, has_side_effects=True, vmem_limit_bytes=24 << 20),
        name="swap",
    )(st)


def reduce_kernel(dq, g, attn, wv, dqa, kvp, m_own, m_far, b0, b1, b2, b3, total, mix, m32, m_near, m_sum,
                  qs, qr, zs, zr, ks, kr, ms, mr, ls):
    x, y, z, t = place()
    up, down = (z + 1) % NZ, (z + NZ - 1) % NZ
    partner, far = t + 1 - 2 * (t % 2), (t + 2) % 4
    other = (partner + 2) % 4
    meet(
        [at((x + dx) % NX, (y + dy) % NY, z, t) for dx, dy in PLANE]
        + [at(x, y, up, t), at(x, y, down, t), at(x, y, z, partner), at(x, y, z, far)]
    )
    sent = []

    def send(src, dst, out, into, device):
        copy = remote(src, dst, out, into, device)
        copy.start()
        sent.append(copy)

    def landed(dst, out, into):
        remote(dst, dst, out, into, at(x, y, up, t)).wait_recv()

    streams = [(0, 0, 4, b0), (1, 1, 4, b1), (0, 1, 3, b2), (1, 0, 3, b3)]

    def hop(step):
        for i, (half, way, hops, buf) in enumerate(streams):
            if step < hops:
                away = hops - step
                block = (z + away) % NZ if way == 0 else (z + NZ - away) % NZ
                src = g.at[half, :, :, block]
                if step > 0:
                    landed(buf.at[step - 1], zs.at[i, step - 1], zr.at[i, step - 1])
                    buf[step - 1] = (buf[step - 1].astype(F32) + g[half, :, :, block].astype(F32)).astype(BF16)
                    src = buf.at[step - 1]
                send(src, buf.at[step], zs.at[i, step], zr.at[i, step], at(x, y, up if way == 0 else down, t))

    hop(0)
    for e in range(1, NX):
        send(dq.at[e], dqa.at[e], qs.at[e], qr.at[e], at((x + NX - e) % NX, y, z, t))
    width = mix.shape[2]
    both = jnp.concatenate([attn[partner], attn[other]], axis=0)
    for c in range(0, width, 512):
        res = jnp.dot(both, wv[:, c : c + 512], preferred_element_type=F32).astype(BF16)
        mix[0, :, c : c + 512] = res[0:64]
        mix[1, :, c : c + 512] = res[64:128]
    send(mix.at[1], m_near.at[1], ms.at[1], mr.at[1], at(x, y, z, partner))
    send(mix.at[0], m_near.at[0], ms.at[0], mr.at[0], at(x, y, z, partner))
    both = jnp.concatenate([attn[t], attn[far]], axis=0)
    for c in range(0, width, 512):
        m32[:, c : c + 512] = jnp.dot(both, wv[:, c : c + 512], preferred_element_type=F32)
    landed(m_near.at[1], ms.at[1], mr.at[1])
    m_sum[...] = (m32[64:128, :] + m_near[1].astype(F32)).astype(BF16)
    send(m_sum, m_far, ms.at[2], mr.at[2], at(x, y, z, far))
    hop(1)
    landed(m_near.at[0], ms.at[0], mr.at[0])
    m_own[...] = (m32[0:64, :] + m_near[0].astype(F32)).astype(BF16)
    hop(2)
    hop(3)
    for i, (half, way, hops, buf) in enumerate(streams):
        landed(buf.at[hops - 1], zs.at[i, hops - 1], zr.at[i, hops - 1])
    total[0] = (b0[3].astype(F32) + b2[2].astype(F32) + g[0, :, :, z].astype(F32)).astype(BF16)
    total[1] = (b1[3].astype(F32) + b3[2].astype(F32) + g[1, :, :, z].astype(F32)).astype(BF16)
    for i, (dx, dy) in enumerate(PLANE):
        tx, ty = (x + dx) % NX, (y + dy) % NY
        send(total.at[:, tx, ty], kvp.at[:, x, y], ks.at[i], kr.at[i], at(tx, ty, z, t))
    own = pltpu.make_async_copy(total.at[:, x, y], kvp.at[:, x, y], ls.at[0])
    own.start()
    for e in range(1, NX):
        landed(dqa.at[e], qs.at[e], qr.at[e])
    landed(m_far, ms.at[2], mr.at[2])
    for i, (dx, dy) in enumerate(PLANE):
        fx, fy = (x + NX - dx) % NX, (y + NY - dy) % NY
        landed(kvp.at[:, fx, fy], ks.at[i], kr.at[i])
    for copy in sent:
        copy.wait_send()
    own.wait()


def reduce(dq, g, attn, w):
    dma = pltpu.SemaphoreType.DMA
    width = w.shape[1]
    block = (NX, NY, SUB, HD)
    return pl.pallas_call(
        reduce_kernel,
        out_shape=(
            jax.ShapeDtypeStruct(dq.shape, BF16),
            jax.ShapeDtypeStruct((2, *block), BF16),
            jax.ShapeDtypeStruct((64, width), BF16),
            jax.ShapeDtypeStruct((64, width), BF16),
        ),
        in_specs=[
            pl.BlockSpec(memory_space=ANY), pl.BlockSpec(memory_space=VMEM),
            pl.BlockSpec(memory_space=VMEM), pl.BlockSpec(memory_space=VMEM),
        ],
        out_specs=(
            pl.BlockSpec(memory_space=ANY), pl.BlockSpec(memory_space=ANY),
            pl.BlockSpec(memory_space=VMEM), pl.BlockSpec(memory_space=ANY),
        ),
        scratch_shapes=[
            pltpu.VMEM((4, *block), BF16), pltpu.VMEM((4, *block), BF16),
            pltpu.VMEM((3, *block), BF16), pltpu.VMEM((3, *block), BF16),
            pltpu.VMEM((2, *block), BF16),
            pltpu.VMEM((2, 64, width), BF16), pltpu.VMEM((128, width), F32),
            pltpu.VMEM((2, 64, width), BF16), pltpu.VMEM((64, width), BF16),
            dma((4,)), dma((4,)), dma((4, 4)), dma((4, 4)), dma((7,)), dma((7,)), dma((3,)), dma((3,)), dma((1,)),
        ],
        compiler_params=pltpu.CompilerParams(
            collective_id=2, has_side_effects=True, vmem_limit_bytes=24 << 20
        ),
        name="reduce",
    )(dq, g, attn, w)


def begin_of(position, lengths):
    end, first = jnp.int32(0), jnp.zeros_like(position)
    for j in range(lengths.shape[0]):
        end = end + lengths[j]
        first = jnp.where(position >= end, end, first)
    return first


def span_of(r, x, y, z, lengths):
    s = ((x + NX - r) % NX) * (NY * NZ) + y * NZ + z
    start = s * TOK
    first = begin_of(start, lengths)
    f = first // TOK
    q_pos = start + lax.broadcasted_iota(jnp.int32, (1, ROWS), 1) // GROUP
    low = begin_of(q_pos, lengths)
    hide = jnp.where(low > start, jnp.float32(-LOW), jnp.float32(0.0))
    count, rest = (s - f + 1) // WIDE, (s - f + 1) % WIDE

    def tile(want, runs):
        a = jnp.minimum(want, SHARDS - runs)
        base = a * TOK + x * SUB
        whole = (a == want) & (base >= first) & (base + (runs - 1) * TOK + SUB - 1 <= start)
        rows = pl.ds(pl.multiple_of(a * SUB, SUB), runs * SUB)
        return rows, base, want * TOK, whole

    def walk(work):
        def step(i, _):
            rows, base, floor, whole = tile(f + WIDE * i, WIDE)
            pl.when(whole)(lambda: work(rows, WIDE, None))
            pl.when(jnp.logical_not(whole))(lambda: work(rows, WIDE, (base, floor)))
            return 0

        wide = count + (rest > WIDE // 2).astype(jnp.int32)
        lax.fori_loop(0, wide, step, 0)
        for runs in (4, 2):
            rows, base, floor, _ = tile(f + WIDE * count, runs)
            here = (rest <= runs) & (rest > runs // 2) if runs > 2 else (rest <= runs) & (rest > 0)
            pl.when(here)(lambda: work(rows, runs, (base, floor)))

    return walk, q_pos, low, hide


def seen(place_of, runs, q_pos, low, cols):
    base, floor = place_of
    low, high = jnp.maximum(low[:, cols], floor) - base, q_pos[:, cols] - base
    i = lax.broadcasted_iota(jnp.int32, (runs * SUB, low.shape[1]), 0)
    k_rel = i + (i // SUB) * (TOK - SUB)
    return (k_rel >= low) & (k_rel <= high)


def forward_kernel(lengths, q, g, kv, o0, o1, o2, o3, st, out, m, part, acc, buf, top):
    x, y, z, _ = place()

    def shard(r, _):
        walk, q_pos, low, hide = span_of(r, x, y, z, lengths)
        m[...] = jnp.full(m.shape, FLOOR, F32)
        part[...] = jnp.zeros(part.shape, F32)
        acc[...] = jnp.zeros(acc.shape, F32)

        def work(rows, runs, masked):
            k, v = kv[0, rows, :], kv[1, rows, :]
            size = runs * SUB
            span = [slice(c * CHUNK, (c + 1) * CHUNK) for c in range(ROWS // CHUNK)]
            for cols in span:
                s = lax.dot_general(k, q[r, cols, :], NT, preferred_element_type=F32) * (SCALE * LOG2E)
                if masked is not None:
                    s = jnp.where(seen(masked, runs, q_pos, low, cols), s, LOW)
                buf[0:size, cols] = s
                top[:, cols] = jnp.max(s.reshape(size // 8, 8, CHUNK), axis=0)
            old = m[...]
            most = jnp.max(top[...], axis=0, keepdims=True)
            new = jnp.maximum(old, most if masked is not None else most - hide)
            m[...] = new
            shrink = jnp.exp2(old - new)
            if masked is None:
                new = new + hide
            for cols in span:
                p = jnp.exp2(buf[0:size, cols] - new[:, cols])
                part[:, cols] = part[:, cols] * shrink[:, cols] + jnp.sum(
                    p.reshape(size // 8, 8, CHUNK), axis=0
                )
                acc[:, cols] = acc[:, cols] * shrink[:, cols] + lax.dot_general(
                    v, p.astype(BF16), TN, preferred_element_type=F32
                )

        walk(work)
        total = jnp.sum(part[...], axis=0, keepdims=True)
        o = (acc[...] / jnp.where(total > 0, total, 1.0)).T
        out[r] = o.astype(BF16)
        prod = o * g[r].astype(F32)
        high = prod.astype(BF16)
        rest = (prod - high.astype(F32)).astype(BF16)
        ones = jnp.ones((8, HD), BF16)
        sums = lax.dot_general(ones, high, NT, preferred_element_type=F32) + lax.dot_general(
            ones, rest, NT, preferred_element_type=F32
        )
        st[pl.ds(r, 1), :] = m[...]
        st[pl.ds(r + NX, 1), :] = total
        st[pl.ds(r + 2 * NX, 1), :] = sums[0:1, :]
        return 0

    lax.fori_loop(0, NX, shard, 0)
    for e, ref in enumerate((o0, o1, o2, o3)):
        ref[...] = out[e]
    st[3 * NX : 4 * NX, :] = jnp.zeros((NX, ROWS), F32)


def forward(lengths, q, g, kv):
    return pl.pallas_call(
        forward_kernel,
        out_shape=(jax.ShapeDtypeStruct((ROWS, HD), BF16),) * NX + (jax.ShapeDtypeStruct((4 * NX, ROWS), F32),),
        in_specs=[pl.BlockSpec(memory_space=SMEM)] + [pl.BlockSpec(memory_space=VMEM)] * 3,
        out_specs=(pl.BlockSpec(memory_space=VMEM),) * 5,
        scratch_shapes=[
            pltpu.VMEM((NX, ROWS, HD), BF16),
            pltpu.VMEM((1, ROWS), F32), pltpu.VMEM((8, ROWS), F32), pltpu.VMEM((HD, ROWS), F32),
            pltpu.VMEM((WIDE * SUB, ROWS), F32), pltpu.VMEM((8, ROWS), F32),
        ],
        compiler_params=pltpu.CompilerParams(vmem_limit_bytes=24 << 20),
        cost_estimate=pl.CostEstimate(flops=4 * 3072 * ROWS * HD, transcendentals=3072 * ROWS, bytes_accessed=8 << 20),
        name="forward",
    )(lengths, q, g, kv)


def backward_kernel(lengths, q, g, kv, st, sta, dq, dkv, acc, dqt, lse, delta):
    x, y, z, _ = place()
    for r in range(NX):
        tops, sums, parts = [], [], []
        for e in range(NX):
            k = (r + e) % NX
            rows = st if e == 0 else sta.at[e]
            tops.append(rows[k : k + 1, :])
            sums.append(rows[NX + k : NX + k + 1, :])
            parts.append(rows[2 * NX + k : 2 * NX + k + 1, :])
        top = jnp.maximum(jnp.maximum(tops[0], tops[1]), jnp.maximum(tops[2], tops[3]))
        weights = [jnp.exp2(a - top) * b for a, b in zip(tops, sums)]
        total = (weights[0] + weights[1]) + (weights[2] + weights[3])
        lse[r : r + 1, :] = top + jnp.log2(total)
        delta[r : r + 1, :] = sum(w * b for w, b in zip(weights, parts)) / total
    acc[...] = jnp.zeros(acc.shape, F32)

    def shard(r, _):
        walk, q_pos, low, hide = span_of(r, x, y, z, lengths)
        dqt[...] = jnp.zeros(dqt.shape, F32)

        def work(rows, runs, masked):
            k, v = kv[0, rows, :], kv[1, rows, :]
            dk, dv = acc[0, rows, :], acc[1, rows, :]
            for c in range(ROWS // BCHUNK):
                cols = slice(c * BCHUNK, (c + 1) * BCHUNK)
                qc, gc = q[r, cols, :], g[r, cols, :]
                s = lax.dot_general(k, qc, NT, preferred_element_type=F32) * (SCALE * LOG2E)
                if masked is None:
                    p = jnp.exp2(s - (lse[pl.ds(r, 1), cols] + hide[:, cols]))
                else:
                    p = jnp.exp2(s - lse[pl.ds(r, 1), cols])
                    p = jnp.where(seen(masked, runs, q_pos, low, cols), p, 0.0)
                dp = lax.dot_general(v, gc, NT, preferred_element_type=F32)
                ds = (p * (dp - delta[pl.ds(r, 1), cols])).astype(BF16)
                dv = dv + lax.dot_general(p.astype(BF16), gc, NN, preferred_element_type=F32)
                dk = dk + lax.dot_general(ds, qc, NN, preferred_element_type=F32)
                dqt[:, cols] = dqt[:, cols] + lax.dot_general(k, ds, TN, preferred_element_type=F32)
            acc[0, rows, :] = dk
            acc[1, rows, :] = dv

        walk(work)
        dq[r] = (dqt[...] * SCALE).T.astype(BF16)
        return 0

    lax.fori_loop(0, NX, shard, 0)

    def finish(i, _):
        rows = pl.ds(pl.multiple_of(i * 256, 256), 256)
        dkv[0, rows, :] = (acc[0, rows, :] * SCALE).astype(BF16)
        dkv[1, rows, :] = acc[1, rows, :].astype(BF16)
        return 0

    lax.fori_loop(0, SHARDS * SUB // 256, finish, 0)


def backward(lengths, q, g, kv, st, sta):
    return pl.pallas_call(
        backward_kernel,
        out_shape=(jax.ShapeDtypeStruct(q.shape, BF16), jax.ShapeDtypeStruct(kv.shape, BF16)),
        in_specs=[pl.BlockSpec(memory_space=SMEM)] + [pl.BlockSpec(memory_space=VMEM)] * 5,
        out_specs=(pl.BlockSpec(memory_space=VMEM),) * 2,
        scratch_shapes=[
            pltpu.VMEM(kv.shape, F32), pltpu.VMEM((HD, ROWS), F32),
            pltpu.VMEM((NX, ROWS), F32), pltpu.VMEM((NX, ROWS), F32),
        ],
        compiler_params=pltpu.CompilerParams(vmem_limit_bytes=24 << 20),
        cost_estimate=pl.CostEstimate(flops=10 * 3072 * ROWS * HD, transcendentals=3072 * ROWS, bytes_accessed=10 << 20),
        name="backward",
    )(lengths, q, g, kv, st, sta)


def blend_kernel(st, sta, o0, o1, o2, o3, attn, rows):
    tops = [st[0:1, :]] + [sta[e, e : e + 1, :] for e in range(1, NX)]
    sums = [st[NX : NX + 1, :]] + [sta[e, NX + e : NX + e + 1, :] for e in range(1, NX)]
    top = jnp.maximum(jnp.maximum(tops[0], tops[1]), jnp.maximum(tops[2], tops[3]))
    weights = [jnp.exp2(m - top) * l for m, l in zip(tops, sums)]
    total = (weights[0] + weights[1]) + (weights[2] + weights[3])
    share = jnp.concatenate([w / total for w in weights] + [jnp.zeros((4, ROWS), F32)], axis=0).T
    rows[...] = sum(share[:, e : e + 1] * o[...].astype(F32) for e, o in enumerate((o0, o1, o2, o3)))
    for slot in range(4):
        for h in range(GROUP):
            part = rows[pl.ds(slot * (ROWS // 4) + h, TOK // 4, stride=GROUP), :]
            attn[slot, :, HD * h : HD * h + HD] = part.astype(BF16)


def blend(st, sta, ox):
    return pl.pallas_call(
        blend_kernel,
        out_shape=jax.ShapeDtypeStruct((4, TOK // 4, GROUP * HD), BF16),
        in_specs=[pl.BlockSpec(memory_space=VMEM)] * 6,
        out_specs=pl.BlockSpec(memory_space=VMEM),
        scratch_shapes=[pltpu.VMEM((ROWS, HD), F32)],
        compiler_params=pltpu.CompilerParams(vmem_limit_bytes=24 << 20),
        cost_estimate=pl.CostEstimate(flops=8 * ROWS * HD, transcendentals=4 * ROWS, bytes_accessed=2 << 20),
        name="blend",
    )(st, sta, *ox)


def finish_kernel(dq, dqa, kvp, m_own, m_far, mixed, d_queries, d_keys, d_values):
    mixed[...] = (m_own[...].astype(F32) + m_far[...].astype(F32)).astype(BF16)
    total = dq[0].astype(F32)
    for e in range(1, NX):
        total = total + dqa[e].astype(F32)
    d_queries[...] = total.astype(BF16)
    for half, out in enumerate((d_keys, d_values)):
        for e in range(NX):
            out[SUB * e : SUB * e + SUB, :] = (
                kvp[half, e, 0].astype(F32) + kvp[half, e, 1].astype(F32)
            ).astype(BF16)


def finish(dq, dqa, kvp, m_own, m_far):
    return pl.pallas_call(
        finish_kernel,
        grid=(1,),
        out_shape=(
            jax.ShapeDtypeStruct(m_own.shape, BF16),
            jax.ShapeDtypeStruct((ROWS, HD), BF16),
            jax.ShapeDtypeStruct((TOK, HD), BF16),
            jax.ShapeDtypeStruct((TOK, HD), BF16),
        ),
        in_specs=[pl.BlockSpec((1, ROWS, HD), lambda i: (0, 0, 0))] + [pl.BlockSpec(memory_space=VMEM)] * 4,
        out_specs=(pl.BlockSpec(memory_space=VMEM),) * 4,
        compiler_params=pltpu.CompilerParams(vmem_limit_bytes=24 << 20),
        cost_estimate=pl.CostEstimate(flops=1 << 20, transcendentals=0, bytes_accessed=4 << 20),
        name="finish",
    )(dq, dqa, kvp, m_own, m_far)


def local(queries, keys, values, w_out, d_out, lengths):
    width = w_out.shape[2]
    w_flat = w_out.reshape(GROUP * HD, width)
    qa, ga, kva = gather(
        queries.reshape(ROWS, HD), keys.reshape(NX, SUB, HD), values.reshape(NX, SUB, HD), d_out, w_flat
    )
    ga = ga.reshape(NX, ROWS, HD)
    kva = kva.reshape(2, SHARDS * SUB, HD)
    *ox, st = forward(lengths, qa, ga, kva)
    sta = swap(st)
    ox[1], ox[2], ox[3], _ = lax.optimization_barrier((ox[1], ox[2], ox[3], sta))
    outer = NX * NY
    oxa = [ox[0]] + [
        lax.ppermute(ox[e], "outer", [(i, (i + outer - NY * e) % outer) for i in range(outer)])
        for e in range(1, NX)
    ]
    dq, dkv = backward(lengths, qa, ga, kva, st, sta)
    attn = blend(st, sta, oxa)
    dqa, kvp, m_own, m_far = reduce(dq, dkv.reshape(2, NX, NY, NZ, SUB, HD), attn, w_flat)
    mixed, d_queries, d_keys, d_values = finish(dq, dqa, kvp, m_own, m_far)
    return (
        mixed,
        d_queries.reshape(TOK, GROUP, HD),
        d_keys.reshape(TOK, 1, HD),
        d_values.reshape(TOK, 1, HD),
    )


def solution(mesh):
    tokens = P(("outer", "inner"), "tensor", None)
    rows = P(("outer", "inner", "tensor"), None)
    return jax.shard_map(
        local,
        mesh=mesh,
        in_specs=(tokens, tokens, tokens, P("tensor", None, None), rows, P()),
        out_specs=(rows, tokens, tokens, tokens),
        check_vma=False,
    )
```

```python
import jax
import jax.numpy as jnp
from jax import lax
from jax.experimental import pallas as pl
from jax.experimental.pallas import tpu as pltpu
from jax.sharding import PartitionSpec as P

MESH = pl.DeviceIdType.MESH
NT = (((1,), (1,)), ((), ()))
NN = (((1,), (0,)), ((), ()))
TN = (((0,), (0,)), ((), ()))
F32, BF16 = jnp.float32, jnp.bfloat16
LOG2E = 1.4426950408889634
LOW, FLOOR = -1e30, -1e20
VMEM, ANY, SMEM = pltpu.VMEM, pl.ANY, pltpu.SMEM

NX, NY, NZ = 4, 2, 8
TOK = 256
SUB = TOK // NX
GROUP = 4
ROWS = TOK * GROUP
HD = 128
SHARDS = NX * NY * NZ
WIDE = 8
CHUNK = 256
BCHUNK = 512
SCALE = HD**-0.5


def place():
    outer, z, t = lax.axis_index("outer"), lax.axis_index("inner"), lax.axis_index("tensor")
    return outer // NY, outer % NY, z, t


def at(x, y, z, t):
    return {"outer": x * NY + y, "inner": z, "tensor": t}


def remote(src, dst, send, recv, device):
    return pltpu.make_async_remote_copy(
        src_ref=src, dst_ref=dst, send_sem=send, recv_sem=recv, device_id=device, device_id_type=MESH
    )


def meet(devices):
    barrier = pltpu.get_barrier_semaphore()
    for device in devices:
        pl.semaphore_signal(barrier, inc=1, device_id=device, device_id_type=MESH)
    pl.semaphore_wait(barrier, len(devices))


PIECES = [(0, 0), (0, 1), (1, 0), (3, 0), (2, 0), (1, 1), (3, 1), (2, 1)]


def hops_of(p, way):
    return 4 if p % 2 == way else 3


def gather_kernel(q, k, v, do, w, qa, ga, kva, doa, wv, gs, gb,
                  qs, qr, ks, kr, zs, zr, ds, dr, gss, gr, ls):
    x, y, z, t = place()
    right, left = (x + 1) % NX, (x + NX - 1) % NX
    up, down = (z + 1) % NZ, (z + NZ - 1) % NZ
    partner, far = t + 1 - 2 * (t % 2), (t + 2) % 4
    other = (partner + 2) % 4
    near_rows, far_rows = pl.ds(2 * (t // 2), 2), pl.ds(2 * (1 - t // 2), 2)
    to_r, to_l, to_p = at(right, y, z, t), at(left, y, z, t), at(x, y, z, partner)
    ring = (at(x, y, up, t), at(x, y, down, t))
    spots = [((x + ex) % NX, (y + ey) % NY) for ex, ey in PIECES]
    backs = [((x + NX - ex) % NX, (y + NY - ey) % NY) for ex, ey in PIECES]
    own = [
        pltpu.make_async_copy(k.at[x], kva.at[0, x, y, z], ls.at[0]),
        pltpu.make_async_copy(v.at[x], kva.at[1, x, y, z], ls.at[1]),
        pltpu.make_async_copy(q, qa.at[0], ls.at[2]),
        pltpu.make_async_copy(w, wv, ls.at[3]),
        pltpu.make_async_copy(do, doa.at[t], ls.at[5]),
    ]
    for copy in own:
        copy.start()
    meet([at(fx, fy, z, t) for fx, fy in backs[1:]] + [ring[0], ring[1], to_p, at(x, y, z, far)])
    sent = []

    def send(src, dst, out, into, device):
        copy = remote(src, dst, out, into, device)
        copy.start()
        sent.append(copy)

    def landed(dst, out, into):
        remote(dst, dst, out, into, to_r).wait_recv()

    for p, (bx, by) in enumerate(backs):
        if p > 0:
            for half, run in enumerate((k, v)):
                send(run.at[bx], kva.at[half, x, y, z], ks.at[p, half], kr.at[p, half], at(bx, by, z, t))
    send(do, doa.at[t], ds.at[0], dr.at[0], to_p)
    for i in range(2):
        rows = slice(32 * i, 32 * i + 32)
        send(do.at[rows], doa.at[t, rows], ds.at[1 + i], dr.at[1 + i], at(x, y, z, far))
    send(q, qa.at[1], qs.at[0], qr.at[0], to_r)
    send(q, qa.at[3], qs.at[1], qr.at[1], to_l)

    def hop(p, way, step):
        if step < hops_of(p, way):
            block = (z + NZ - step) % NZ if way == 0 else (z + step) % NZ
            part = kva.at[:, spots[p][0], spots[p][1], block]
            send(part, part, zs.at[way, p, step], zr.at[way, p, step], ring[way])

    def turn(step, pieces=range(8)):
        for p in pieces:
            for way in range(2):
                if step < hops_of(p, way):
                    block = (z + NZ - step - 1) % NZ if way == 0 else (z + step + 1) % NZ
                    landed(kva.at[:, spots[p][0], spots[p][1], block], zs.at[way, p, step], zr.at[way, p, step])
                    hop(p, way, step + 1)

    def project(first, second, slots, halves):
        res = lax.dot_general(
            jnp.concatenate([first, second], axis=0), wv[...], NT, preferred_element_type=F32
        )
        size = 32 * len(halves)
        for i, slot in enumerate(slots):
            for h in range(GROUP):
                gs[i, pl.ds(h, size, stride=GROUP), :] = res[size * i : size * i + size, HD * h : HD * h + HD]
            for j, half in enumerate(halves):
                gb[slot, half] = gs[i, 128 * j : 128 * j + 128, :].astype(BF16)

    def spread(i, rows, halves):
        send(gb.at[rows, halves], ga.at[1, rows, halves], gss.at[3 * i], gr.at[3 * i], to_r)
        send(gb.at[rows, halves], ga.at[3, rows, halves], gss.at[3 * i + 1], gr.at[3 * i + 1], to_l)

    def relay(i, rows, halves, slot, device):
        landed(ga.at[slot, rows, halves], gss.at[3 * i + slot // 3], gr.at[3 * i + slot // 3])
        part = ga.at[slot, rows, halves]
        send(part, ga.at[2, rows, halves], gss.at[3 * i + 2], gr.at[3 * i + 2], device)

    groups = [(near_rows, slice(0, 2)), (far_rows, slice(0, 1)), (far_rows, slice(1, 2))]
    own[0].wait()
    own[1].wait()
    for p, (fx, fy) in enumerate(spots):
        if p > 0:
            for half in range(2):
                landed(kva.at[half, fx, fy, z], ks.at[p, half], kr.at[p, half])
        for way in range(2):
            hop(p, way, 0)
    landed(doa.at[partner], ds.at[0], dr.at[0])
    own[3].wait()
    own[4].wait()
    project(doa[t], doa[partner], (t, partner), (0, 1))
    spread(0, *groups[0])
    half = ROWS // 2
    landed(qa.at[1], qs.at[0], qr.at[0])
    send(qa.at[1, 0:half], qa.at[2, 0:half], qs.at[2], qr.at[2], to_r)
    landed(qa.at[3], qs.at[1], qr.at[1])
    send(qa.at[3, half:ROWS], qa.at[2, half:ROWS], qs.at[3], qr.at[3], to_l)

    def pass_on(i):
        rows = slice(32 * i, 32 * i + 32)
        landed(doa.at[far, rows], ds.at[1 + i], dr.at[1 + i])
        send(doa.at[far, rows], doa.at[far, rows], ds.at[3 + i], dr.at[3 + i], to_p)

    def project_far(i):
        rows = slice(32 * i, 32 * i + 32)
        landed(doa.at[other, rows], ds.at[3 + i], dr.at[3 + i])
        project(doa[far, rows], doa[other, rows], (far, other), (i,))
        spread(1 + i, *groups[1 + i])

    turn(0)
    pass_on(0)
    relay(0, *groups[0], 1, to_r)
    turn(1, range(4))
    project_far(0)
    pass_on(1)
    turn(1, range(4, 8))
    turn(2, range(2))
    project_far(1)
    relay(1, *groups[1], 3, to_l)
    turn(2, range(2, 8))
    relay(2, *groups[2], 3, to_l)
    own_g = pltpu.make_async_copy(gb, ga.at[0], ls.at[4])
    own_g.start()
    turn(3)
    landed(qa.at[2, 0:half], qs.at[2], qr.at[2])
    landed(qa.at[2, half:ROWS], qs.at[3], qr.at[3])
    for i, (rows, halves) in enumerate(groups):
        last = 3 if i == 0 else 1
        landed(ga.at[last, rows, halves], gss.at[3 * i + last // 3], gr.at[3 * i + last // 3])
        landed(ga.at[2, rows, halves], gss.at[3 * i + 2], gr.at[3 * i + 2])
    for copy in sent:
        copy.wait_send()
    own[2].wait()
    own_g.wait()


def gather(q, k, v, do, w):
    dma = pltpu.SemaphoreType.DMA
    return pl.pallas_call(
        gather_kernel,
        out_shape=(
            jax.ShapeDtypeStruct((NX, ROWS, HD), BF16),
            jax.ShapeDtypeStruct((NX, 4, 2, ROWS // 8, HD), BF16),
            jax.ShapeDtypeStruct((2, NX, NY, NZ, SUB, HD), BF16),
        ),
        in_specs=[pl.BlockSpec(memory_space=ANY)] * 5,
        out_specs=(pl.BlockSpec(memory_space=ANY),) * 3,
        scratch_shapes=[
            pltpu.VMEM((4, *do.shape), BF16), pltpu.VMEM(w.shape, BF16),
            pltpu.VMEM((2, ROWS // 4, HD), F32), pltpu.VMEM((4, 2, ROWS // 8, HD), BF16),
            dma((4,)), dma((4,)), dma((8, 2)), dma((8, 2)), dma((2, 8, 4)), dma((2, 8, 4)),
            dma((5,)), dma((5,)), dma((9,)), dma((9,)), dma((6,)),
        ],
        compiler_params=pltpu.CompilerParams(
            collective_id=0, has_side_effects=True, vmem_limit_bytes=24 << 20
        ),
        name="gather",
    )(*(pltpu.with_memory_space_constraint(a, pltpu.HBM) for a in (q, k, v, do, w)))


def swap_kernel(st, sta, ss, sr):
    x, y, z, t = place()
    meet([at((x + dx) % NX, y, z, t) for dx in range(1, NX)])
    copies = [
        remote(st, sta.at[e], ss.at[e], sr.at[e], at((x + NX - e) % NX, y, z, t)) for e in range(1, NX)
    ]
    for copy in copies:
        copy.start()
    for copy in copies:
        copy.wait_recv()
    for copy in copies:
        copy.wait_send()


def swap(st):
    dma = pltpu.SemaphoreType.DMA
    return pl.pallas_call(
        swap_kernel,
        out_shape=jax.ShapeDtypeStruct((NX, *st.shape), st.dtype),
        in_specs=[pl.BlockSpec(memory_space=VMEM)],
        out_specs=pl.BlockSpec(memory_space=ANY),
        scratch_shapes=[dma((4,))] * 2,
        compiler_params=pltpu.CompilerParams(collective_id=1, has_side_effects=True, vmem_limit_bytes=24 << 20),
        name="swap",
    )(st)


def reduce_kernel(dq, g, attn, wv, dqa, kvp, m_own, m_far, b_up, b_down, total, mix, m32, m_near, m_sum,
                  qs, qr, zs, zr, ks, kr, ms, mr, ls):
    x, y, z, t = place()
    up, down = (z + 1) % NZ, (z + NZ - 1) % NZ
    partner, far = t + 1 - 2 * (t % 2), (t + 2) % 4
    other = (partner + 2) % 4
    to_p, to_f = at(x, y, z, partner), at(x, y, z, far)
    ring, bufs = (at(x, y, up, t), at(x, y, down, t)), (b_up, b_down)
    spots = [((x + ex) % NX, (y + ey) % NY) for ex, ey in PIECES]
    backs = [((x + NX - ex) % NX, (y + NY - ey) % NY) for ex, ey in PIECES]
    meet([at(fx, fy, z, t) for fx, fy in spots[1:]] + [ring[0], ring[1], to_p, to_f])
    sent = []

    def send(src, dst, out, into, device):
        copy = remote(src, dst, out, into, device)
        copy.start()
        sent.append(copy)

    def landed(dst, out, into):
        remote(dst, dst, out, into, to_p).wait_recv()

    def turn(step, pieces=range(8)):
        for p in pieces:
            for way, buf in enumerate(bufs):
                away = hops_of(p, way) - step
                if away > 0:
                    block = (z + away) % NZ if way == 0 else (z + NZ - away) % NZ
                    src = g.at[:, spots[p][0], spots[p][1], block]
                    if step > 0:
                        landed(buf.at[step - 1, p], zs.at[way, p, step - 1], zr.at[way, p, step - 1])
                        mine = g[:, spots[p][0], spots[p][1], block].astype(F32)
                        buf[step - 1, p] = (buf[step - 1, p].astype(F32) + mine).astype(BF16)
                        src = buf.at[step - 1, p]
                    send(src, buf.at[step, p], zs.at[way, p, step], zr.at[way, p, step], ring[way])

    turn(0)
    for e in range(1, NX):
        send(dq.at[e], dqa.at[e], qs.at[e], qr.at[e], at((x + NX - e) % NX, y, z, t))
    width = mix.shape[2]
    both = jnp.concatenate([attn[partner], attn[other]], axis=0)
    for c in range(0, width, 512):
        res = jnp.dot(both, wv[:, c : c + 512], preferred_element_type=F32).astype(BF16)
        mix[0, :, c : c + 512] = res[0:64]
        mix[1, :, c : c + 512] = res[64:128]
    send(mix.at[1], m_near.at[1], ms.at[1], mr.at[1], to_p)
    send(mix.at[0], m_near.at[0], ms.at[0], mr.at[0], to_p)
    both = jnp.concatenate([attn[t], attn[far]], axis=0)
    for c in range(0, width, 512):
        m32[:, c : c + 512] = jnp.dot(both, wv[:, c : c + 512], preferred_element_type=F32)
    turn(1, range(2))
    landed(m_near.at[1], ms.at[1], mr.at[1])
    m_sum[...] = (m32[64:128, :] + m_near[1].astype(F32)).astype(BF16)
    send(m_sum, m_far, ms.at[2], mr.at[2], to_f)
    turn(1, range(2, 8))
    turn(2, range(4))
    landed(m_near.at[0], ms.at[0], mr.at[0])
    m_own[...] = (m32[0:64, :] + m_near[0].astype(F32)).astype(BF16)
    turn(2, range(4, 8))
    turn(3)
    own = pltpu.make_async_copy(total.at[0], kvp.at[:, x, y], ls.at[0])
    for p, (tx, ty) in enumerate(spots):
        last = g[:, tx, ty, z].astype(F32)
        for way, buf in enumerate(bufs):
            end = hops_of(p, way) - 1
            landed(buf.at[end, p], zs.at[way, p, end], zr.at[way, p, end])
            last = last + buf[end, p].astype(F32)
        total[p] = last.astype(BF16)
        if p == 0:
            own.start()
        else:
            send(total.at[p], kvp.at[:, x, y], ks.at[p], kr.at[p], at(tx, ty, z, t))
    for e in range(1, NX):
        landed(dqa.at[e], qs.at[e], qr.at[e])
    landed(m_far, ms.at[2], mr.at[2])
    for p, (fx, fy) in enumerate(backs):
        if p > 0:
            landed(kvp.at[:, fx, fy], ks.at[p], kr.at[p])
    for copy in sent:
        copy.wait_send()
    own.wait()


def reduce(dq, g, attn, w):
    dma = pltpu.SemaphoreType.DMA
    width = w.shape[1]
    piece = (2, SUB, HD)
    return pl.pallas_call(
        reduce_kernel,
        out_shape=(
            jax.ShapeDtypeStruct(dq.shape, BF16),
            jax.ShapeDtypeStruct((2, NX, NY, SUB, HD), BF16),
            jax.ShapeDtypeStruct((64, width), BF16),
            jax.ShapeDtypeStruct((64, width), BF16),
        ),
        in_specs=[
            pl.BlockSpec(memory_space=ANY), pl.BlockSpec(memory_space=VMEM),
            pl.BlockSpec(memory_space=VMEM), pl.BlockSpec(memory_space=VMEM),
        ],
        out_specs=(
            pl.BlockSpec(memory_space=ANY), pl.BlockSpec(memory_space=ANY),
            pl.BlockSpec(memory_space=VMEM), pl.BlockSpec(memory_space=ANY),
        ),
        scratch_shapes=[
            pltpu.VMEM((4, 8, *piece), BF16), pltpu.VMEM((4, 8, *piece), BF16),
            pltpu.VMEM((8, *piece), BF16),
            pltpu.VMEM((2, 64, width), BF16), pltpu.VMEM((128, width), F32),
            pltpu.VMEM((2, 64, width), BF16), pltpu.VMEM((64, width), BF16),
            dma((4,)), dma((4,)), dma((2, 8, 4)), dma((2, 8, 4)), dma((8,)), dma((8,)),
            dma((3,)), dma((3,)), dma((1,)),
        ],
        compiler_params=pltpu.CompilerParams(
            collective_id=2, has_side_effects=True, vmem_limit_bytes=24 << 20
        ),
        name="reduce",
    )(dq, g, attn, w)


def begin_of(position, lengths):
    end, first = jnp.int32(0), jnp.zeros_like(position)
    for j in range(lengths.shape[0]):
        end = end + lengths[j]
        first = jnp.where(position >= end, end, first)
    return first


def span_of(r, x, y, z, lengths):
    s = ((x + NX - r) % NX) * (NY * NZ) + y * NZ + z
    start = s * TOK
    first = begin_of(start, lengths)
    f = first // TOK
    q_pos = start + lax.broadcasted_iota(jnp.int32, (1, ROWS), 1) // GROUP
    low = begin_of(q_pos, lengths)
    hide = jnp.where(low > start, jnp.float32(-LOW), jnp.float32(0.0))
    count, rest = (s - f + 1) // WIDE, (s - f + 1) % WIDE

    def tile(want, runs):
        a = jnp.minimum(want, SHARDS - runs)
        base = a * TOK + x * SUB
        whole = (a == want) & (base >= first) & (base + (runs - 1) * TOK + SUB - 1 <= start)
        rows = pl.ds(pl.multiple_of(a * SUB, SUB), runs * SUB)
        return rows, base, want * TOK, whole

    def walk(work):
        def step(i, _):
            rows, base, floor, whole = tile(f + WIDE * i, WIDE)
            pl.when(whole)(lambda: work(rows, WIDE, None))
            pl.when(jnp.logical_not(whole))(lambda: work(rows, WIDE, (base, floor)))
            return 0

        wide = count + (rest > WIDE // 2).astype(jnp.int32)
        lax.fori_loop(0, wide, step, 0)
        for runs in (4, 2):
            rows, base, floor, _ = tile(f + WIDE * count, runs)
            here = (rest <= runs) & (rest > runs // 2) if runs > 2 else (rest <= runs) & (rest > 0)
            pl.when(here)(lambda: work(rows, runs, (base, floor)))

    return walk, q_pos, low, hide


def seen(place_of, runs, q_pos, low, cols):
    base, floor = place_of
    low, high = jnp.maximum(low[:, cols], floor) - base, q_pos[:, cols] - base
    i = lax.broadcasted_iota(jnp.int32, (runs * SUB, low.shape[1]), 0)
    k_rel = i + (i // SUB) * (TOK - SUB)
    return (k_rel >= low) & (k_rel <= high)


def forward_kernel(lengths, q, g, kv, o0, o1, o2, o3, st, out, m, part, acc, buf, top):
    x, y, z, _ = place()

    def shard(r, _):
        walk, q_pos, low, hide = span_of(r, x, y, z, lengths)
        m[...] = jnp.full(m.shape, FLOOR, F32)
        part[...] = jnp.zeros(part.shape, F32)
        acc[...] = jnp.zeros(acc.shape, F32)

        def work(rows, runs, masked):
            k, v = kv[0, rows, :], kv[1, rows, :]
            size = runs * SUB
            span = [slice(c * CHUNK, (c + 1) * CHUNK) for c in range(ROWS // CHUNK)]
            for cols in span:
                s = lax.dot_general(k, q[r, cols, :], NT, preferred_element_type=F32) * (SCALE * LOG2E)
                if masked is not None:
                    s = jnp.where(seen(masked, runs, q_pos, low, cols), s, LOW)
                buf[0:size, cols] = s
                top[:, cols] = jnp.max(s.reshape(size // 8, 8, CHUNK), axis=0)
            old = m[...]
            most = jnp.max(top[...], axis=0, keepdims=True)
            new = jnp.maximum(old, most if masked is not None else most - hide)
            m[...] = new
            shrink = jnp.exp2(old - new)
            if masked is None:
                new = new + hide
            for cols in span:
                p = jnp.exp2(buf[0:size, cols] - new[:, cols])
                part[:, cols] = part[:, cols] * shrink[:, cols] + jnp.sum(
                    p.reshape(size // 8, 8, CHUNK), axis=0
                )
                acc[:, cols] = acc[:, cols] * shrink[:, cols] + lax.dot_general(
                    v, p.astype(BF16), TN, preferred_element_type=F32
                )

        walk(work)
        total = jnp.sum(part[...], axis=0, keepdims=True)
        o = (acc[...] / jnp.where(total > 0, total, 1.0)).T
        out[r] = o.astype(BF16)
        prod = o * g[r].astype(F32)
        high = prod.astype(BF16)
        rest = (prod - high.astype(F32)).astype(BF16)
        ones = jnp.ones((8, HD), BF16)
        sums = lax.dot_general(ones, high, NT, preferred_element_type=F32) + lax.dot_general(
            ones, rest, NT, preferred_element_type=F32
        )
        st[pl.ds(r, 1), :] = m[...]
        st[pl.ds(r + NX, 1), :] = total
        st[pl.ds(r + 2 * NX, 1), :] = sums[0:1, :]
        return 0

    lax.fori_loop(0, NX, shard, 0)
    for e, ref in enumerate((o0, o1, o2, o3)):
        ref[...] = out[e]
    st[3 * NX : 4 * NX, :] = jnp.zeros((NX, ROWS), F32)


def forward(lengths, q, g, kv):
    return pl.pallas_call(
        forward_kernel,
        out_shape=(jax.ShapeDtypeStruct((ROWS, HD), BF16),) * NX + (jax.ShapeDtypeStruct((4 * NX, ROWS), F32),),
        in_specs=[pl.BlockSpec(memory_space=SMEM)] + [pl.BlockSpec(memory_space=VMEM)] * 3,
        out_specs=(pl.BlockSpec(memory_space=VMEM),) * 5,
        scratch_shapes=[
            pltpu.VMEM((NX, ROWS, HD), BF16),
            pltpu.VMEM((1, ROWS), F32), pltpu.VMEM((8, ROWS), F32), pltpu.VMEM((HD, ROWS), F32),
            pltpu.VMEM((WIDE * SUB, ROWS), F32), pltpu.VMEM((8, ROWS), F32),
        ],
        compiler_params=pltpu.CompilerParams(vmem_limit_bytes=24 << 20),
        cost_estimate=pl.CostEstimate(flops=4 * 3072 * ROWS * HD, transcendentals=3072 * ROWS, bytes_accessed=8 << 20),
        name="forward",
    )(lengths, q, g, kv)


def backward_kernel(lengths, q, g, kv, st, sta, dq, dkv, acc, dqt, lse, delta):
    x, y, z, _ = place()
    for r in range(NX):
        tops, sums, parts = [], [], []
        for e in range(NX):
            k = (r + e) % NX
            rows = st if e == 0 else sta.at[e]
            tops.append(rows[k : k + 1, :])
            sums.append(rows[NX + k : NX + k + 1, :])
            parts.append(rows[2 * NX + k : 2 * NX + k + 1, :])
        top = jnp.maximum(jnp.maximum(tops[0], tops[1]), jnp.maximum(tops[2], tops[3]))
        weights = [jnp.exp2(a - top) * b for a, b in zip(tops, sums)]
        total = (weights[0] + weights[1]) + (weights[2] + weights[3])
        lse[r : r + 1, :] = top + jnp.log2(total)
        delta[r : r + 1, :] = sum(w * b for w, b in zip(weights, parts)) / total
    acc[...] = jnp.zeros(acc.shape, F32)

    def shard(r, _):
        walk, q_pos, low, hide = span_of(r, x, y, z, lengths)
        dqt[...] = jnp.zeros(dqt.shape, F32)

        def work(rows, runs, masked):
            k, v = kv[0, rows, :], kv[1, rows, :]
            dk, dv = acc[0, rows, :], acc[1, rows, :]
            for c in range(ROWS // BCHUNK):
                cols = slice(c * BCHUNK, (c + 1) * BCHUNK)
                qc, gc = q[r, cols, :], g[r, cols, :]
                s = lax.dot_general(k, qc, NT, preferred_element_type=F32) * (SCALE * LOG2E)
                if masked is None:
                    p = jnp.exp2(s - (lse[pl.ds(r, 1), cols] + hide[:, cols]))
                else:
                    p = jnp.exp2(s - lse[pl.ds(r, 1), cols])
                    p = jnp.where(seen(masked, runs, q_pos, low, cols), p, 0.0)
                dp = lax.dot_general(v, gc, NT, preferred_element_type=F32)
                ds = (p * (dp - delta[pl.ds(r, 1), cols])).astype(BF16)
                dv = dv + lax.dot_general(p.astype(BF16), gc, NN, preferred_element_type=F32)
                dk = dk + lax.dot_general(ds, qc, NN, preferred_element_type=F32)
                dqt[:, cols] = dqt[:, cols] + lax.dot_general(k, ds, TN, preferred_element_type=F32)
            acc[0, rows, :] = dk
            acc[1, rows, :] = dv

        walk(work)
        dq[r] = (dqt[...] * SCALE).T.astype(BF16)
        return 0

    lax.fori_loop(0, NX, shard, 0)

    def finish(i, _):
        rows = pl.ds(pl.multiple_of(i * 256, 256), 256)
        dkv[0, rows, :] = (acc[0, rows, :] * SCALE).astype(BF16)
        dkv[1, rows, :] = acc[1, rows, :].astype(BF16)
        return 0

    lax.fori_loop(0, SHARDS * SUB // 256, finish, 0)


def backward(lengths, q, g, kv, st, sta):
    return pl.pallas_call(
        backward_kernel,
        out_shape=(jax.ShapeDtypeStruct(q.shape, BF16), jax.ShapeDtypeStruct(kv.shape, BF16)),
        in_specs=[pl.BlockSpec(memory_space=SMEM)] + [pl.BlockSpec(memory_space=VMEM)] * 5,
        out_specs=(pl.BlockSpec(memory_space=VMEM),) * 2,
        scratch_shapes=[
            pltpu.VMEM(kv.shape, F32), pltpu.VMEM((HD, ROWS), F32),
            pltpu.VMEM((NX, ROWS), F32), pltpu.VMEM((NX, ROWS), F32),
        ],
        compiler_params=pltpu.CompilerParams(vmem_limit_bytes=24 << 20),
        cost_estimate=pl.CostEstimate(flops=10 * 3072 * ROWS * HD, transcendentals=3072 * ROWS, bytes_accessed=10 << 20),
        name="backward",
    )(lengths, q, g, kv, st, sta)


def blend_kernel(st, sta, o0, o1, o2, o3, attn, rows):
    tops = [st[0:1, :]] + [sta[e, e : e + 1, :] for e in range(1, NX)]
    sums = [st[NX : NX + 1, :]] + [sta[e, NX + e : NX + e + 1, :] for e in range(1, NX)]
    top = jnp.maximum(jnp.maximum(tops[0], tops[1]), jnp.maximum(tops[2], tops[3]))
    weights = [jnp.exp2(m - top) * l for m, l in zip(tops, sums)]
    total = (weights[0] + weights[1]) + (weights[2] + weights[3])
    share = jnp.concatenate([w / total for w in weights] + [jnp.zeros((4, ROWS), F32)], axis=0).T
    rows[...] = sum(share[:, e : e + 1] * o[...].astype(F32) for e, o in enumerate((o0, o1, o2, o3)))
    for slot in range(4):
        for h in range(GROUP):
            part = rows[pl.ds(slot * (ROWS // 4) + h, TOK // 4, stride=GROUP), :]
            attn[slot, :, HD * h : HD * h + HD] = part.astype(BF16)


def blend(st, sta, ox):
    return pl.pallas_call(
        blend_kernel,
        out_shape=jax.ShapeDtypeStruct((4, TOK // 4, GROUP * HD), BF16),
        in_specs=[pl.BlockSpec(memory_space=VMEM)] * 6,
        out_specs=pl.BlockSpec(memory_space=VMEM),
        scratch_shapes=[pltpu.VMEM((ROWS, HD), F32)],
        compiler_params=pltpu.CompilerParams(vmem_limit_bytes=24 << 20),
        cost_estimate=pl.CostEstimate(flops=8 * ROWS * HD, transcendentals=4 * ROWS, bytes_accessed=2 << 20),
        name="blend",
    )(st, sta, *ox)


def finish_kernel(dq, dqa, kvp, m_own, m_far, mixed, d_queries, d_keys, d_values):
    mixed[...] = (m_own[...].astype(F32) + m_far[...].astype(F32)).astype(BF16)
    total = dq[0].astype(F32)
    for e in range(1, NX):
        total = total + dqa[e].astype(F32)
    d_queries[...] = total.astype(BF16)
    for half, out in enumerate((d_keys, d_values)):
        for e in range(NX):
            out[SUB * e : SUB * e + SUB, :] = (
                kvp[half, e, 0].astype(F32) + kvp[half, e, 1].astype(F32)
            ).astype(BF16)


def finish(dq, dqa, kvp, m_own, m_far):
    return pl.pallas_call(
        finish_kernel,
        grid=(1,),
        out_shape=(
            jax.ShapeDtypeStruct(m_own.shape, BF16),
            jax.ShapeDtypeStruct((ROWS, HD), BF16),
            jax.ShapeDtypeStruct((TOK, HD), BF16),
            jax.ShapeDtypeStruct((TOK, HD), BF16),
        ),
        in_specs=[pl.BlockSpec((1, ROWS, HD), lambda i: (0, 0, 0))] + [pl.BlockSpec(memory_space=VMEM)] * 4,
        out_specs=(pl.BlockSpec(memory_space=VMEM),) * 4,
        compiler_params=pltpu.CompilerParams(vmem_limit_bytes=24 << 20),
        cost_estimate=pl.CostEstimate(flops=1 << 20, transcendentals=0, bytes_accessed=4 << 20),
        name="finish",
    )(dq, dqa, kvp, m_own, m_far)


def local(queries, keys, values, w_out, d_out, lengths):
    width = w_out.shape[2]
    w_flat = w_out.reshape(GROUP * HD, width)
    qa, ga, kva = gather(
        queries.reshape(ROWS, HD), keys.reshape(NX, SUB, HD), values.reshape(NX, SUB, HD), d_out, w_flat
    )
    ga = ga.reshape(NX, ROWS, HD)
    kva = kva.reshape(2, SHARDS * SUB, HD)
    *ox, st = forward(lengths, qa, ga, kva)
    sta = swap(st)
    ox[1], ox[2], ox[3], _ = lax.optimization_barrier((ox[1], ox[2], ox[3], sta))
    outer = NX * NY
    oxa = [ox[0]] + [
        lax.ppermute(ox[e], "outer", [(i, (i + outer - NY * e) % outer) for i in range(outer)])
        for e in range(1, NX)
    ]
    dq, dkv = backward(lengths, qa, ga, kva, st, sta)
    attn = blend(st, sta, oxa)
    dqa, kvp, m_own, m_far = reduce(dq, dkv.reshape(2, NX, NY, NZ, SUB, HD), attn, w_flat)
    mixed, d_queries, d_keys, d_values = finish(dq, dqa, kvp, m_own, m_far)
    return (
        mixed,
        d_queries.reshape(TOK, GROUP, HD),
        d_keys.reshape(TOK, 1, HD),
        d_values.reshape(TOK, 1, HD),
    )


def solution(mesh):
    tokens = P(("outer", "inner"), "tensor", None)
    rows = P(("outer", "inner", "tensor"), None)
    return jax.shard_map(
        local,
        mesh=mesh,
        in_specs=(tokens, tokens, tokens, P("tensor", None, None), rows, P()),
        out_specs=(rows, tokens, tokens, tokens),
        check_vma=False,
    )
```

```python
import jax
import jax.numpy as jnp
from jax import lax
from jax.experimental import pallas as pl
from jax.experimental.pallas import tpu as pltpu
from jax.sharding import PartitionSpec as P

MESH = pl.DeviceIdType.MESH
NT = (((1,), (1,)), ((), ()))
NN = (((1,), (0,)), ((), ()))
TN = (((0,), (0,)), ((), ()))
F32, BF16 = jnp.float32, jnp.bfloat16
LOG2E = 1.4426950408889634
LOW, FLOOR = -1e30, -1e20
VMEM, ANY, SMEM = pltpu.VMEM, pl.ANY, pltpu.SMEM

NX, NY, NZ = 4, 2, 8
TOK = 256
SUB = TOK // NX
GROUP = 4
ROWS = TOK * GROUP
HD = 128
SHARDS = NX * NY * NZ
WIDE = 8
CHUNK = 256
BCHUNK = 512
SCALE = HD**-0.5


def place():
    outer, z, t = lax.axis_index("outer"), lax.axis_index("inner"), lax.axis_index("tensor")
    return outer // NY, outer % NY, z, t


def at(x, y, z, t):
    return {"outer": x * NY + y, "inner": z, "tensor": t}


def remote(src, dst, send, recv, device):
    return pltpu.make_async_remote_copy(
        src_ref=src, dst_ref=dst, send_sem=send, recv_sem=recv, device_id=device, device_id_type=MESH
    )


def meet(devices):
    barrier = pltpu.get_barrier_semaphore()
    for device in devices:
        pl.semaphore_signal(barrier, inc=1, device_id=device, device_id_type=MESH)
    pl.semaphore_wait(barrier, len(devices))


PLANE = [(dx, dy) for dy in range(NY) for dx in range(NX) if (dx, dy) != (0, 0)]


def gather_kernel(q, k, v, do, w, qa, ga, kva, doa, wv, gs, gb,
                  qs, qr, ks, kr, zs, zr, ds, dr, gss, gr, ls):
    x, y, z, t = place()
    right, left = (x + 1) % NX, (x + NX - 1) % NX
    up, down = (z + 1) % NZ, (z + NZ - 1) % NZ
    partner, far = t + 1 - 2 * (t % 2), (t + 2) % 4
    other = (partner + 2) % 4
    near_rows, far_rows = pl.ds(2 * (t // 2), 2), pl.ds(2 * (1 - t // 2), 2)
    to_r, to_l, to_p = at(right, y, z, t), at(left, y, z, t), at(x, y, z, partner)
    own = [
        pltpu.make_async_copy(k.at[x], kva.at[0, x, y, z], ls.at[0]),
        pltpu.make_async_copy(v.at[x], kva.at[1, x, y, z], ls.at[1]),
        pltpu.make_async_copy(q, qa.at[0], ls.at[2]),
        pltpu.make_async_copy(w, wv, ls.at[3]),
        pltpu.make_async_copy(do, doa.at[t], ls.at[5]),
    ]
    for copy in own:
        copy.start()
    meet(
        [at((x + dx) % NX, (y + dy) % NY, z, t) for dx, dy in PLANE]
        + [at(x, y, up, t), at(x, y, down, t), at(x, y, z, partner), at(x, y, z, far)]
    )
    sent = []

    def send(src, dst, out, into, device):
        copy = remote(src, dst, out, into, device)
        copy.start()
        sent.append(copy)

    def landed(dst, out, into):
        remote(dst, dst, out, into, to_r).wait_recv()

    for i, (dx, dy) in enumerate(PLANE):
        tx, ty = (x + dx) % NX, (y + dy) % NY
        for half, run in enumerate((k, v)):
            send(run.at[tx], kva.at[half, x, y, z], ks.at[i, half], kr.at[i, half], at(tx, ty, z, t))
    send(do, doa.at[t], ds.at[0], dr.at[0], at(x, y, z, partner))
    for i in range(2):
        rows = slice(32 * i, 32 * i + 32)
        send(do.at[rows], doa.at[t, rows], ds.at[1 + i], dr.at[1 + i], at(x, y, z, far))
    send(q, qa.at[1], qs.at[0], qr.at[0], to_r)
    send(q, qa.at[3], qs.at[1], qr.at[1], to_l)
    streams = [(0, 0, 4), (1, 1, 4), (0, 1, 3), (1, 0, 3)]

    def hop(i, step):
        half, way, hops = streams[i]
        if step < hops:
            block = (z + NZ - step) % NZ if way == 0 else (z + step) % NZ
            part = kva.at[half, :, :, block]
            send(part, part, zs.at[i, step], zr.at[i, step], at(x, y, up if way == 0 else down, t))

    def turn(step, some=range(4)):
        for i in some:
            half, way, hops = streams[i]
            if step < hops:
                block = (z + NZ - step - 1) % NZ if way == 0 else (z + step + 1) % NZ
                landed(kva.at[half, :, :, block], zs.at[i, step], zr.at[i, step])
                hop(i, step + 1)

    def project(first, second, slots, halves):
        res = lax.dot_general(
            jnp.concatenate([first, second], axis=0), wv[...], NT, preferred_element_type=F32
        )
        size = 32 * len(halves)
        for i, slot in enumerate(slots):
            for h in range(GROUP):
                gs[i, pl.ds(h, size, stride=GROUP), :] = res[size * i : size * i + size, HD * h : HD * h + HD]
            for j, half in enumerate(halves):
                gb[slot, half] = gs[i, 128 * j : 128 * j + 128, :].astype(BF16)

    def spread(i, rows, halves):
        send(gb.at[rows, halves], ga.at[1, rows, halves], gss.at[3 * i], gr.at[3 * i], to_r)
        send(gb.at[rows, halves], ga.at[3, rows, halves], gss.at[3 * i + 1], gr.at[3 * i + 1], to_l)

    def relay(i, rows, halves, slot, device):
        landed(ga.at[slot, rows, halves], gss.at[3 * i + slot // 3], gr.at[3 * i + slot // 3])
        part = ga.at[slot, rows, halves]
        send(part, ga.at[2, rows, halves], gss.at[3 * i + 2], gr.at[3 * i + 2], device)

    groups = [(near_rows, slice(0, 2)), (far_rows, slice(0, 1)), (far_rows, slice(1, 2))]
    own[0].wait()
    own[1].wait()
    for i, (dx, dy) in enumerate(PLANE):
        fx, fy = (x + NX - dx) % NX, (y + NY - dy) % NY
        for half in range(2):
            landed(kva.at[half, fx, fy, z], ks.at[i, half], kr.at[i, half])
    for i in range(4):
        hop(i, 0)
    landed(doa.at[partner], ds.at[0], dr.at[0])
    own[3].wait()
    own[4].wait()
    project(doa[t], doa[partner], (t, partner), (0, 1))
    spread(0, *groups[0])
    half = ROWS // 2
    landed(qa.at[1], qs.at[0], qr.at[0])
    send(qa.at[1, 0:half], qa.at[2, 0:half], qs.at[2], qr.at[2], to_r)
    landed(qa.at[3], qs.at[1], qr.at[1])
    send(qa.at[3, half:ROWS], qa.at[2, half:ROWS], qs.at[3], qr.at[3], to_l)

    def pass_on(i):
        rows = slice(32 * i, 32 * i + 32)
        landed(doa.at[far, rows], ds.at[1 + i], dr.at[1 + i])
        send(doa.at[far, rows], doa.at[far, rows], ds.at[3 + i], dr.at[3 + i], to_p)

    def project_far(i):
        rows = slice(32 * i, 32 * i + 32)
        landed(doa.at[other, rows], ds.at[3 + i], dr.at[3 + i])
        project(doa[far, rows], doa[other, rows], (far, other), (i,))
        spread(1 + i, *groups[1 + i])

    turn(0)
    pass_on(0)
    relay(0, *groups[0], 1, to_r)
    turn(1, range(2))
    project_far(0)
    pass_on(1)
    turn(1, range(2, 4))
    turn(2, range(2))
    project_far(1)
    relay(1, *groups[1], 3, to_l)
    turn(2, range(2, 4))
    relay(2, *groups[2], 3, to_l)
    own_g = pltpu.make_async_copy(gb, ga.at[0], ls.at[4])
    own_g.start()
    turn(3)
    landed(qa.at[2, 0:half], qs.at[2], qr.at[2])
    landed(qa.at[2, half:ROWS], qs.at[3], qr.at[3])
    for i, (rows, halves) in enumerate(groups):
        last = 3 if i == 0 else 1
        landed(ga.at[last, rows, halves], gss.at[3 * i + last // 3], gr.at[3 * i + last // 3])
        landed(ga.at[2, rows, halves], gss.at[3 * i + 2], gr.at[3 * i + 2])
    for copy in sent:
        copy.wait_send()
    own[2].wait()
    own_g.wait()


def gather(q, k, v, do, w):
    dma = pltpu.SemaphoreType.DMA
    return pl.pallas_call(
        gather_kernel,
        out_shape=(
            jax.ShapeDtypeStruct((NX, ROWS, HD), BF16),
            jax.ShapeDtypeStruct((NX, 4, 2, ROWS // 8, HD), BF16),
            jax.ShapeDtypeStruct((2, NX, NY, NZ, SUB, HD), BF16),
        ),
        in_specs=[pl.BlockSpec(memory_space=ANY)] * 5,
        out_specs=(pl.BlockSpec(memory_space=ANY),) * 3,
        scratch_shapes=[
            pltpu.VMEM((4, *do.shape), BF16), pltpu.VMEM(w.shape, BF16),
            pltpu.VMEM((2, ROWS // 4, HD), F32), pltpu.VMEM((4, 2, ROWS // 8, HD), BF16),
            dma((4,)), dma((4,)), dma((7, 2)), dma((7, 2)), dma((4, 4)), dma((4, 4)),
            dma((5,)), dma((5,)), dma((9,)), dma((9,)), dma((6,)),
        ],
        compiler_params=pltpu.CompilerParams(
            collective_id=0, has_side_effects=True, vmem_limit_bytes=24 << 20
        ),
        name="gather",
    )(*(pltpu.with_memory_space_constraint(a, pltpu.HBM) for a in (q, k, v, do, w)))


def swap_kernel(st, sta, ss, sr):
    x, y, z, t = place()
    meet([at((x + dx) % NX, y, z, t) for dx in range(1, NX)])
    copies = [
        remote(st, sta.at[e], ss.at[e], sr.at[e], at((x + NX - e) % NX, y, z, t)) for e in range(1, NX)
    ]
    for copy in copies:
        copy.start()
    for copy in copies:
        copy.wait_recv()
    for copy in copies:
        copy.wait_send()


def swap(st):
    dma = pltpu.SemaphoreType.DMA
    return pl.pallas_call(
        swap_kernel,
        out_shape=jax.ShapeDtypeStruct((NX, *st.shape), st.dtype),
        in_specs=[pl.BlockSpec(memory_space=VMEM)],
        out_specs=pl.BlockSpec(memory_space=ANY),
        scratch_shapes=[dma((4,))] * 2,
        compiler_params=pltpu.CompilerParams(collective_id=1, has_side_effects=True, vmem_limit_bytes=24 << 20),
        name="swap",
    )(st)


def reduce_kernel(dq, g, share, o0, o1, o2, o3, wv, dqa, kvp, m_own, m_far, b0, b1, b2, b3, total, mix, m32, m_near, m_sum, joined, attn,
                  qs, qr, zs, zr, ks, kr, ms, mr, ls):
    x, y, z, t = place()
    up, down = (z + 1) % NZ, (z + NZ - 1) % NZ
    partner, far = t + 1 - 2 * (t % 2), (t + 2) % 4
    other = (partner + 2) % 4
    meet(
        [at((x + dx) % NX, (y + dy) % NY, z, t) for dx, dy in PLANE]
        + [at(x, y, up, t), at(x, y, down, t), at(x, y, z, partner), at(x, y, z, far)]
    )
    sent = []

    def send(src, dst, out, into, device):
        copy = remote(src, dst, out, into, device)
        copy.start()
        sent.append(copy)

    def landed(dst, out, into):
        remote(dst, dst, out, into, at(x, y, up, t)).wait_recv()

    streams = [(0, 0, 4, b0), (1, 1, 4, b1), (0, 1, 3, b2), (1, 0, 3, b3)]

    def hop(step):
        for i, (half, way, hops, buf) in enumerate(streams):
            if step < hops:
                away = hops - step
                block = (z + away) % NZ if way == 0 else (z + NZ - away) % NZ
                src = g.at[half, :, :, block]
                if step > 0:
                    landed(buf.at[step - 1], zs.at[i, step - 1], zr.at[i, step - 1])
                    buf[step - 1] = (buf[step - 1].astype(F32) + g[half, :, :, block].astype(F32)).astype(BF16)
                    src = buf.at[step - 1]
                send(src, buf.at[step], zs.at[i, step], zr.at[i, step], at(x, y, up if way == 0 else down, t))

    hop(0)
    for e in range(1, NX):
        send(dq.at[e], dqa.at[e], qs.at[e], qr.at[e], at((x + NX - e) % NX, y, z, t))
    joined[...] = sum(share[:, e : e + 1] * o[...].astype(F32) for e, o in enumerate((o0, o1, o2, o3)))
    for slot in range(4):
        for h in range(GROUP):
            part = joined[pl.ds(slot * (ROWS // 4) + h, TOK // 4, stride=GROUP), :]
            attn[slot, :, HD * h : HD * h + HD] = part.astype(BF16)
    width = mix.shape[2]
    both = jnp.concatenate([attn[partner], attn[other]], axis=0)
    for c in range(0, width, 512):
        res = jnp.dot(both, wv[:, c : c + 512], preferred_element_type=F32).astype(BF16)
        mix[0, :, c : c + 512] = res[0:64]
        mix[1, :, c : c + 512] = res[64:128]
    send(mix.at[1], m_near.at[1], ms.at[1], mr.at[1], at(x, y, z, partner))
    send(mix.at[0], m_near.at[0], ms.at[0], mr.at[0], at(x, y, z, partner))
    both = jnp.concatenate([attn[t], attn[far]], axis=0)
    for c in range(0, width, 512):
        m32[:, c : c + 512] = jnp.dot(both, wv[:, c : c + 512], preferred_element_type=F32)
    landed(m_near.at[1], ms.at[1], mr.at[1])
    m_sum[...] = (m32[64:128, :] + m_near[1].astype(F32)).astype(BF16)
    send(m_sum, m_far, ms.at[2], mr.at[2], at(x, y, z, far))
    hop(1)
    landed(m_near.at[0], ms.at[0], mr.at[0])
    m_own[...] = (m32[0:64, :] + m_near[0].astype(F32)).astype(BF16)
    hop(2)
    hop(3)
    for i, (half, way, hops, buf) in enumerate(streams):
        landed(buf.at[hops - 1], zs.at[i, hops - 1], zr.at[i, hops - 1])
    total[0] = (b0[3].astype(F32) + b2[2].astype(F32) + g[0, :, :, z].astype(F32)).astype(BF16)
    total[1] = (b1[3].astype(F32) + b3[2].astype(F32) + g[1, :, :, z].astype(F32)).astype(BF16)
    for i, (dx, dy) in enumerate(PLANE):
        tx, ty = (x + dx) % NX, (y + dy) % NY
        send(total.at[:, tx, ty], kvp.at[:, x, y], ks.at[i], kr.at[i], at(tx, ty, z, t))
    own = pltpu.make_async_copy(total.at[:, x, y], kvp.at[:, x, y], ls.at[0])
    own.start()
    for e in range(1, NX):
        landed(dqa.at[e], qs.at[e], qr.at[e])
    landed(m_far, ms.at[2], mr.at[2])
    for i, (dx, dy) in enumerate(PLANE):
        fx, fy = (x + NX - dx) % NX, (y + NY - dy) % NY
        landed(kvp.at[:, fx, fy], ks.at[i], kr.at[i])
    for copy in sent:
        copy.wait_send()
    own.wait()


def reduce(dq, g, share, ox, w):
    dma = pltpu.SemaphoreType.DMA
    width = w.shape[1]
    block = (NX, NY, SUB, HD)
    return pl.pallas_call(
        reduce_kernel,
        out_shape=(
            jax.ShapeDtypeStruct(dq.shape, BF16),
            jax.ShapeDtypeStruct((2, *block), BF16),
            jax.ShapeDtypeStruct((64, width), BF16),
            jax.ShapeDtypeStruct((64, width), BF16),
        ),
        in_specs=[
            pl.BlockSpec(memory_space=ANY), *[pl.BlockSpec(memory_space=VMEM)] * 7,
        ],
        out_specs=(
            pl.BlockSpec(memory_space=ANY), pl.BlockSpec(memory_space=ANY),
            pl.BlockSpec(memory_space=VMEM), pl.BlockSpec(memory_space=ANY),
        ),
        scratch_shapes=[
            pltpu.VMEM((4, *block), BF16), pltpu.VMEM((4, *block), BF16),
            pltpu.VMEM((3, *block), BF16), pltpu.VMEM((3, *block), BF16),
            pltpu.VMEM((2, *block), BF16),
            pltpu.VMEM((2, 64, width), BF16), pltpu.VMEM((128, width), F32),
            pltpu.VMEM((2, 64, width), BF16), pltpu.VMEM((64, width), BF16),
            pltpu.VMEM((ROWS, HD), F32), pltpu.VMEM((4, TOK // 4, GROUP * HD), BF16),
            dma((4,)), dma((4,)), dma((4, 4)), dma((4, 4)), dma((7,)), dma((7,)), dma((3,)), dma((3,)), dma((1,)),
        ],
        compiler_params=pltpu.CompilerParams(
            collective_id=2, has_side_effects=True, vmem_limit_bytes=24 << 20
        ),
        name="reduce",
    )(dq, g, share, *ox, w)


def begin_of(position, lengths):
    end, first = jnp.int32(0), jnp.zeros_like(position)
    for j in range(lengths.shape[0]):
        end = end + lengths[j]
        first = jnp.where(position >= end, end, first)
    return first


def span_of(r, x, y, z, lengths, trims):
    s = ((x + NX - r) % NX) * (NY * NZ) + y * NZ + z
    start = s * TOK
    first = begin_of(start, lengths)
    f = first // TOK
    q_pos = start + lax.broadcasted_iota(jnp.int32, (1, ROWS), 1) // GROUP
    low = begin_of(q_pos, lengths)
    hide = jnp.where(low > start, jnp.float32(-LOW), jnp.float32(0.0))
    count, rest = (s - f + 1) // WIDE, (s - f + 1) % WIDE

    def tile(want, runs):
        a = jnp.minimum(want, SHARDS - runs)
        base = a * TOK + x * SUB
        whole = (a == want) & (base + (runs - 1) * TOK + SUB - 1 <= start)
        if not trims:
            whole = whole & (base >= first)
        rows = pl.ds(pl.multiple_of(a * SUB, SUB), runs * SUB)
        return rows, base, want * TOK, whole

    def walk(work):
        def step(i, _):
            rows, base, floor, whole = tile(f + WIDE * i, WIDE)
            pl.when(whole)(lambda: work(rows, WIDE, None, first - base))
            pl.when(jnp.logical_not(whole))(lambda: work(rows, WIDE, (base, floor), None))
            return 0

        wide = count + (rest > WIDE // 2).astype(jnp.int32)
        lax.fori_loop(0, wide, step, 0)
        for runs in (4, 2):
            rows, base, floor, _ = tile(f + WIDE * count, runs)
            here = (rest <= runs) & (rest > runs // 2) if runs > 2 else (rest <= runs) & (rest > 0)
            pl.when(here)(lambda: work(rows, runs, (base, floor), None))

    return walk, q_pos, low, hide


def seen(place_of, runs, q_pos, low, cols):
    base, floor = place_of
    low, high = jnp.maximum(low[:, cols], floor) - base, q_pos[:, cols] - base
    i = lax.broadcasted_iota(jnp.int32, (runs * SUB, low.shape[1]), 0)
    k_rel = i + (i // SUB) * (TOK - SUB)
    return (k_rel >= low) & (k_rel <= high)


def trim(value, skip, fill):
    head = value[0:SUB]
    i = lax.broadcasted_iota(jnp.int32, head.shape, 0)
    return jnp.concatenate([jnp.where(i >= skip, head, fill), value[SUB:]], axis=0)


def forward_kernel(lengths, q, g, kv, o0, o1, o2, o3, st, out, m, part, acc, buf, top):
    x, y, z, _ = place()

    def shard(r, _):
        walk, q_pos, low, hide = span_of(r, x, y, z, lengths, True)
        m[...] = jnp.full(m.shape, FLOOR, F32)
        part[...] = jnp.zeros(part.shape, F32)
        acc[...] = jnp.zeros(acc.shape, F32)

        def work(rows, runs, masked, skip):
            k, v = kv[0, rows, :], kv[1, rows, :]
            size = runs * SUB
            span = [slice(c * CHUNK, (c + 1) * CHUNK) for c in range(ROWS // CHUNK)]
            for cols in span:
                s = lax.dot_general(k, q[r, cols, :], NT, preferred_element_type=F32) * (SCALE * LOG2E)
                if masked is not None:
                    s = jnp.where(seen(masked, runs, q_pos, low, cols), s, LOW)
                else:
                    s = trim(s, skip, LOW)
                buf[0:size, cols] = s
                top[:, cols] = jnp.max(s.reshape(size // 8, 8, CHUNK), axis=0)
            old = m[...]
            most = jnp.max(top[...], axis=0, keepdims=True)
            new = jnp.maximum(old, most if masked is not None else most - hide)
            m[...] = new
            shrink = jnp.exp2(old - new)
            if masked is None:
                new = new + hide
            for cols in span:
                p = jnp.exp2(buf[0:size, cols] - new[:, cols])
                part[:, cols] = part[:, cols] * shrink[:, cols] + jnp.sum(
                    p.reshape(size // 8, 8, CHUNK), axis=0
                )
                acc[:, cols] = acc[:, cols] * shrink[:, cols] + lax.dot_general(
                    v, p.astype(BF16), TN, preferred_element_type=F32
                )

        walk(work)
        total = jnp.sum(part[...], axis=0, keepdims=True)
        o = (acc[...] / jnp.where(total > 0, total, 1.0)).T
        out[r] = o.astype(BF16)
        prod = o * g[r].astype(F32)
        high = prod.astype(BF16)
        rest = (prod - high.astype(F32)).astype(BF16)
        ones = jnp.ones((8, HD), BF16)
        sums = lax.dot_general(ones, high, NT, preferred_element_type=F32) + lax.dot_general(
            ones, rest, NT, preferred_element_type=F32
        )
        st[pl.ds(r, 1), :] = m[...]
        st[pl.ds(r + NX, 1), :] = total
        st[pl.ds(r + 2 * NX, 1), :] = sums[0:1, :]
        return 0

    lax.fori_loop(0, NX, shard, 0)
    for e, ref in enumerate((o0, o1, o2, o3)):
        ref[...] = out[e]
    st[3 * NX : 4 * NX, :] = jnp.zeros((NX, ROWS), F32)


def forward(lengths, q, g, kv):
    return pl.pallas_call(
        forward_kernel,
        out_shape=(jax.ShapeDtypeStruct((ROWS, HD), BF16),) * NX + (jax.ShapeDtypeStruct((4 * NX, ROWS), F32),),
        in_specs=[pl.BlockSpec(memory_space=SMEM)] + [pl.BlockSpec(memory_space=VMEM)] * 3,
        out_specs=(pl.BlockSpec(memory_space=VMEM),) * 5,
        scratch_shapes=[
            pltpu.VMEM((NX, ROWS, HD), BF16),
            pltpu.VMEM((1, ROWS), F32), pltpu.VMEM((8, ROWS), F32), pltpu.VMEM((HD, ROWS), F32),
            pltpu.VMEM((WIDE * SUB, ROWS), F32), pltpu.VMEM((8, ROWS), F32),
        ],
        compiler_params=pltpu.CompilerParams(vmem_limit_bytes=24 << 20),
        cost_estimate=pl.CostEstimate(flops=4 * 3072 * ROWS * HD, transcendentals=3072 * ROWS, bytes_accessed=8 << 20),
        name="forward",
    )(lengths, q, g, kv)


def backward_kernel(lengths, q, g, kv, st, sta, dq, dkv, share, acc, dqt, lse, delta):
    x, y, z, _ = place()
    for r in range(NX):
        tops, sums, parts = [], [], []
        for e in range(NX):
            k = (r + e) % NX
            rows = st if e == 0 else sta.at[e]
            tops.append(rows[k : k + 1, :])
            sums.append(rows[NX + k : NX + k + 1, :])
            parts.append(rows[2 * NX + k : 2 * NX + k + 1, :])
        top = jnp.maximum(jnp.maximum(tops[0], tops[1]), jnp.maximum(tops[2], tops[3]))
        weights = [jnp.exp2(a - top) * b for a, b in zip(tops, sums)]
        total = (weights[0] + weights[1]) + (weights[2] + weights[3])
        lse[r : r + 1, :] = top + jnp.log2(total)
        delta[r : r + 1, :] = sum(w * b for w, b in zip(weights, parts)) / total
        if r == 0:
            cols = [w / total for w in weights] + [jnp.zeros((8 - NX, ROWS), F32)]
            share[...] = jnp.concatenate(cols, axis=0).T
    acc[...] = jnp.zeros(acc.shape, F32)

    def shard(r, _):
        walk, q_pos, low, hide = span_of(r, x, y, z, lengths, False)
        dqt[...] = jnp.zeros(dqt.shape, F32)

        def work(rows, runs, masked, skip):
            k, v = kv[0, rows, :], kv[1, rows, :]
            dk, dv = acc[0, rows, :], acc[1, rows, :]
            for c in range(ROWS // BCHUNK):
                cols = slice(c * BCHUNK, (c + 1) * BCHUNK)
                qc, gc = q[r, cols, :], g[r, cols, :]
                s = lax.dot_general(k, qc, NT, preferred_element_type=F32) * (SCALE * LOG2E)
                if masked is None:
                    p = jnp.exp2(s - (lse[pl.ds(r, 1), cols] + hide[:, cols]))
                else:
                    p = jnp.exp2(s - lse[pl.ds(r, 1), cols])
                    p = jnp.where(seen(masked, runs, q_pos, low, cols), p, 0.0)
                dp = lax.dot_general(v, gc, NT, preferred_element_type=F32)
                ds = (p * (dp - delta[pl.ds(r, 1), cols])).astype(BF16)
                dv = dv + lax.dot_general(p.astype(BF16), gc, NN, preferred_element_type=F32)
                dk = dk + lax.dot_general(ds, qc, NN, preferred_element_type=F32)
                dqt[:, cols] = dqt[:, cols] + lax.dot_general(k, ds, TN, preferred_element_type=F32)
            acc[0, rows, :] = dk
            acc[1, rows, :] = dv

        walk(work)
        dq[r] = (dqt[...] * SCALE).T.astype(BF16)
        return 0

    lax.fori_loop(0, NX, shard, 0)

    def finish(i, _):
        rows = pl.ds(pl.multiple_of(i * 256, 256), 256)
        dkv[0, rows, :] = (acc[0, rows, :] * SCALE).astype(BF16)
        dkv[1, rows, :] = acc[1, rows, :].astype(BF16)
        return 0

    lax.fori_loop(0, SHARDS * SUB // 256, finish, 0)


def backward(lengths, q, g, kv, st, sta):
    return pl.pallas_call(
        backward_kernel,
        out_shape=(
            jax.ShapeDtypeStruct(q.shape, BF16),
            jax.ShapeDtypeStruct(kv.shape, BF16),
            jax.ShapeDtypeStruct((ROWS, 8), F32),
        ),
        in_specs=[pl.BlockSpec(memory_space=SMEM)] + [pl.BlockSpec(memory_space=VMEM)] * 5,
        out_specs=(pl.BlockSpec(memory_space=VMEM),) * 3,
        scratch_shapes=[
            pltpu.VMEM(kv.shape, F32), pltpu.VMEM((HD, ROWS), F32),
            pltpu.VMEM((NX, ROWS), F32), pltpu.VMEM((NX, ROWS), F32),
        ],
        compiler_params=pltpu.CompilerParams(vmem_limit_bytes=24 << 20),
        cost_estimate=pl.CostEstimate(flops=10 * 3072 * ROWS * HD, transcendentals=3072 * ROWS, bytes_accessed=10 << 20),
        name="backward",
    )(lengths, q, g, kv, st, sta)


def finish_kernel(dq, dqa, kvp, m_own, m_far, mixed, d_queries, d_keys, d_values):
    mixed[...] = (m_own[...].astype(F32) + m_far[...].astype(F32)).astype(BF16)
    total = dq[0].astype(F32)
    for e in range(1, NX):
        total = total + dqa[e].astype(F32)
    d_queries[...] = total.astype(BF16)
    for half, out in enumerate((d_keys, d_values)):
        for e in range(NX):
            out[SUB * e : SUB * e + SUB, :] = (
                kvp[half, e, 0].astype(F32) + kvp[half, e, 1].astype(F32)
            ).astype(BF16)


def finish(dq, dqa, kvp, m_own, m_far):
    return pl.pallas_call(
        finish_kernel,
        grid=(1,),
        out_shape=(
            jax.ShapeDtypeStruct(m_own.shape, BF16),
            jax.ShapeDtypeStruct((ROWS, HD), BF16),
            jax.ShapeDtypeStruct((TOK, HD), BF16),
            jax.ShapeDtypeStruct((TOK, HD), BF16),
        ),
        in_specs=[pl.BlockSpec((1, ROWS, HD), lambda i: (0, 0, 0))] + [pl.BlockSpec(memory_space=VMEM)] * 4,
        out_specs=(pl.BlockSpec(memory_space=VMEM),) * 4,
        compiler_params=pltpu.CompilerParams(vmem_limit_bytes=24 << 20),
        cost_estimate=pl.CostEstimate(flops=1 << 20, transcendentals=0, bytes_accessed=4 << 20),
        name="finish",
    )(dq, dqa, kvp, m_own, m_far)


def local(queries, keys, values, w_out, d_out, lengths):
    width = w_out.shape[2]
    w_flat = w_out.reshape(GROUP * HD, width)
    qa, ga, kva = gather(
        queries.reshape(ROWS, HD), keys.reshape(NX, SUB, HD), values.reshape(NX, SUB, HD), d_out, w_flat
    )
    ga = ga.reshape(NX, ROWS, HD)
    kva = kva.reshape(2, SHARDS * SUB, HD)
    *ox, st = forward(lengths, qa, ga, kva)
    sta = swap(st)
    ox[1], ox[2], ox[3], _ = lax.optimization_barrier((ox[1], ox[2], ox[3], sta))
    outer = NX * NY
    oxa = [ox[0]] + [
        lax.ppermute(ox[e], "outer", [(i, (i + outer - NY * e) % outer) for i in range(outer)])
        for e in range(1, NX)
    ]
    dq, dkv, share = backward(lengths, qa, ga, kva, st, sta)
    dqa, kvp, m_own, m_far = reduce(dq, dkv.reshape(2, NX, NY, NZ, SUB, HD), share, oxa, w_flat)
    mixed, d_queries, d_keys, d_values = finish(dq, dqa, kvp, m_own, m_far)
    return (
        mixed,
        d_queries.reshape(TOK, GROUP, HD),
        d_keys.reshape(TOK, 1, HD),
        d_values.reshape(TOK, 1, HD),
    )


def solution(mesh):
    tokens = P(("outer", "inner"), "tensor", None)
    rows = P(("outer", "inner", "tensor"), None)
    return jax.shard_map(
        local,
        mesh=mesh,
        in_specs=(tokens, tokens, tokens, P("tensor", None, None), rows, P()),
        out_specs=(rows, tokens, tokens, tokens),
        check_vma=False,
    )
```

```python
import jax
import jax.numpy as jnp
from jax import lax
from jax.experimental import pallas as pl
from jax.experimental.pallas import tpu as pltpu
from jax.sharding import PartitionSpec as P

MESH = pl.DeviceIdType.MESH
NT = (((1,), (1,)), ((), ()))
NN = (((1,), (0,)), ((), ()))
TN = (((0,), (0,)), ((), ()))
F32, BF16 = jnp.float32, jnp.bfloat16
LOG2E = 1.4426950408889634
LOW, FLOOR = -1e30, -1e20
VMEM, ANY, SMEM = pltpu.VMEM, pl.ANY, pltpu.SMEM

NX, NY, NZ = 4, 2, 8
TOK = 256
SUB = TOK // NX
GROUP = 4
ROWS = TOK * GROUP
HD = 128
SHARDS = NX * NY * NZ
WIDE = 8
CHUNK = 256
BCHUNK = 512
SCALE = HD**-0.5


def place():
    outer, z, t = lax.axis_index("outer"), lax.axis_index("inner"), lax.axis_index("tensor")
    return outer // NY, outer % NY, z, t


def at(x, y, z, t):
    return {"outer": x * NY + y, "inner": z, "tensor": t}


def remote(src, dst, send, recv, device):
    return pltpu.make_async_remote_copy(
        src_ref=src, dst_ref=dst, send_sem=send, recv_sem=recv, device_id=device, device_id_type=MESH
    )


def meet(devices):
    barrier = pltpu.get_barrier_semaphore()
    for device in devices:
        pl.semaphore_signal(barrier, inc=1, device_id=device, device_id_type=MESH)
    pl.semaphore_wait(barrier, len(devices))


PLANE = [(dx, dy) for dy in range(NY) for dx in range(NX) if (dx, dy) != (0, 0)]


def gather_kernel(q, k, v, do, w, qa, ga, kva, doa, wv, gs, gb,
                  qs, qr, ks, kr, zs, zr, ds, dr, gss, gr, ls):
    x, y, z, t = place()
    right, left = (x + 1) % NX, (x + NX - 1) % NX
    up, down = (z + 1) % NZ, (z + NZ - 1) % NZ
    partner, far = t + 1 - 2 * (t % 2), (t + 2) % 4
    other = (partner + 2) % 4
    near_rows, far_rows = pl.ds(2 * (t // 2), 2), pl.ds(2 * (1 - t // 2), 2)
    to_r, to_l, to_p = at(right, y, z, t), at(left, y, z, t), at(x, y, z, partner)
    own = [
        pltpu.make_async_copy(k.at[x], kva.at[0, x, y, z], ls.at[0]),
        pltpu.make_async_copy(v.at[x], kva.at[1, x, y, z], ls.at[1]),
        pltpu.make_async_copy(q, qa.at[0], ls.at[2]),
        pltpu.make_async_copy(w, wv, ls.at[3]),
        pltpu.make_async_copy(do, doa.at[t], ls.at[5]),
    ]
    for copy in own:
        copy.start()
    meet(
        [at((x + dx) % NX, (y + dy) % NY, z, t) for dx, dy in PLANE]
        + [at(x, y, up, t), at(x, y, down, t), at(x, y, z, partner), at(x, y, z, far)]
    )
    sent = []

    def send(src, dst, out, into, device):
        copy = remote(src, dst, out, into, device)
        copy.start()
        sent.append(copy)

    def landed(dst, out, into):
        remote(dst, dst, out, into, to_r).wait_recv()

    for i, (dx, dy) in enumerate(PLANE):
        tx, ty = (x + dx) % NX, (y + dy) % NY
        for half, run in enumerate((k, v)):
            send(run.at[tx], kva.at[half, x, y, z], ks.at[i, half], kr.at[i, half], at(tx, ty, z, t))
    send(do, doa.at[t], ds.at[0], dr.at[0], at(x, y, z, partner))
    for i in range(2):
        rows = slice(32 * i, 32 * i + 32)
        send(do.at[rows], doa.at[t, rows], ds.at[1 + i], dr.at[1 + i], at(x, y, z, far))
    send(q, qa.at[1], qs.at[0], qr.at[0], to_r)
    send(q, qa.at[3], qs.at[1], qr.at[1], to_l)
    streams = [(0, 0, 4), (1, 1, 4), (0, 1, 3), (1, 0, 3)]

    def hop(i, step):
        half, way, hops = streams[i]
        if step < hops:
            block = (z + NZ - step) % NZ if way == 0 else (z + step) % NZ
            part = kva.at[half, :, :, block]
            send(part, part, zs.at[i, step], zr.at[i, step], at(x, y, up if way == 0 else down, t))

    def turn(step, some=range(4)):
        for i in some:
            half, way, hops = streams[i]
            if step < hops:
                block = (z + NZ - step - 1) % NZ if way == 0 else (z + step + 1) % NZ
                landed(kva.at[half, :, :, block], zs.at[i, step], zr.at[i, step])
                hop(i, step + 1)

    def project(first, second, slots, halves):
        res = lax.dot_general(
            jnp.concatenate([first, second], axis=0), wv[...], NT, preferred_element_type=F32
        )
        size = 32 * len(halves)
        for i, slot in enumerate(slots):
            for h in range(GROUP):
                gs[i, pl.ds(h, size, stride=GROUP), :] = res[size * i : size * i + size, HD * h : HD * h + HD]
            for j, half in enumerate(halves):
                gb[slot, half] = gs[i, 128 * j : 128 * j + 128, :].astype(BF16)

    def spread(i, rows, halves):
        send(gb.at[rows, halves], ga.at[1, rows, halves], gss.at[3 * i], gr.at[3 * i], to_r)
        send(gb.at[rows, halves], ga.at[3, rows, halves], gss.at[3 * i + 1], gr.at[3 * i + 1], to_l)

    def relay(i, rows, halves, slot, device):
        landed(ga.at[slot, rows, halves], gss.at[3 * i + slot // 3], gr.at[3 * i + slot // 3])
        part = ga.at[slot, rows, halves]
        send(part, ga.at[2, rows, halves], gss.at[3 * i + 2], gr.at[3 * i + 2], device)

    groups = [(near_rows, slice(0, 2)), (far_rows, slice(0, 1)), (far_rows, slice(1, 2))]
    own[0].wait()
    own[1].wait()
    for i, (dx, dy) in enumerate(PLANE):
        fx, fy = (x + NX - dx) % NX, (y + NY - dy) % NY
        for half in range(2):
            landed(kva.at[half, fx, fy, z], ks.at[i, half], kr.at[i, half])
    for i in range(4):
        hop(i, 0)
    landed(doa.at[partner], ds.at[0], dr.at[0])
    own[3].wait()
    own[4].wait()
    project(doa[t], doa[partner], (t, partner), (0, 1))
    spread(0, *groups[0])
    half = ROWS // 2
    landed(qa.at[1], qs.at[0], qr.at[0])
    send(qa.at[1, 0:half], qa.at[2, 0:half], qs.at[2], qr.at[2], to_r)
    landed(qa.at[3], qs.at[1], qr.at[1])
    send(qa.at[3, half:ROWS], qa.at[2, half:ROWS], qs.at[3], qr.at[3], to_l)

    def pass_on(i):
        rows = slice(32 * i, 32 * i + 32)
        landed(doa.at[far, rows], ds.at[1 + i], dr.at[1 + i])
        send(doa.at[far, rows], doa.at[far, rows], ds.at[3 + i], dr.at[3 + i], to_p)

    def project_far(i):
        rows = slice(32 * i, 32 * i + 32)
        landed(doa.at[other, rows], ds.at[3 + i], dr.at[3 + i])
        project(doa[far, rows], doa[other, rows], (far, other), (i,))
        spread(1 + i, *groups[1 + i])

    turn(0)
    pass_on(0)
    relay(0, *groups[0], 1, to_r)
    turn(1, range(2))
    project_far(0)
    pass_on(1)
    turn(1, range(2, 4))
    turn(2, range(2))
    project_far(1)
    relay(1, *groups[1], 3, to_l)
    turn(2, range(2, 4))
    relay(2, *groups[2], 3, to_l)
    own_g = pltpu.make_async_copy(gb, ga.at[0], ls.at[4])
    own_g.start()
    turn(3)
    landed(qa.at[2, 0:half], qs.at[2], qr.at[2])
    landed(qa.at[2, half:ROWS], qs.at[3], qr.at[3])
    for i, (rows, halves) in enumerate(groups):
        last = 3 if i == 0 else 1
        landed(ga.at[last, rows, halves], gss.at[3 * i + last // 3], gr.at[3 * i + last // 3])
        landed(ga.at[2, rows, halves], gss.at[3 * i + 2], gr.at[3 * i + 2])
    for copy in sent:
        copy.wait_send()
    own[2].wait()
    own_g.wait()


def gather(q, k, v, do, w):
    dma = pltpu.SemaphoreType.DMA
    return pl.pallas_call(
        gather_kernel,
        out_shape=(
            jax.ShapeDtypeStruct((NX, ROWS, HD), BF16),
            jax.ShapeDtypeStruct((NX, 4, 2, ROWS // 8, HD), BF16),
            jax.ShapeDtypeStruct((2, NX, NY, NZ, SUB, HD), BF16),
        ),
        in_specs=[pl.BlockSpec(memory_space=ANY)] * 5,
        out_specs=(pl.BlockSpec(memory_space=ANY),) * 3,
        scratch_shapes=[
            pltpu.VMEM((4, *do.shape), BF16), pltpu.VMEM(w.shape, BF16),
            pltpu.VMEM((2, ROWS // 4, HD), F32), pltpu.VMEM((4, 2, ROWS // 8, HD), BF16),
            dma((4,)), dma((4,)), dma((7, 2)), dma((7, 2)), dma((4, 4)), dma((4, 4)),
            dma((5,)), dma((5,)), dma((9,)), dma((9,)), dma((6,)),
        ],
        compiler_params=pltpu.CompilerParams(
            collective_id=0, has_side_effects=True, vmem_limit_bytes=24 << 20
        ),
        name="gather",
    )(*(pltpu.with_memory_space_constraint(a, pltpu.HBM) for a in (q, k, v, do, w)))


def swap_kernel(st, sta, ss, sr):
    x, y, z, t = place()
    meet([at((x + dx) % NX, y, z, t) for dx in range(1, NX)])
    copies = [
        remote(st, sta.at[e], ss.at[e], sr.at[e], at((x + NX - e) % NX, y, z, t)) for e in range(1, NX)
    ]
    for copy in copies:
        copy.start()
    for copy in copies:
        copy.wait_recv()
    for copy in copies:
        copy.wait_send()


def swap(st):
    dma = pltpu.SemaphoreType.DMA
    return pl.pallas_call(
        swap_kernel,
        out_shape=jax.ShapeDtypeStruct((NX, *st.shape), st.dtype),
        in_specs=[pl.BlockSpec(memory_space=VMEM)],
        out_specs=pl.BlockSpec(memory_space=ANY),
        scratch_shapes=[dma((4,))] * 2,
        compiler_params=pltpu.CompilerParams(collective_id=1, has_side_effects=True, vmem_limit_bytes=24 << 20),
        name="swap",
    )(st)


def reduce_kernel(dq, g, share, o0, o1, o2, o3, wv, dqa, kvp, m_own, m_far, b0, b1, b2, b3, total, mix, m32, m_near, m_sum, joined, attn,
                  qs, qr, zs, zr, ks, kr, ms, mr, ls):
    x, y, z, t = place()
    up, down = (z + 1) % NZ, (z + NZ - 1) % NZ
    partner, far = t + 1 - 2 * (t % 2), (t + 2) % 4
    other = (partner + 2) % 4
    meet(
        [at((x + dx) % NX, (y + dy) % NY, z, t) for dx, dy in PLANE]
        + [at(x, y, up, t), at(x, y, down, t), at(x, y, z, partner), at(x, y, z, far)]
    )
    sent = []

    def send(src, dst, out, into, device):
        copy = remote(src, dst, out, into, device)
        copy.start()
        sent.append(copy)

    def landed(dst, out, into):
        remote(dst, dst, out, into, at(x, y, up, t)).wait_recv()

    streams = [(0, 0, 4, b0), (1, 1, 4, b1), (0, 1, 3, b2), (1, 0, 3, b3)]

    def hop(step):
        for i, (half, way, hops, buf) in enumerate(streams):
            if step < hops:
                away = hops - step
                block = (z + away) % NZ if way == 0 else (z + NZ - away) % NZ
                src = g.at[half, :, :, block]
                if step > 0:
                    landed(buf.at[step - 1], zs.at[i, step - 1], zr.at[i, step - 1])
                    buf[step - 1] = (buf[step - 1].astype(F32) + g[half, :, :, block].astype(F32)).astype(BF16)
                    src = buf.at[step - 1]
                send(src, buf.at[step], zs.at[i, step], zr.at[i, step], at(x, y, up if way == 0 else down, t))

    hop(0)
    for e in range(1, NX):
        send(dq.at[e], dqa.at[e], qs.at[e], qr.at[e], at((x + NX - e) % NX, y, z, t))
    joined[...] = sum(share[:, e : e + 1] * o[...].astype(F32) for e, o in enumerate((o0, o1, o2, o3)))
    for slot in range(4):
        for h in range(GROUP):
            part = joined[pl.ds(slot * (ROWS // 4) + h, TOK // 4, stride=GROUP), :]
            attn[slot, :, HD * h : HD * h + HD] = part.astype(BF16)
    width = mix.shape[2]
    both = jnp.concatenate([attn[partner], attn[other]], axis=0)
    for c in range(0, width, 512):
        res = jnp.dot(both, wv[:, c : c + 512], preferred_element_type=F32).astype(BF16)
        mix[0, :, c : c + 512] = res[0:64]
        mix[1, :, c : c + 512] = res[64:128]
    send(mix.at[1], m_near.at[1], ms.at[1], mr.at[1], at(x, y, z, partner))
    send(mix.at[0], m_near.at[0], ms.at[0], mr.at[0], at(x, y, z, partner))
    both = jnp.concatenate([attn[t], attn[far]], axis=0)
    for c in range(0, width, 512):
        m32[:, c : c + 512] = jnp.dot(both, wv[:, c : c + 512], preferred_element_type=F32)
    landed(m_near.at[1], ms.at[1], mr.at[1])
    m_sum[...] = (m32[64:128, :] + m_near[1].astype(F32)).astype(BF16)
    send(m_sum, m_far, ms.at[2], mr.at[2], at(x, y, z, far))
    hop(1)
    landed(m_near.at[0], ms.at[0], mr.at[0])
    m_own[...] = (m32[0:64, :] + m_near[0].astype(F32)).astype(BF16)
    hop(2)
    hop(3)
    for i, (half, way, hops, buf) in enumerate(streams):
        landed(buf.at[hops - 1], zs.at[i, hops - 1], zr.at[i, hops - 1])
    total[0] = (b0[3].astype(F32) + b2[2].astype(F32) + g[0, :, :, z].astype(F32)).astype(BF16)
    total[1] = (b1[3].astype(F32) + b3[2].astype(F32) + g[1, :, :, z].astype(F32)).astype(BF16)
    for i, (dx, dy) in enumerate(PLANE):
        tx, ty = (x + dx) % NX, (y + dy) % NY
        send(total.at[:, tx, ty], kvp.at[:, x, y], ks.at[i], kr.at[i], at(tx, ty, z, t))
    own = pltpu.make_async_copy(total.at[:, x, y], kvp.at[:, x, y], ls.at[0])
    own.start()
    for e in range(1, NX):
        landed(dqa.at[e], qs.at[e], qr.at[e])
    landed(m_far, ms.at[2], mr.at[2])
    for i, (dx, dy) in enumerate(PLANE):
        fx, fy = (x + NX - dx) % NX, (y + NY - dy) % NY
        landed(kvp.at[:, fx, fy], ks.at[i], kr.at[i])
    for copy in sent:
        copy.wait_send()
    own.wait()


def reduce(dq, g, share, ox, w):
    dma = pltpu.SemaphoreType.DMA
    width = w.shape[1]
    block = (NX, NY, SUB, HD)
    return pl.pallas_call(
        reduce_kernel,
        out_shape=(
            jax.ShapeDtypeStruct(dq.shape, BF16),
            jax.ShapeDtypeStruct((2, *block), BF16),
            jax.ShapeDtypeStruct((64, width), BF16),
            jax.ShapeDtypeStruct((64, width), BF16),
        ),
        in_specs=[
            pl.BlockSpec(memory_space=ANY), *[pl.BlockSpec(memory_space=VMEM)] * 7,
        ],
        out_specs=(
            pl.BlockSpec(memory_space=ANY), pl.BlockSpec(memory_space=ANY),
            pl.BlockSpec(memory_space=VMEM), pl.BlockSpec(memory_space=ANY),
        ),
        scratch_shapes=[
            pltpu.VMEM((4, *block), BF16), pltpu.VMEM((4, *block), BF16),
            pltpu.VMEM((3, *block), BF16), pltpu.VMEM((3, *block), BF16),
            pltpu.VMEM((2, *block), BF16),
            pltpu.VMEM((2, 64, width), BF16), pltpu.VMEM((128, width), F32),
            pltpu.VMEM((2, 64, width), BF16), pltpu.VMEM((64, width), BF16),
            pltpu.VMEM((ROWS, HD), F32), pltpu.VMEM((4, TOK // 4, GROUP * HD), BF16),
            dma((4,)), dma((4,)), dma((4, 4)), dma((4, 4)), dma((7,)), dma((7,)), dma((3,)), dma((3,)), dma((1,)),
        ],
        compiler_params=pltpu.CompilerParams(
            collective_id=2, has_side_effects=True, vmem_limit_bytes=24 << 20
        ),
        name="reduce",
    )(dq, g, share, *ox, w)


def begin_of(position, lengths):
    end, first = jnp.int32(0), jnp.zeros_like(position)
    for j in range(lengths.shape[0]):
        end = end + lengths[j]
        first = jnp.where(position >= end, end, first)
    return first


def span_of(r, x, y, z, lengths, trims):
    s = ((x + NX - r) % NX) * (NY * NZ) + y * NZ + z
    start = s * TOK
    first = begin_of(start, lengths)
    f = first // TOK
    q_pos = start + lax.broadcasted_iota(jnp.int32, (1, ROWS), 1) // GROUP
    low = begin_of(q_pos, lengths)
    hide = jnp.where(low > start, jnp.float32(-LOW), jnp.float32(0.0))
    count, rest = (s - f + 1) // WIDE, (s - f + 1) % WIDE

    def tile(want, runs):
        a = jnp.minimum(want, SHARDS - runs)
        base = a * TOK + x * SUB
        whole = (a == want) & (base + (runs - 1) * TOK + SUB - 1 <= start)
        if not trims:
            whole = whole & (base >= first)
        rows = pl.ds(pl.multiple_of(a * SUB, SUB), runs * SUB)
        return rows, base, want * TOK, whole

    def walk(work):
        def step(i, _):
            rows, base, floor, whole = tile(f + WIDE * i, WIDE)
            pl.when(whole)(lambda: work(rows, WIDE, None, first - base))
            pl.when(jnp.logical_not(whole))(lambda: work(rows, WIDE, (base, floor), None))
            return 0

        wide = count + (rest > WIDE // 2).astype(jnp.int32)
        lax.fori_loop(0, wide, step, 0)
        for runs in (4, 2):
            rows, base, floor, _ = tile(f + WIDE * count, runs)
            here = (rest <= runs) & (rest > runs // 2) if runs > 2 else (rest <= runs) & (rest > 0)
            pl.when(here)(lambda: work(rows, runs, (base, floor), None))

    return walk, q_pos, low, hide


def seen(place_of, runs, q_pos, low, cols):
    base, floor = place_of
    low, high = jnp.maximum(low[:, cols], floor) - base, q_pos[:, cols] - base
    i = lax.broadcasted_iota(jnp.int32, (runs * SUB, low.shape[1]), 0)
    k_rel = i + (i // SUB) * (TOK - SUB)
    return (k_rel >= low) & (k_rel <= high)


def trim(value, skip, fill):
    head = value[0:SUB]
    i = lax.broadcasted_iota(jnp.int32, head.shape, 0)
    return jnp.concatenate([jnp.where(i >= skip, head, fill), value[SUB:]], axis=0)


def forward_kernel(lengths, q, g, kv, o0, o1, o2, o3, st, out, m, part, acc, buf, top):
    x, y, z, _ = place()

    def shard(r, _):
        walk, q_pos, low, hide = span_of(r, x, y, z, lengths, True)
        m[...] = jnp.full(m.shape, FLOOR, F32)
        part[...] = jnp.zeros(part.shape, F32)
        acc[...] = jnp.zeros(acc.shape, F32)

        def work(rows, runs, masked, skip):
            k, v = kv[0, rows, :], kv[1, rows, :]
            size = runs * SUB
            span = [slice(c * CHUNK, (c + 1) * CHUNK) for c in range(ROWS // CHUNK)]
            for cols in span:
                s = lax.dot_general(k, q[r, cols, :], NT, preferred_element_type=F32) * (SCALE * LOG2E)
                if masked is not None:
                    s = jnp.where(seen(masked, runs, q_pos, low, cols), s, LOW)
                else:
                    s = trim(s, skip, LOW)
                buf[0:size, cols] = s
                top[:, cols] = jnp.max(s.reshape(size // 8, 8, CHUNK), axis=0)
            old = m[...]
            most = jnp.max(top[...], axis=0, keepdims=True)
            new = jnp.maximum(old, most if masked is not None else most - hide)
            m[...] = new
            shrink = jnp.exp2(old - new)
            if masked is None:
                new = new + hide
            for cols in span:
                p = jnp.exp2(buf[0:size, cols] - new[:, cols])
                part[:, cols] = part[:, cols] * shrink[:, cols] + jnp.sum(
                    p.reshape(size // 8, 8, CHUNK), axis=0
                )
                acc[:, cols] = acc[:, cols] * shrink[:, cols] + lax.dot_general(
                    v, p.astype(BF16), TN, preferred_element_type=F32
                )

        walk(work)
        total = jnp.sum(part[...], axis=0, keepdims=True)
        o = (acc[...] / jnp.where(total > 0, total, 1.0)).T
        out[r] = o.astype(BF16)
        prod = o * g[r].astype(F32)
        high = prod.astype(BF16)
        rest = (prod - high.astype(F32)).astype(BF16)
        ones = jnp.ones((8, HD), BF16)
        sums = lax.dot_general(ones, high, NT, preferred_element_type=F32) + lax.dot_general(
            ones, rest, NT, preferred_element_type=F32
        )
        st[pl.ds(r, 1), :] = jnp.where(total > 0, m[...] + jnp.log2(total), LOW)
        st[pl.ds(r + NX, 1), :] = sums[0:1, :]
        return 0

    lax.fori_loop(0, NX, shard, 0)
    for e, ref in enumerate((o0, o1, o2, o3)):
        ref[...] = out[e]


def forward(lengths, q, g, kv):
    return pl.pallas_call(
        forward_kernel,
        out_shape=(jax.ShapeDtypeStruct((ROWS, HD), BF16),) * NX + (jax.ShapeDtypeStruct((2 * NX, ROWS), F32),),
        in_specs=[pl.BlockSpec(memory_space=SMEM)] + [pl.BlockSpec(memory_space=VMEM)] * 3,
        out_specs=(pl.BlockSpec(memory_space=VMEM),) * 5,
        scratch_shapes=[
            pltpu.VMEM((NX, ROWS, HD), BF16),
            pltpu.VMEM((1, ROWS), F32), pltpu.VMEM((8, ROWS), F32), pltpu.VMEM((HD, ROWS), F32),
            pltpu.VMEM((WIDE * SUB, ROWS), F32), pltpu.VMEM((8, ROWS), F32),
        ],
        compiler_params=pltpu.CompilerParams(vmem_limit_bytes=24 << 20),
        cost_estimate=pl.CostEstimate(flops=4 * 3072 * ROWS * HD, transcendentals=3072 * ROWS, bytes_accessed=8 << 20),
        name="forward",
    )(lengths, q, g, kv)


def backward_kernel(lengths, q, g, kv, st, sta, dq, dkv, share, acc, dqt, lse, delta):
    x, y, z, _ = place()
    for r in range(NX):
        tops, parts = [], []
        for e in range(NX):
            k = (r + e) % NX
            rows = st if e == 0 else sta.at[e]
            tops.append(rows[k : k + 1, :])
            parts.append(rows[NX + k : NX + k + 1, :])
        top = jnp.maximum(jnp.maximum(tops[0], tops[1]), jnp.maximum(tops[2], tops[3]))
        weights = [jnp.exp2(a - top) for a in tops]
        total = (weights[0] + weights[1]) + (weights[2] + weights[3])
        lse[r : r + 1, :] = top + jnp.log2(total)
        delta[r : r + 1, :] = sum(w * b for w, b in zip(weights, parts)) / total
        if r == 0:
            cols = [w / total for w in weights] + [jnp.zeros((8 - NX, ROWS), F32)]
            share[...] = jnp.concatenate(cols, axis=0).T
    acc[...] = jnp.zeros(acc.shape, F32)

    def shard(r, _):
        walk, q_pos, low, hide = span_of(r, x, y, z, lengths, False)
        dqt[...] = jnp.zeros(dqt.shape, F32)

        def work(rows, runs, masked, skip):
            k, v = kv[0, rows, :], kv[1, rows, :]
            dk, dv = acc[0, rows, :], acc[1, rows, :]
            for c in range(ROWS // BCHUNK):
                cols = slice(c * BCHUNK, (c + 1) * BCHUNK)
                qc, gc = q[r, cols, :], g[r, cols, :]
                s = lax.dot_general(k, qc, NT, preferred_element_type=F32) * (SCALE * LOG2E)
                if masked is None:
                    p = jnp.exp2(s - (lse[pl.ds(r, 1), cols] + hide[:, cols]))
                else:
                    p = jnp.exp2(s - lse[pl.ds(r, 1), cols])
                    p = jnp.where(seen(masked, runs, q_pos, low, cols), p, 0.0)
                dp = lax.dot_general(v, gc, NT, preferred_element_type=F32)
                ds = (p * (dp - delta[pl.ds(r, 1), cols])).astype(BF16)
                dv = dv + lax.dot_general(p.astype(BF16), gc, NN, preferred_element_type=F32)
                dk = dk + lax.dot_general(ds, qc, NN, preferred_element_type=F32)
                dqt[:, cols] = dqt[:, cols] + lax.dot_general(k, ds, TN, preferred_element_type=F32)
            acc[0, rows, :] = dk
            acc[1, rows, :] = dv

        walk(work)
        dq[r] = (dqt[...] * SCALE).T.astype(BF16)
        return 0

    lax.fori_loop(0, NX, shard, 0)

    def finish(i, _):
        rows = pl.ds(pl.multiple_of(i * 256, 256), 256)
        dkv[0, rows, :] = (acc[0, rows, :] * SCALE).astype(BF16)
        dkv[1, rows, :] = acc[1, rows, :].astype(BF16)
        return 0

    lax.fori_loop(0, SHARDS * SUB // 256, finish, 0)


def backward(lengths, q, g, kv, st, sta):
    return pl.pallas_call(
        backward_kernel,
        out_shape=(
            jax.ShapeDtypeStruct(q.shape, BF16),
            jax.ShapeDtypeStruct(kv.shape, BF16),
            jax.ShapeDtypeStruct((ROWS, 8), F32),
        ),
        in_specs=[pl.BlockSpec(memory_space=SMEM)] + [pl.BlockSpec(memory_space=VMEM)] * 5,
        out_specs=(pl.BlockSpec(memory_space=VMEM),) * 3,
        scratch_shapes=[
            pltpu.VMEM(kv.shape, F32), pltpu.VMEM((HD, ROWS), F32),
            pltpu.VMEM((NX, ROWS), F32), pltpu.VMEM((NX, ROWS), F32),
        ],
        compiler_params=pltpu.CompilerParams(vmem_limit_bytes=24 << 20),
        cost_estimate=pl.CostEstimate(flops=10 * 3072 * ROWS * HD, transcendentals=3072 * ROWS, bytes_accessed=10 << 20),
        name="backward",
    )(lengths, q, g, kv, st, sta)


def finish_kernel(dq, dqa, kvp, m_own, m_far, mixed, d_queries, d_keys, d_values):
    mixed[...] = (m_own[...].astype(F32) + m_far[...].astype(F32)).astype(BF16)
    total = dq[0].astype(F32)
    for e in range(1, NX):
        total = total + dqa[e].astype(F32)
    d_queries[...] = total.astype(BF16)
    for half, out in enumerate((d_keys, d_values)):
        for e in range(NX):
            out[SUB * e : SUB * e + SUB, :] = (
                kvp[half, e, 0].astype(F32) + kvp[half, e, 1].astype(F32)
            ).astype(BF16)


def finish(dq, dqa, kvp, m_own, m_far):
    return pl.pallas_call(
        finish_kernel,
        grid=(1,),
        out_shape=(
            jax.ShapeDtypeStruct(m_own.shape, BF16),
            jax.ShapeDtypeStruct((ROWS, HD), BF16),
            jax.ShapeDtypeStruct((TOK, HD), BF16),
            jax.ShapeDtypeStruct((TOK, HD), BF16),
        ),
        in_specs=[pl.BlockSpec((1, ROWS, HD), lambda i: (0, 0, 0))] + [pl.BlockSpec(memory_space=VMEM)] * 4,
        out_specs=(pl.BlockSpec(memory_space=VMEM),) * 4,
        compiler_params=pltpu.CompilerParams(vmem_limit_bytes=24 << 20),
        cost_estimate=pl.CostEstimate(flops=1 << 20, transcendentals=0, bytes_accessed=4 << 20),
        name="finish",
    )(dq, dqa, kvp, m_own, m_far)


def local(queries, keys, values, w_out, d_out, lengths):
    width = w_out.shape[2]
    w_flat = w_out.reshape(GROUP * HD, width)
    qa, ga, kva = gather(
        queries.reshape(ROWS, HD), keys.reshape(NX, SUB, HD), values.reshape(NX, SUB, HD), d_out, w_flat
    )
    ga = ga.reshape(NX, ROWS, HD)
    kva = kva.reshape(2, SHARDS * SUB, HD)
    *ox, st = forward(lengths, qa, ga, kva)
    sta = swap(st)
    ox[1], ox[2], ox[3], _ = lax.optimization_barrier((ox[1], ox[2], ox[3], sta))
    outer = NX * NY
    oxa = [ox[0]] + [
        lax.ppermute(ox[e], "outer", [(i, (i + outer - NY * e) % outer) for i in range(outer)])
        for e in range(1, NX)
    ]
    dq, dkv, share = backward(lengths, qa, ga, kva, st, sta)
    dqa, kvp, m_own, m_far = reduce(dq, dkv.reshape(2, NX, NY, NZ, SUB, HD), share, oxa, w_flat)
    mixed, d_queries, d_keys, d_values = finish(dq, dqa, kvp, m_own, m_far)
    return (
        mixed,
        d_queries.reshape(TOK, GROUP, HD),
        d_keys.reshape(TOK, 1, HD),
        d_values.reshape(TOK, 1, HD),
    )


def solution(mesh):
    tokens = P(("outer", "inner"), "tensor", None)
    rows = P(("outer", "inner", "tensor"), None)
    return jax.shard_map(
        local,
        mesh=mesh,
        in_specs=(tokens, tokens, tokens, P("tensor", None, None), rows, P()),
        out_specs=(rows, tokens, tokens, tokens),
        check_vma=False,
    )
```

```python
import jax
import jax.numpy as jnp
from jax import lax
from jax.experimental import pallas as pl
from jax.experimental.pallas import tpu as pltpu
from jax.sharding import PartitionSpec as P

MESH = pl.DeviceIdType.MESH
NT = (((1,), (1,)), ((), ()))
NN = (((1,), (0,)), ((), ()))
TN = (((0,), (0,)), ((), ()))
F32, BF16 = jnp.float32, jnp.bfloat16
LOG2E = 1.4426950408889634
LOW, FLOOR = -1e30, -1e20
VMEM, ANY, SMEM = pltpu.VMEM, pl.ANY, pltpu.SMEM

NX, NY, NZ = 4, 2, 8
TOK = 256
SUB = TOK // NX
GROUP = 4
ROWS = TOK * GROUP
HD = 128
SHARDS = NX * NY * NZ
WIDE = 8
CHUNK = 256
BCHUNK = 512
SCALE = HD**-0.5


def place():
    outer, z, t = lax.axis_index("outer"), lax.axis_index("inner"), lax.axis_index("tensor")
    return outer // NY, outer % NY, z, t


def at(x, y, z, t):
    return {"outer": x * NY + y, "inner": z, "tensor": t}


def remote(src, dst, send, recv, device):
    return pltpu.make_async_remote_copy(
        src_ref=src, dst_ref=dst, send_sem=send, recv_sem=recv, device_id=device, device_id_type=MESH
    )


def meet(devices):
    barrier = pltpu.get_barrier_semaphore()
    for device in devices:
        pl.semaphore_signal(barrier, inc=1, device_id=device, device_id_type=MESH)
    pl.semaphore_wait(barrier, len(devices))


PLANE = [(dx, dy) for dy in range(NY) for dx in range(NX) if (dx, dy) != (0, 0)]


def gather_kernel(q, k, v, do, w, qa, ga, kva, doa, wv, gs, gb,
                  qs, qr, ks, kr, zs, zr, ds, dr, gss, gr, ls):
    x, y, z, t = place()
    right, left = (x + 1) % NX, (x + NX - 1) % NX
    up, down = (z + 1) % NZ, (z + NZ - 1) % NZ
    partner, far = t + 1 - 2 * (t % 2), (t + 2) % 4
    other = (partner + 2) % 4
    near_half, far_half = t // 2, 1 - t // 2
    to_r, to_l = at(right, y, z, t), at(left, y, z, t)
    own = [
        pltpu.make_async_copy(k.at[x], kva.at[0, x, y, z], ls.at[0]),
        pltpu.make_async_copy(v.at[x], kva.at[1, x, y, z], ls.at[1]),
        pltpu.make_async_copy(q, qa.at[0], ls.at[2]),
        pltpu.make_async_copy(w, wv, ls.at[3]),
        pltpu.make_async_copy(do, doa.at[t], ls.at[5]),
    ]
    for copy in own:
        copy.start()
    meet(
        [at((x + dx) % NX, (y + dy) % NY, z, t) for dx, dy in PLANE]
        + [at(x, y, up, t), at(x, y, down, t), at(x, y, z, partner), at(x, y, z, far)]
    )
    sent = []

    def send(src, dst, out, into, device):
        copy = remote(src, dst, out, into, device)
        copy.start()
        sent.append(copy)

    def landed(dst, out, into):
        remote(dst, dst, out, into, to_r).wait_recv()

    for i, (dx, dy) in enumerate(PLANE):
        tx, ty = (x + dx) % NX, (y + dy) % NY
        for half, run in enumerate((k, v)):
            send(run.at[tx], kva.at[half, x, y, z], ks.at[i, half], kr.at[i, half], at(tx, ty, z, t))
    send(do, doa.at[t], ds.at[0], dr.at[0], at(x, y, z, partner))
    for i in range(2):
        rows = slice(32 * i, 32 * i + 32)
        send(do.at[rows], doa.at[t, rows], ds.at[1 + i], dr.at[1 + i], at(x, y, z, far))
    send(q, qa.at[1], qs.at[0], qr.at[0], to_r)
    send(q, qa.at[3], qs.at[1], qr.at[1], to_l)
    streams = [(0, 0, 4), (1, 1, 4), (0, 1, 3), (1, 0, 3)]

    def hop(i, step):
        half, way, hops = streams[i]
        if step < hops:
            block = (z + NZ - step) % NZ if way == 0 else (z + step) % NZ
            part = kva.at[half, :, :, block]
            send(part, part, zs.at[i, step], zr.at[i, step], at(x, y, up if way == 0 else down, t))

    def turn(step):
        for i, (half, way, hops) in enumerate(streams):
            if step < hops:
                block = (z + NZ - step - 1) % NZ if way == 0 else (z + step + 1) % NZ
                landed(kva.at[half, :, :, block], zs.at[i, step], zr.at[i, step])
                hop(i, step + 1)

    def project(first, second, slots, half):
        both = jnp.concatenate([first, second], axis=0)
        res = lax.dot_general(both, wv[...], NT, preferred_element_type=F32)
        for i, slot in enumerate(slots):
            for h in range(GROUP):
                gs[i, pl.ds(h, 64, stride=GROUP), :] = res[64 * i : 64 * i + 64, HD * h : HD * h + HD]
            gb[slot] = gs[i].astype(BF16)
        rows = pl.ds(2 * half, 2)
        i = 0 if half is near_half else 2
        send(gb.at[rows], ga.at[1, rows], gss.at[i], gr.at[i], to_r)
        send(gb.at[rows], ga.at[3, rows], gss.at[i + 1], gr.at[i + 1], to_l)

    own[0].wait()
    own[1].wait()
    for i, (dx, dy) in enumerate(PLANE):
        fx, fy = (x + NX - dx) % NX, (y + NY - dy) % NY
        for half in range(2):
            landed(kva.at[half, fx, fy, z], ks.at[i, half], kr.at[i, half])
    for i in range(4):
        hop(i, 0)
    landed(doa.at[partner], ds.at[0], dr.at[0])
    own[3].wait()
    own[4].wait()
    project(doa[t], doa[partner], (t, partner), near_half)
    half = ROWS // 2
    landed(qa.at[1], qs.at[0], qr.at[0])
    send(qa.at[1, 0:half], qa.at[2, 0:half], qs.at[2], qr.at[2], to_r)
    landed(qa.at[3], qs.at[1], qr.at[1])
    send(qa.at[3, half:ROWS], qa.at[2, half:ROWS], qs.at[3], qr.at[3], to_l)
    turn(0)
    for i in range(2):
        rows = slice(32 * i, 32 * i + 32)
        landed(doa.at[far, rows], ds.at[1 + i], dr.at[1 + i])
        send(doa.at[far, rows], doa.at[far, rows], ds.at[3 + i], dr.at[3 + i], at(x, y, z, partner))
    turn(1)
    for i in range(2):
        landed(doa.at[other, 32 * i : 32 * i + 32], ds.at[3 + i], dr.at[3 + i])
    project(doa[far], doa[other], (far, other), far_half)
    turn(2)
    near_rows, far_rows = pl.ds(2 * near_half, 2), pl.ds(2 * far_half, 2)
    landed(ga.at[1, near_rows], gss.at[0], gr.at[0])
    send(ga.at[1, near_rows], ga.at[2, near_rows], gss.at[4], gr.at[4], to_r)
    landed(ga.at[3, near_rows], gss.at[1], gr.at[1])
    landed(ga.at[3, far_rows], gss.at[3], gr.at[3])
    send(ga.at[3, far_rows], ga.at[2, far_rows], gss.at[5], gr.at[5], to_l)
    landed(ga.at[1, far_rows], gss.at[2], gr.at[2])
    own_g = pltpu.make_async_copy(gb, ga.at[0], ls.at[4])
    own_g.start()
    turn(3)
    landed(qa.at[2, 0:half], qs.at[2], qr.at[2])
    landed(qa.at[2, half:ROWS], qs.at[3], qr.at[3])
    landed(ga.at[2, near_rows], gss.at[4], gr.at[4])
    landed(ga.at[2, far_rows], gss.at[5], gr.at[5])
    for copy in sent:
        copy.wait_send()
    own[2].wait()
    own_g.wait()


def gather(q, k, v, do, w):
    dma = pltpu.SemaphoreType.DMA
    return pl.pallas_call(
        gather_kernel,
        out_shape=(
            jax.ShapeDtypeStruct((NX, ROWS, HD), BF16),
            jax.ShapeDtypeStruct((NX, 4, ROWS // 4, HD), BF16),
            jax.ShapeDtypeStruct((2, NX, NY, NZ, SUB, HD), BF16),
        ),
        in_specs=[pl.BlockSpec(memory_space=ANY)] * 5,
        out_specs=(pl.BlockSpec(memory_space=ANY),) * 3,
        scratch_shapes=[
            pltpu.VMEM((4, *do.shape), BF16), pltpu.VMEM(w.shape, BF16),
            pltpu.VMEM((2, ROWS // 4, HD), F32), pltpu.VMEM((4, ROWS // 4, HD), BF16),
            dma((4,)), dma((4,)), dma((7, 2)), dma((7, 2)), dma((4, 4)), dma((4, 4)),
            dma((5,)), dma((5,)), dma((6,)), dma((6,)), dma((6,)),
        ],
        compiler_params=pltpu.CompilerParams(
            collective_id=0, has_side_effects=True, vmem_limit_bytes=24 << 20
        ),
        name="gather",
    )(*(pltpu.with_memory_space_constraint(a, pltpu.HBM) for a in (q, k, v, do, w)))


def swap_kernel(st, sta, ss, sr):
    x, y, z, t = place()
    meet([at((x + dx) % NX, y, z, t) for dx in range(1, NX)])
    copies = [
        remote(st, sta.at[e], ss.at[e], sr.at[e], at((x + NX - e) % NX, y, z, t)) for e in range(1, NX)
    ]
    for copy in copies:
        copy.start()
    for copy in copies:
        copy.wait_recv()
    for copy in copies:
        copy.wait_send()


def swap(st):
    dma = pltpu.SemaphoreType.DMA
    return pl.pallas_call(
        swap_kernel,
        out_shape=jax.ShapeDtypeStruct((NX, *st.shape), st.dtype),
        in_specs=[pl.BlockSpec(memory_space=VMEM)],
        out_specs=pl.BlockSpec(memory_space=ANY),
        scratch_shapes=[dma((4,))] * 2,
        compiler_params=pltpu.CompilerParams(collective_id=1, has_side_effects=True, vmem_limit_bytes=24 << 20),
        name="swap",
    )(st)


def reduce_kernel(dq, g, share, o0, o1, o2, o3, wv, dqa, kvp, m_own, m_far, b0, b1, b2, b3, total, mix, m32, m_near, m_sum, joined, attn,
                  qs, qr, zs, zr, ks, kr, ms, mr, ls):
    x, y, z, t = place()
    up, down = (z + 1) % NZ, (z + NZ - 1) % NZ
    partner, far = t + 1 - 2 * (t % 2), (t + 2) % 4
    other = (partner + 2) % 4
    meet(
        [at((x + dx) % NX, (y + dy) % NY, z, t) for dx, dy in PLANE]
        + [at(x, y, up, t), at(x, y, down, t), at(x, y, z, partner), at(x, y, z, far)]
    )
    sent = []

    def send(src, dst, out, into, device):
        copy = remote(src, dst, out, into, device)
        copy.start()
        sent.append(copy)

    def landed(dst, out, into):
        remote(dst, dst, out, into, at(x, y, up, t)).wait_recv()

    streams = [(0, 0, 4, b0), (1, 1, 4, b1), (0, 1, 3, b2), (1, 0, 3, b3)]

    def hop(step):
        for i, (half, way, hops, buf) in enumerate(streams):
            if step < hops:
                away = hops - step
                block = (z + away) % NZ if way == 0 else (z + NZ - away) % NZ
                src = g.at[half, :, :, block]
                if step > 0:
                    landed(buf.at[step - 1], zs.at[i, step - 1], zr.at[i, step - 1])
                    buf[step - 1] = (buf[step - 1].astype(F32) + g[half, :, :, block].astype(F32)).astype(BF16)
                    src = buf.at[step - 1]
                send(src, buf.at[step], zs.at[i, step], zr.at[i, step], at(x, y, up if way == 0 else down, t))

    hop(0)
    for e in range(1, NX):
        send(dq.at[e], dqa.at[e], qs.at[e], qr.at[e], at((x + NX - e) % NX, y, z, t))
    joined[...] = sum(share[:, e : e + 1] * o[...].astype(F32) for e, o in enumerate((o0, o1, o2, o3)))
    for slot in range(4):
        for h in range(GROUP):
            part = joined[pl.ds(slot * (ROWS // 4) + h, TOK // 4, stride=GROUP), :]
            attn[slot, :, HD * h : HD * h + HD] = part.astype(BF16)
    width = mix.shape[2]
    both = jnp.concatenate([attn[partner], attn[other]], axis=0)
    for c in range(0, width, 512):
        res = jnp.dot(both, wv[:, c : c + 512], preferred_element_type=F32).astype(BF16)
        mix[0, :, c : c + 512] = res[0:64]
        mix[1, :, c : c + 512] = res[64:128]
    send(mix.at[1], m_near.at[1], ms.at[1], mr.at[1], at(x, y, z, partner))
    send(mix.at[0], m_near.at[0], ms.at[0], mr.at[0], at(x, y, z, partner))
    both = jnp.concatenate([attn[t], attn[far]], axis=0)
    for c in range(0, width, 512):
        m32[:, c : c + 512] = jnp.dot(both, wv[:, c : c + 512], preferred_element_type=F32)
    landed(m_near.at[1], ms.at[1], mr.at[1])
    m_sum[...] = (m32[64:128, :] + m_near[1].astype(F32)).astype(BF16)
    send(m_sum, m_far, ms.at[2], mr.at[2], at(x, y, z, far))
    hop(1)
    landed(m_near.at[0], ms.at[0], mr.at[0])
    m_own[...] = (m32[0:64, :] + m_near[0].astype(F32)).astype(BF16)
    hop(2)
    hop(3)
    for i, (half, way, hops, buf) in enumerate(streams):
        landed(buf.at[hops - 1], zs.at[i, hops - 1], zr.at[i, hops - 1])
    total[0] = (b0[3].astype(F32) + b2[2].astype(F32) + g[0, :, :, z].astype(F32)).astype(BF16)
    total[1] = (b1[3].astype(F32) + b3[2].astype(F32) + g[1, :, :, z].astype(F32)).astype(BF16)
    for i, (dx, dy) in enumerate(PLANE):
        tx, ty = (x + dx) % NX, (y + dy) % NY
        send(total.at[:, tx, ty], kvp.at[:, x, y], ks.at[i], kr.at[i], at(tx, ty, z, t))
    own = pltpu.make_async_copy(total.at[:, x, y], kvp.at[:, x, y], ls.at[0])
    own.start()
    for e in range(1, NX):
        landed(dqa.at[e], qs.at[e], qr.at[e])
    landed(m_far, ms.at[2], mr.at[2])
    for i, (dx, dy) in enumerate(PLANE):
        fx, fy = (x + NX - dx) % NX, (y + NY - dy) % NY
        landed(kvp.at[:, fx, fy], ks.at[i], kr.at[i])
    for copy in sent:
        copy.wait_send()
    own.wait()


def reduce(dq, g, share, ox, w):
    dma = pltpu.SemaphoreType.DMA
    width = w.shape[1]
    block = (NX, NY, SUB, HD)
    return pl.pallas_call(
        reduce_kernel,
        out_shape=(
            jax.ShapeDtypeStruct(dq.shape, BF16),
            jax.ShapeDtypeStruct((2, *block), BF16),
            jax.ShapeDtypeStruct((64, width), BF16),
            jax.ShapeDtypeStruct((64, width), BF16),
        ),
        in_specs=[
            pl.BlockSpec(memory_space=ANY), *[pl.BlockSpec(memory_space=VMEM)] * 7,
        ],
        out_specs=(
            pl.BlockSpec(memory_space=ANY), pl.BlockSpec(memory_space=ANY),
            pl.BlockSpec(memory_space=VMEM), pl.BlockSpec(memory_space=ANY),
        ),
        scratch_shapes=[
            pltpu.VMEM((4, *block), BF16), pltpu.VMEM((4, *block), BF16),
            pltpu.VMEM((3, *block), BF16), pltpu.VMEM((3, *block), BF16),
            pltpu.VMEM((2, *block), BF16),
            pltpu.VMEM((2, 64, width), BF16), pltpu.VMEM((128, width), F32),
            pltpu.VMEM((2, 64, width), BF16), pltpu.VMEM((64, width), BF16),
            pltpu.VMEM((ROWS, HD), F32), pltpu.VMEM((4, TOK // 4, GROUP * HD), BF16),
            dma((4,)), dma((4,)), dma((4, 4)), dma((4, 4)), dma((7,)), dma((7,)), dma((3,)), dma((3,)), dma((1,)),
        ],
        compiler_params=pltpu.CompilerParams(
            collective_id=2, has_side_effects=True, vmem_limit_bytes=24 << 20
        ),
        name="reduce",
    )(dq, g, share, *ox, w)


def begin_of(position, lengths):
    end, first = jnp.int32(0), jnp.zeros_like(position)
    for j in range(lengths.shape[0]):
        end = end + lengths[j]
        first = jnp.where(position >= end, end, first)
    return first


def span_of(r, x, y, z, lengths, trims):
    s = ((x + NX - r) % NX) * (NY * NZ) + y * NZ + z
    start = s * TOK
    first = begin_of(start, lengths)
    f = first // TOK
    q_pos = start + lax.broadcasted_iota(jnp.int32, (1, ROWS), 1) // GROUP
    low = begin_of(q_pos, lengths)
    hide = jnp.where(low > start, jnp.float32(-LOW), jnp.float32(0.0))
    count, rest = (s - f + 1) // WIDE, (s - f + 1) % WIDE

    def tile(want, runs):
        a = jnp.minimum(want, SHARDS - runs)
        base = a * TOK + x * SUB
        whole = (a == want) & (base + (runs - 1) * TOK + SUB - 1 <= start)
        if not trims:
            whole = whole & (base >= first)
        rows = pl.ds(pl.multiple_of(a * SUB, SUB), runs * SUB)
        return rows, base, want * TOK, whole

    def walk(work):
        def step(i, _):
            rows, base, floor, whole = tile(f + WIDE * i, WIDE)
            pl.when(whole)(lambda: work(rows, WIDE, None, first - base))
            pl.when(jnp.logical_not(whole))(lambda: work(rows, WIDE, (base, floor), None))
            return 0

        wide = count + (rest > WIDE // 2).astype(jnp.int32)
        lax.fori_loop(0, wide, step, 0)
        for runs in (4, 2):
            rows, base, floor, _ = tile(f + WIDE * count, runs)
            here = (rest <= runs) & (rest > runs // 2) if runs > 2 else (rest <= runs) & (rest > 0)
            pl.when(here)(lambda: work(rows, runs, (base, floor), None))

    return walk, q_pos, low, hide


def seen(place_of, runs, q_pos, low, cols):
    base, floor = place_of
    low, high = jnp.maximum(low[:, cols], floor) - base, q_pos[:, cols] - base
    i = lax.broadcasted_iota(jnp.int32, (runs * SUB, low.shape[1]), 0)
    k_rel = i + (i // SUB) * (TOK - SUB)
    return (k_rel >= low) & (k_rel <= high)


def trim(value, skip, fill):
    head = value[0:SUB]
    i = lax.broadcasted_iota(jnp.int32, head.shape, 0)
    return jnp.concatenate([jnp.where(i >= skip, head, fill), value[SUB:]], axis=0)


def forward_kernel(lengths, q, g, kv, o0, o1, o2, o3, st, out, m, part, acc, buf, top):
    x, y, z, _ = place()

    def shard(r, _):
        walk, q_pos, low, hide = span_of(r, x, y, z, lengths, True)
        m[...] = jnp.full(m.shape, FLOOR, F32)
        part[...] = jnp.zeros(part.shape, F32)
        acc[...] = jnp.zeros(acc.shape, F32)

        def work(rows, runs, masked, skip):
            k, v = kv[0, rows, :], kv[1, rows, :]
            size = runs * SUB
            span = [slice(c * CHUNK, (c + 1) * CHUNK) for c in range(ROWS // CHUNK)]
            for cols in span:
                s = lax.dot_general(k, q[r, cols, :], NT, preferred_element_type=F32) * (SCALE * LOG2E)
                if masked is not None:
                    s = jnp.where(seen(masked, runs, q_pos, low, cols), s, LOW)
                else:
                    s = trim(s, skip, LOW)
                buf[0:size, cols] = s
                top[:, cols] = jnp.max(s.reshape(size // 8, 8, CHUNK), axis=0)
            old = m[...]
            most = jnp.max(top[...], axis=0, keepdims=True)
            new = jnp.maximum(old, most if masked is not None else most - hide)
            m[...] = new
            shrink = jnp.exp2(old - new)
            if masked is None:
                new = new + hide
            for cols in span:
                p = jnp.exp2(buf[0:size, cols] - new[:, cols])
                part[:, cols] = part[:, cols] * shrink[:, cols] + jnp.sum(
                    p.reshape(size // 8, 8, CHUNK), axis=0
                )
                acc[:, cols] = acc[:, cols] * shrink[:, cols] + lax.dot_general(
                    v, p.astype(BF16), TN, preferred_element_type=F32
                )

        walk(work)
        total = jnp.sum(part[...], axis=0, keepdims=True)
        o = (acc[...] / jnp.where(total > 0, total, 1.0)).T
        out[r] = o.astype(BF16)
        prod = o * g[r].astype(F32)
        high = prod.astype(BF16)
        rest = (prod - high.astype(F32)).astype(BF16)
        ones = jnp.ones((8, HD), BF16)
        sums = lax.dot_general(ones, high, NT, preferred_element_type=F32) + lax.dot_general(
            ones, rest, NT, preferred_element_type=F32
        )
        st[pl.ds(r, 1), :] = jnp.where(total > 0, m[...] + jnp.log2(total), LOW)
        st[pl.ds(r + NX, 1), :] = sums[0:1, :]
        return 0

    lax.fori_loop(0, NX, shard, 0)
    for e, ref in enumerate((o0, o1, o2, o3)):
        ref[...] = out[e]


def forward(lengths, q, g, kv):
    return pl.pallas_call(
        forward_kernel,
        out_shape=(jax.ShapeDtypeStruct((ROWS, HD), BF16),) * NX + (jax.ShapeDtypeStruct((2 * NX, ROWS), F32),),
        in_specs=[pl.BlockSpec(memory_space=SMEM)] + [pl.BlockSpec(memory_space=VMEM)] * 3,
        out_specs=(pl.BlockSpec(memory_space=VMEM),) * 5,
        scratch_shapes=[
            pltpu.VMEM((NX, ROWS, HD), BF16),
            pltpu.VMEM((1, ROWS), F32), pltpu.VMEM((8, ROWS), F32), pltpu.VMEM((HD, ROWS), F32),
            pltpu.VMEM((WIDE * SUB, ROWS), F32), pltpu.VMEM((8, ROWS), F32),
        ],
        compiler_params=pltpu.CompilerParams(vmem_limit_bytes=24 << 20),
        cost_estimate=pl.CostEstimate(flops=4 * 3072 * ROWS * HD, transcendentals=3072 * ROWS, bytes_accessed=8 << 20),
        name="forward",
    )(lengths, q, g, kv)


def backward_kernel(lengths, q, g, kv, st, sta, dq, dkv, share, acc, dqt, lse, delta):
    x, y, z, _ = place()
    for r in range(NX):
        tops, parts = [], []
        for e in range(NX):
            k = (r + e) % NX
            rows = st if e == 0 else sta.at[e]
            tops.append(rows[k : k + 1, :])
            parts.append(rows[NX + k : NX + k + 1, :])
        top = jnp.maximum(jnp.maximum(tops[0], tops[1]), jnp.maximum(tops[2], tops[3]))
        weights = [jnp.exp2(a - top) for a in tops]
        total = (weights[0] + weights[1]) + (weights[2] + weights[3])
        lse[r : r + 1, :] = top + jnp.log2(total)
        delta[r : r + 1, :] = sum(w * b for w, b in zip(weights, parts)) / total
        if r == 0:
            cols = [w / total for w in weights] + [jnp.zeros((8 - NX, ROWS), F32)]
            share[...] = jnp.concatenate(cols, axis=0).T
    acc[...] = jnp.zeros(acc.shape, F32)

    def shard(r, _):
        walk, q_pos, low, hide = span_of(r, x, y, z, lengths, False)
        dqt[...] = jnp.zeros(dqt.shape, F32)

        def work(rows, runs, masked, skip):
            k, v = kv[0, rows, :], kv[1, rows, :]
            dk, dv = acc[0, rows, :], acc[1, rows, :]
            for c in range(ROWS // BCHUNK):
                cols = slice(c * BCHUNK, (c + 1) * BCHUNK)
                qc, gc = q[r, cols, :], g[r, cols, :]
                s = lax.dot_general(k, qc, NT, preferred_element_type=F32) * (SCALE * LOG2E)
                if masked is None:
                    p = jnp.exp2(s - (lse[pl.ds(r, 1), cols] + hide[:, cols]))
                else:
                    p = jnp.exp2(s - lse[pl.ds(r, 1), cols])
                    p = jnp.where(seen(masked, runs, q_pos, low, cols), p, 0.0)
                dp = lax.dot_general(v, gc, NT, preferred_element_type=F32)
                ds = (p * (dp - delta[pl.ds(r, 1), cols])).astype(BF16)
                dv = dv + lax.dot_general(p.astype(BF16), gc, NN, preferred_element_type=F32)
                dk = dk + lax.dot_general(ds, qc, NN, preferred_element_type=F32)
                dqt[:, cols] = dqt[:, cols] + lax.dot_general(k, ds, TN, preferred_element_type=F32)
            acc[0, rows, :] = dk
            acc[1, rows, :] = dv

        walk(work)
        dq[r] = (dqt[...] * SCALE).T.astype(BF16)
        return 0

    lax.fori_loop(0, NX, shard, 0)

    def finish(i, _):
        rows = pl.ds(pl.multiple_of(i * 256, 256), 256)
        dkv[0, rows, :] = (acc[0, rows, :] * SCALE).astype(BF16)
        dkv[1, rows, :] = acc[1, rows, :].astype(BF16)
        return 0

    lax.fori_loop(0, SHARDS * SUB // 256, finish, 0)


def backward(lengths, q, g, kv, st, sta):
    return pl.pallas_call(
        backward_kernel,
        out_shape=(
            jax.ShapeDtypeStruct(q.shape, BF16),
            jax.ShapeDtypeStruct(kv.shape, BF16),
            jax.ShapeDtypeStruct((ROWS, 8), F32),
        ),
        in_specs=[pl.BlockSpec(memory_space=SMEM)] + [pl.BlockSpec(memory_space=VMEM)] * 5,
        out_specs=(pl.BlockSpec(memory_space=VMEM),) * 3,
        scratch_shapes=[
            pltpu.VMEM(kv.shape, F32), pltpu.VMEM((HD, ROWS), F32),
            pltpu.VMEM((NX, ROWS), F32), pltpu.VMEM((NX, ROWS), F32),
        ],
        compiler_params=pltpu.CompilerParams(vmem_limit_bytes=24 << 20),
        cost_estimate=pl.CostEstimate(flops=10 * 3072 * ROWS * HD, transcendentals=3072 * ROWS, bytes_accessed=10 << 20),
        name="backward",
    )(lengths, q, g, kv, st, sta)


def finish_kernel(dq, dqa, kvp, m_own, m_far, mixed, d_queries, d_keys, d_values):
    mixed[...] = (m_own[...].astype(F32) + m_far[...].astype(F32)).astype(BF16)
    total = dq[0].astype(F32)
    for e in range(1, NX):
        total = total + dqa[e].astype(F32)
    d_queries[...] = total.astype(BF16)
    for half, out in enumerate((d_keys, d_values)):
        for e in range(NX):
            out[SUB * e : SUB * e + SUB, :] = (
                kvp[half, e, 0].astype(F32) + kvp[half, e, 1].astype(F32)
            ).astype(BF16)


def finish(dq, dqa, kvp, m_own, m_far):
    return pl.pallas_call(
        finish_kernel,
        grid=(1,),
        out_shape=(
            jax.ShapeDtypeStruct(m_own.shape, BF16),
            jax.ShapeDtypeStruct((ROWS, HD), BF16),
            jax.ShapeDtypeStruct((TOK, HD), BF16),
            jax.ShapeDtypeStruct((TOK, HD), BF16),
        ),
        in_specs=[pl.BlockSpec((1, ROWS, HD), lambda i: (0, 0, 0))] + [pl.BlockSpec(memory_space=VMEM)] * 4,
        out_specs=(pl.BlockSpec(memory_space=VMEM),) * 4,
        compiler_params=pltpu.CompilerParams(vmem_limit_bytes=24 << 20),
        cost_estimate=pl.CostEstimate(flops=1 << 20, transcendentals=0, bytes_accessed=4 << 20),
        name="finish",
    )(dq, dqa, kvp, m_own, m_far)


def local(queries, keys, values, w_out, d_out, lengths):
    width = w_out.shape[2]
    w_flat = w_out.reshape(GROUP * HD, width)
    qa, ga, kva = gather(
        queries.reshape(ROWS, HD), keys.reshape(NX, SUB, HD), values.reshape(NX, SUB, HD), d_out, w_flat
    )
    ga = ga.reshape(NX, ROWS, HD)
    kva = kva.reshape(2, SHARDS * SUB, HD)
    *ox, st = forward(lengths, qa, ga, kva)
    sta = swap(st)
    ox[1], ox[2], ox[3], _ = lax.optimization_barrier((ox[1], ox[2], ox[3], sta))
    outer = NX * NY
    oxa = [ox[0]] + [
        lax.ppermute(ox[e], "outer", [(i, (i + outer - NY * e) % outer) for i in range(outer)])
        for e in range(1, NX)
    ]
    dq, dkv, share = backward(lengths, qa, ga, kva, st, sta)
    dqa, kvp, m_own, m_far = reduce(dq, dkv.reshape(2, NX, NY, NZ, SUB, HD), share, oxa, w_flat)
    mixed, d_queries, d_keys, d_values = finish(dq, dqa, kvp, m_own, m_far)
    return (
        mixed,
        d_queries.reshape(TOK, GROUP, HD),
        d_keys.reshape(TOK, 1, HD),
        d_values.reshape(TOK, 1, HD),
    )


def solution(mesh):
    tokens = P(("outer", "inner"), "tensor", None)
    rows = P(("outer", "inner", "tensor"), None)
    return jax.shard_map(
        local,
        mesh=mesh,
        in_specs=(tokens, tokens, tokens, P("tensor", None, None), rows, P()),
        out_specs=(rows, tokens, tokens, tokens),
        check_vma=False,
    )
```

```python
import jax
import jax.numpy as jnp
from jax import lax
from jax.experimental import pallas as pl
from jax.experimental.pallas import tpu as pltpu
from jax.sharding import PartitionSpec as P

MESH = pl.DeviceIdType.MESH
NT = (((1,), (1,)), ((), ()))
NN = (((1,), (0,)), ((), ()))
TN = (((0,), (0,)), ((), ()))
F32, BF16 = jnp.float32, jnp.bfloat16
LOG2E = 1.4426950408889634
LOW, FLOOR = -1e30, -1e20
VMEM, ANY, SMEM = pltpu.VMEM, pl.ANY, pltpu.SMEM

NX, NY, NZ = 4, 2, 8
TOK = 256
SUB = TOK // NX
GROUP = 4
ROWS = TOK * GROUP
HD = 128
SHARDS = NX * NY * NZ
WIDE = 8
CHUNK = 256
BCHUNK = 512
SCALE = HD**-0.5


def place():
    outer, z, t = lax.axis_index("outer"), lax.axis_index("inner"), lax.axis_index("tensor")
    return outer // NY, outer % NY, z, t


def at(x, y, z, t):
    return {"outer": x * NY + y, "inner": z, "tensor": t}


def remote(src, dst, send, recv, device):
    return pltpu.make_async_remote_copy(
        src_ref=src, dst_ref=dst, send_sem=send, recv_sem=recv, device_id=device, device_id_type=MESH
    )


def meet(devices):
    barrier = pltpu.get_barrier_semaphore()
    for device in devices:
        pl.semaphore_signal(barrier, inc=1, device_id=device, device_id_type=MESH)
    pl.semaphore_wait(barrier, len(devices))


PLANE = [(dx, dy) for dy in range(NY) for dx in range(NX) if (dx, dy) != (0, 0)]


def gather_kernel(q, k, v, do, w, qa, ga, kva, doa, wv, gs, gb,
                  qs, qr, ks, kr, zs, zr, ds, dr, gss, gr, ls):
    x, y, z, t = place()
    right, left = (x + 1) % NX, (x + NX - 1) % NX
    up, down = (z + 1) % NZ, (z + NZ - 1) % NZ
    partner, far = t + 1 - 2 * (t % 2), (t + 2) % 4
    other = (partner + 2) % 4
    near_half, far_half = t // 2, 1 - t // 2
    to_r, to_l = at(right, y, z, t), at(left, y, z, t)
    own = [
        pltpu.make_async_copy(k.at[x], kva.at[0, x, y, z], ls.at[0]),
        pltpu.make_async_copy(v.at[x], kva.at[1, x, y, z], ls.at[1]),
        pltpu.make_async_copy(q, qa.at[0], ls.at[2]),
        pltpu.make_async_copy(w, wv, ls.at[3]),
        pltpu.make_async_copy(do, doa.at[t], ls.at[5]),
    ]
    for copy in own:
        copy.start()
    meet(
        [at((x + dx) % NX, (y + dy) % NY, z, t) for dx, dy in PLANE]
        + [at(x, y, up, t), at(x, y, down, t), at(x, y, z, partner), at(x, y, z, far)]
    )
    sent = []

    def send(src, dst, out, into, device):
        copy = remote(src, dst, out, into, device)
        copy.start()
        sent.append(copy)

    def landed(dst, out, into):
        remote(dst, dst, out, into, to_r).wait_recv()

    for i, (dx, dy) in enumerate(PLANE):
        tx, ty = (x + dx) % NX, (y + dy) % NY
        for half, run in enumerate((k, v)):
            send(run.at[tx], kva.at[half, x, y, z], ks.at[i, half], kr.at[i, half], at(tx, ty, z, t))
    send(do, doa.at[t], ds.at[0], dr.at[0], at(x, y, z, partner))
    for i in range(2):
        rows = slice(32 * i, 32 * i + 32)
        send(do.at[rows], doa.at[t, rows], ds.at[1 + i], dr.at[1 + i], at(x, y, z, far))
    send(q, qa.at[1], qs.at[0], qr.at[0], to_r)
    send(q, qa.at[3], qs.at[1], qr.at[1], to_l)
    streams = [(0, 0, 4), (1, 1, 4), (0, 1, 3), (1, 0, 3)]

    def hop(i, step):
        half, way, hops = streams[i]
        if step < hops:
            block = (z + NZ - step) % NZ if way == 0 else (z + step) % NZ
            part = kva.at[half, :, :, block]
            send(part, part, zs.at[i, step], zr.at[i, step], at(x, y, up if way == 0 else down, t))

    def turn(step):
        for i, (half, way, hops) in enumerate(streams):
            if step < hops:
                block = (z + NZ - step - 1) % NZ if way == 0 else (z + step + 1) % NZ
                landed(kva.at[half, :, :, block], zs.at[i, step], zr.at[i, step])
                hop(i, step + 1)

    def project(first, second, slots, half):
        both = jnp.concatenate([first, second], axis=0)
        res = lax.dot_general(both, wv[...], NT, preferred_element_type=F32)
        for i, slot in enumerate(slots):
            for h in range(GROUP):
                gs[i, pl.ds(h, 64, stride=GROUP), :] = res[64 * i : 64 * i + 64, HD * h : HD * h + HD]
            gb[slot] = gs[i].astype(BF16)
        rows = pl.ds(2 * half, 2)
        i = 0 if half is near_half else 2
        send(gb.at[rows], ga.at[1, rows], gss.at[i], gr.at[i], to_r)
        send(gb.at[rows], ga.at[3, rows], gss.at[i + 1], gr.at[i + 1], to_l)

    own[0].wait()
    own[1].wait()
    for i, (dx, dy) in enumerate(PLANE):
        fx, fy = (x + NX - dx) % NX, (y + NY - dy) % NY
        for half in range(2):
            landed(kva.at[half, fx, fy, z], ks.at[i, half], kr.at[i, half])
    for i in range(4):
        hop(i, 0)
    landed(doa.at[partner], ds.at[0], dr.at[0])
    own[3].wait()
    own[4].wait()
    project(doa[t], doa[partner], (t, partner), near_half)
    half = ROWS // 2
    landed(qa.at[1], qs.at[0], qr.at[0])
    send(qa.at[1, 0:half], qa.at[2, 0:half], qs.at[2], qr.at[2], to_r)
    landed(qa.at[3], qs.at[1], qr.at[1])
    send(qa.at[3, half:ROWS], qa.at[2, half:ROWS], qs.at[3], qr.at[3], to_l)
    turn(0)
    for i in range(2):
        rows = slice(32 * i, 32 * i + 32)
        landed(doa.at[far, rows], ds.at[1 + i], dr.at[1 + i])
        send(doa.at[far, rows], doa.at[far, rows], ds.at[3 + i], dr.at[3 + i], at(x, y, z, partner))
    turn(1)
    near_rows, far_rows = pl.ds(2 * near_half, 2), pl.ds(2 * far_half, 2)
    landed(ga.at[1, near_rows], gss.at[0], gr.at[0])
    send(ga.at[1, near_rows], ga.at[2, near_rows], gss.at[4], gr.at[4], to_r)
    for i in range(2):
        landed(doa.at[other, 32 * i : 32 * i + 32], ds.at[3 + i], dr.at[3 + i])
    project(doa[far], doa[other], (far, other), far_half)
    turn(2)
    landed(ga.at[3, near_rows], gss.at[1], gr.at[1])
    landed(ga.at[3, far_rows], gss.at[3], gr.at[3])
    send(ga.at[3, far_rows], ga.at[2, far_rows], gss.at[5], gr.at[5], to_l)
    landed(ga.at[1, far_rows], gss.at[2], gr.at[2])
    own_g = pltpu.make_async_copy(gb, ga.at[0], ls.at[4])
    own_g.start()
    turn(3)
    landed(qa.at[2, 0:half], qs.at[2], qr.at[2])
    landed(qa.at[2, half:ROWS], qs.at[3], qr.at[3])
    landed(ga.at[2, near_rows], gss.at[4], gr.at[4])
    landed(ga.at[2, far_rows], gss.at[5], gr.at[5])
    for copy in sent:
        copy.wait_send()
    own[2].wait()
    own_g.wait()


def gather(q, k, v, do, w):
    dma = pltpu.SemaphoreType.DMA
    return pl.pallas_call(
        gather_kernel,
        out_shape=(
            jax.ShapeDtypeStruct((NX, ROWS, HD), BF16),
            jax.ShapeDtypeStruct((NX, 4, ROWS // 4, HD), BF16),
            jax.ShapeDtypeStruct((2, NX, NY, NZ, SUB, HD), BF16),
        ),
        in_specs=[pl.BlockSpec(memory_space=ANY)] * 5,
        out_specs=(pl.BlockSpec(memory_space=ANY),) * 3,
        scratch_shapes=[
            pltpu.VMEM((4, *do.shape), BF16), pltpu.VMEM(w.shape, BF16),
            pltpu.VMEM((2, ROWS // 4, HD), F32), pltpu.VMEM((4, ROWS // 4, HD), BF16),
            dma((4,)), dma((4,)), dma((7, 2)), dma((7, 2)), dma((4, 4)), dma((4, 4)),
            dma((5,)), dma((5,)), dma((6,)), dma((6,)), dma((6,)),
        ],
        compiler_params=pltpu.CompilerParams(
            collective_id=0, has_side_effects=True, vmem_limit_bytes=24 << 20
        ),
        name="gather",
    )(*(pltpu.with_memory_space_constraint(a, pltpu.HBM) for a in (q, k, v, do, w)))


def swap_kernel(st, sta, ss, sr):
    x, y, z, t = place()
    meet([at((x + dx) % NX, y, z, t) for dx in range(1, NX)])
    copies = [
        remote(st, sta.at[e], ss.at[e], sr.at[e], at((x + NX - e) % NX, y, z, t)) for e in range(1, NX)
    ]
    for copy in copies:
        copy.start()
    for copy in copies:
        copy.wait_recv()
    for copy in copies:
        copy.wait_send()


def swap(st):
    dma = pltpu.SemaphoreType.DMA
    return pl.pallas_call(
        swap_kernel,
        out_shape=jax.ShapeDtypeStruct((NX, *st.shape), st.dtype),
        in_specs=[pl.BlockSpec(memory_space=VMEM)],
        out_specs=pl.BlockSpec(memory_space=ANY),
        scratch_shapes=[dma((4,))] * 2,
        compiler_params=pltpu.CompilerParams(collective_id=1, has_side_effects=True, vmem_limit_bytes=24 << 20),
        name="swap",
    )(st)


def reduce_kernel(dq, g, share, o0, o1, o2, o3, wv, dqa, kvp, m_own, m_far, b0, b1, b2, b3, total, mix, m32, m_near, m_sum, joined, attn,
                  qs, qr, zs, zr, ks, kr, ms, mr, ls):
    x, y, z, t = place()
    up, down = (z + 1) % NZ, (z + NZ - 1) % NZ
    partner, far = t + 1 - 2 * (t % 2), (t + 2) % 4
    other = (partner + 2) % 4
    meet(
        [at((x + dx) % NX, (y + dy) % NY, z, t) for dx, dy in PLANE]
        + [at(x, y, up, t), at(x, y, down, t), at(x, y, z, partner), at(x, y, z, far)]
    )
    sent = []

    def send(src, dst, out, into, device):
        copy = remote(src, dst, out, into, device)
        copy.start()
        sent.append(copy)

    def landed(dst, out, into):
        remote(dst, dst, out, into, at(x, y, up, t)).wait_recv()

    streams = [(0, 0, 4, b0), (1, 1, 4, b1), (0, 1, 3, b2), (1, 0, 3, b3)]

    def hop(step):
        for i, (half, way, hops, buf) in enumerate(streams):
            if step < hops:
                away = hops - step
                block = (z + away) % NZ if way == 0 else (z + NZ - away) % NZ
                src = g.at[half, :, :, block]
                if step > 0:
                    landed(buf.at[step - 1], zs.at[i, step - 1], zr.at[i, step - 1])
                    buf[step - 1] = (buf[step - 1].astype(F32) + g[half, :, :, block].astype(F32)).astype(BF16)
                    src = buf.at[step - 1]
                send(src, buf.at[step], zs.at[i, step], zr.at[i, step], at(x, y, up if way == 0 else down, t))

    hop(0)
    for e in range(1, NX):
        send(dq.at[e], dqa.at[e], qs.at[e], qr.at[e], at((x + NX - e) % NX, y, z, t))
    joined[...] = sum(share[:, e : e + 1] * o[...].astype(F32) for e, o in enumerate((o0, o1, o2, o3)))
    for slot in range(4):
        for h in range(GROUP):
            part = joined[pl.ds(slot * (ROWS // 4) + h, TOK // 4, stride=GROUP), :]
            attn[slot, :, HD * h : HD * h + HD] = part.astype(BF16)
    width = mix.shape[2]
    both = jnp.concatenate([attn[partner], attn[other]], axis=0)
    for c in range(0, width, 512):
        res = jnp.dot(both, wv[:, c : c + 512], preferred_element_type=F32).astype(BF16)
        mix[0, :, c : c + 512] = res[0:64]
        mix[1, :, c : c + 512] = res[64:128]
    send(mix.at[1], m_near.at[1], ms.at[1], mr.at[1], at(x, y, z, partner))
    send(mix.at[0], m_near.at[0], ms.at[0], mr.at[0], at(x, y, z, partner))
    both = jnp.concatenate([attn[t], attn[far]], axis=0)
    for c in range(0, width, 512):
        m32[:, c : c + 512] = jnp.dot(both, wv[:, c : c + 512], preferred_element_type=F32)
    landed(m_near.at[1], ms.at[1], mr.at[1])
    m_sum[...] = (m32[64:128, :] + m_near[1].astype(F32)).astype(BF16)
    send(m_sum, m_far, ms.at[2], mr.at[2], at(x, y, z, far))
    hop(1)
    landed(m_near.at[0], ms.at[0], mr.at[0])
    m_own[...] = (m32[0:64, :] + m_near[0].astype(F32)).astype(BF16)
    hop(2)
    hop(3)
    for i, (half, way, hops, buf) in enumerate(streams):
        landed(buf.at[hops - 1], zs.at[i, hops - 1], zr.at[i, hops - 1])
    total[0] = (b0[3].astype(F32) + b2[2].astype(F32) + g[0, :, :, z].astype(F32)).astype(BF16)
    total[1] = (b1[3].astype(F32) + b3[2].astype(F32) + g[1, :, :, z].astype(F32)).astype(BF16)
    for i, (dx, dy) in enumerate(PLANE):
        tx, ty = (x + dx) % NX, (y + dy) % NY
        send(total.at[:, tx, ty], kvp.at[:, x, y], ks.at[i], kr.at[i], at(tx, ty, z, t))
    own = pltpu.make_async_copy(total.at[:, x, y], kvp.at[:, x, y], ls.at[0])
    own.start()
    for e in range(1, NX):
        landed(dqa.at[e], qs.at[e], qr.at[e])
    landed(m_far, ms.at[2], mr.at[2])
    for i, (dx, dy) in enumerate(PLANE):
        fx, fy = (x + NX - dx) % NX, (y + NY - dy) % NY
        landed(kvp.at[:, fx, fy], ks.at[i], kr.at[i])
    for copy in sent:
        copy.wait_send()
    own.wait()


def reduce(dq, g, share, ox, w):
    dma = pltpu.SemaphoreType.DMA
    width = w.shape[1]
    block = (NX, NY, SUB, HD)
    return pl.pallas_call(
        reduce_kernel,
        out_shape=(
            jax.ShapeDtypeStruct(dq.shape, BF16),
            jax.ShapeDtypeStruct((2, *block), BF16),
            jax.ShapeDtypeStruct((64, width), BF16),
            jax.ShapeDtypeStruct((64, width), BF16),
        ),
        in_specs=[
            pl.BlockSpec(memory_space=ANY), *[pl.BlockSpec(memory_space=VMEM)] * 7,
        ],
        out_specs=(
            pl.BlockSpec(memory_space=ANY), pl.BlockSpec(memory_space=ANY),
            pl.BlockSpec(memory_space=VMEM), pl.BlockSpec(memory_space=ANY),
        ),
        scratch_shapes=[
            pltpu.VMEM((4, *block), BF16), pltpu.VMEM((4, *block), BF16),
            pltpu.VMEM((3, *block), BF16), pltpu.VMEM((3, *block), BF16),
            pltpu.VMEM((2, *block), BF16),
            pltpu.VMEM((2, 64, width), BF16), pltpu.VMEM((128, width), F32),
            pltpu.VMEM((2, 64, width), BF16), pltpu.VMEM((64, width), BF16),
            pltpu.VMEM((ROWS, HD), F32), pltpu.VMEM((4, TOK // 4, GROUP * HD), BF16),
            dma((4,)), dma((4,)), dma((4, 4)), dma((4, 4)), dma((7,)), dma((7,)), dma((3,)), dma((3,)), dma((1,)),
        ],
        compiler_params=pltpu.CompilerParams(
            collective_id=2, has_side_effects=True, vmem_limit_bytes=24 << 20
        ),
        name="reduce",
    )(dq, g, share, *ox, w)


def begin_of(position, lengths):
    end, first = jnp.int32(0), jnp.zeros_like(position)
    for j in range(lengths.shape[0]):
        end = end + lengths[j]
        first = jnp.where(position >= end, end, first)
    return first


def span_of(r, x, y, z, lengths, trims):
    s = ((x + NX - r) % NX) * (NY * NZ) + y * NZ + z
    start = s * TOK
    first = begin_of(start, lengths)
    f = first // TOK
    q_pos = start + lax.broadcasted_iota(jnp.int32, (1, ROWS), 1) // GROUP
    low = begin_of(q_pos, lengths)
    hide = jnp.where(low > start, jnp.float32(-LOW), jnp.float32(0.0))
    count, rest = (s - f + 1) // WIDE, (s - f + 1) % WIDE

    def tile(want, runs):
        a = jnp.minimum(want, SHARDS - runs)
        base = a * TOK + x * SUB
        whole = (a == want) & (base + (runs - 1) * TOK + SUB - 1 <= start)
        if not trims:
            whole = whole & (base >= first)
        rows = pl.ds(pl.multiple_of(a * SUB, SUB), runs * SUB)
        return rows, base, want * TOK, whole

    def walk(work):
        def step(i, _):
            rows, base, floor, whole = tile(f + WIDE * i, WIDE)
            pl.when(whole)(lambda: work(rows, WIDE, None, first - base))
            pl.when(jnp.logical_not(whole))(lambda: work(rows, WIDE, (base, floor), None))
            return 0

        wide = count + (rest > WIDE // 2).astype(jnp.int32)
        lax.fori_loop(0, wide, step, 0)
        for runs in (4, 2):
            rows, base, floor, _ = tile(f + WIDE * count, runs)
            here = (rest <= runs) & (rest > runs // 2) if runs > 2 else (rest <= runs) & (rest > 0)
            pl.when(here)(lambda: work(rows, runs, (base, floor), None))

    return walk, q_pos, low, hide


def seen(place_of, runs, q_pos, low, cols):
    base, floor = place_of
    low, high = jnp.maximum(low[:, cols], floor) - base, q_pos[:, cols] - base
    i = lax.broadcasted_iota(jnp.int32, (runs * SUB, low.shape[1]), 0)
    k_rel = i + (i // SUB) * (TOK - SUB)
    return (k_rel >= low) & (k_rel <= high)


def trim(value, skip, fill):
    head = value[0:SUB]
    i = lax.broadcasted_iota(jnp.int32, head.shape, 0)
    return jnp.concatenate([jnp.where(i >= skip, head, fill), value[SUB:]], axis=0)


def forward_kernel(lengths, q, g, kv, o0, o1, o2, o3, st, out, m, part, acc, buf, top):
    x, y, z, _ = place()

    def shard(r, _):
        walk, q_pos, low, hide = span_of(r, x, y, z, lengths, True)
        m[...] = jnp.full(m.shape, FLOOR, F32)
        part[...] = jnp.zeros(part.shape, F32)
        acc[...] = jnp.zeros(acc.shape, F32)

        def work(rows, runs, masked, skip):
            k, v = kv[0, rows, :], kv[1, rows, :]
            size = runs * SUB
            span = [slice(c * CHUNK, (c + 1) * CHUNK) for c in range(ROWS // CHUNK)]
            for cols in span:
                s = lax.dot_general(k, q[r, cols, :], NT, preferred_element_type=F32) * (SCALE * LOG2E)
                if masked is not None:
                    s = jnp.where(seen(masked, runs, q_pos, low, cols), s, LOW)
                else:
                    s = trim(s, skip, LOW)
                buf[0:size, cols] = s
                top[:, cols] = jnp.max(s.reshape(size // 8, 8, CHUNK), axis=0)
            old = m[...]
            most = jnp.max(top[...], axis=0, keepdims=True)
            new = jnp.maximum(old, most if masked is not None else most - hide)
            m[...] = new
            shrink = jnp.exp2(old - new)
            if masked is None:
                new = new + hide
            for cols in span:
                p = jnp.exp2(buf[0:size, cols] - new[:, cols])
                part[:, cols] = part[:, cols] * shrink[:, cols] + jnp.sum(
                    p.reshape(size // 8, 8, CHUNK), axis=0
                )
                acc[:, cols] = acc[:, cols] * shrink[:, cols] + lax.dot_general(
                    v, p.astype(BF16), TN, preferred_element_type=F32
                )

        walk(work)
        total = jnp.sum(part[...], axis=0, keepdims=True)
        o = (acc[...] / jnp.where(total > 0, total, 1.0)).T
        out[r] = o.astype(BF16)
        prod = o * g[r].astype(F32)
        high = prod.astype(BF16)
        rest = (prod - high.astype(F32)).astype(BF16)
        ones = jnp.ones((8, HD), BF16)
        sums = lax.dot_general(ones, high, NT, preferred_element_type=F32) + lax.dot_general(
            ones, rest, NT, preferred_element_type=F32
        )
        st[pl.ds(r, 1), :] = jnp.where(total > 0, m[...] + jnp.log2(total), LOW)
        st[pl.ds(r + NX, 1), :] = sums[0:1, :]
        return 0

    lax.fori_loop(0, NX, shard, 0)
    for e, ref in enumerate((o0, o1, o2, o3)):
        ref[...] = out[e]


def forward(lengths, q, g, kv):
    return pl.pallas_call(
        forward_kernel,
        out_shape=(jax.ShapeDtypeStruct((ROWS, HD), BF16),) * NX + (jax.ShapeDtypeStruct((2 * NX, ROWS), F32),),
        in_specs=[pl.BlockSpec(memory_space=SMEM)] + [pl.BlockSpec(memory_space=VMEM)] * 3,
        out_specs=(pl.BlockSpec(memory_space=VMEM),) * 5,
        scratch_shapes=[
            pltpu.VMEM((NX, ROWS, HD), BF16),
            pltpu.VMEM((1, ROWS), F32), pltpu.VMEM((8, ROWS), F32), pltpu.VMEM((HD, ROWS), F32),
            pltpu.VMEM((WIDE * SUB, ROWS), F32), pltpu.VMEM((8, ROWS), F32),
        ],
        compiler_params=pltpu.CompilerParams(vmem_limit_bytes=24 << 20),
        cost_estimate=pl.CostEstimate(flops=4 * 3072 * ROWS * HD, transcendentals=3072 * ROWS, bytes_accessed=8 << 20),
        name="forward",
    )(lengths, q, g, kv)


def backward_kernel(lengths, q, g, kv, st, sta, dq, dkv, share, acc, dqt, lse, delta):
    x, y, z, _ = place()
    for r in range(NX):
        tops, parts = [], []
        for e in range(NX):
            k = (r + e) % NX
            rows = st if e == 0 else sta.at[e]
            tops.append(rows[k : k + 1, :])
            parts.append(rows[NX + k : NX + k + 1, :])
        top = jnp.maximum(jnp.maximum(tops[0], tops[1]), jnp.maximum(tops[2], tops[3]))
        weights = [jnp.exp2(a - top) for a in tops]
        total = (weights[0] + weights[1]) + (weights[2] + weights[3])
        lse[r : r + 1, :] = top + jnp.log2(total)
        delta[r : r + 1, :] = sum(w * b for w, b in zip(weights, parts)) / total
        if r == 0:
            cols = [w / total for w in weights] + [jnp.zeros((8 - NX, ROWS), F32)]
            share[...] = jnp.concatenate(cols, axis=0).T
    acc[...] = jnp.zeros(acc.shape, F32)

    def shard(r, _):
        walk, q_pos, low, hide = span_of(r, x, y, z, lengths, False)
        dqt[...] = jnp.zeros(dqt.shape, F32)

        def work(rows, runs, masked, skip):
            k, v = kv[0, rows, :], kv[1, rows, :]
            dk, dv = acc[0, rows, :], acc[1, rows, :]
            for c in range(ROWS // BCHUNK):
                cols = slice(c * BCHUNK, (c + 1) * BCHUNK)
                qc, gc = q[r, cols, :], g[r, cols, :]
                s = lax.dot_general(k, qc, NT, preferred_element_type=F32) * (SCALE * LOG2E)
                if masked is None:
                    p = jnp.exp2(s - (lse[pl.ds(r, 1), cols] + hide[:, cols]))
                else:
                    p = jnp.exp2(s - lse[pl.ds(r, 1), cols])
                    p = jnp.where(seen(masked, runs, q_pos, low, cols), p, 0.0)
                dp = lax.dot_general(v, gc, NT, preferred_element_type=F32)
                ds = (p * (dp - delta[pl.ds(r, 1), cols])).astype(BF16)
                dv = dv + lax.dot_general(p.astype(BF16), gc, NN, preferred_element_type=F32)
                dk = dk + lax.dot_general(ds, qc, NN, preferred_element_type=F32)
                dqt[:, cols] = dqt[:, cols] + lax.dot_general(k, ds, TN, preferred_element_type=F32)
            acc[0, rows, :] = dk
            acc[1, rows, :] = dv

        walk(work)
        dq[r] = (dqt[...] * SCALE).T.astype(BF16)
        return 0

    lax.fori_loop(0, NX, shard, 0)

    def finish(i, _):
        rows = pl.ds(pl.multiple_of(i * 256, 256), 256)
        dkv[0, rows, :] = (acc[0, rows, :] * SCALE).astype(BF16)
        dkv[1, rows, :] = acc[1, rows, :].astype(BF16)
        return 0

    lax.fori_loop(0, SHARDS * SUB // 256, finish, 0)


def backward(lengths, q, g, kv, st, sta):
    return pl.pallas_call(
        backward_kernel,
        out_shape=(
            jax.ShapeDtypeStruct(q.shape, BF16),
            jax.ShapeDtypeStruct(kv.shape, BF16),
            jax.ShapeDtypeStruct((ROWS, 8), F32),
        ),
        in_specs=[pl.BlockSpec(memory_space=SMEM)] + [pl.BlockSpec(memory_space=VMEM)] * 5,
        out_specs=(pl.BlockSpec(memory_space=VMEM),) * 3,
        scratch_shapes=[
            pltpu.VMEM(kv.shape, F32), pltpu.VMEM((HD, ROWS), F32),
            pltpu.VMEM((NX, ROWS), F32), pltpu.VMEM((NX, ROWS), F32),
        ],
        compiler_params=pltpu.CompilerParams(vmem_limit_bytes=24 << 20),
        cost_estimate=pl.CostEstimate(flops=10 * 3072 * ROWS * HD, transcendentals=3072 * ROWS, bytes_accessed=10 << 20),
        name="backward",
    )(lengths, q, g, kv, st, sta)


def finish_kernel(dq, dqa, kvp, m_own, m_far, mixed, d_queries, d_keys, d_values):
    mixed[...] = (m_own[...].astype(F32) + m_far[...].astype(F32)).astype(BF16)
    total = dq[0].astype(F32)
    for e in range(1, NX):
        total = total + dqa[e].astype(F32)
    d_queries[...] = total.astype(BF16)
    for half, out in enumerate((d_keys, d_values)):
        for e in range(NX):
            out[SUB * e : SUB * e + SUB, :] = (
                kvp[half, e, 0].astype(F32) + kvp[half, e, 1].astype(F32)
            ).astype(BF16)


def finish(dq, dqa, kvp, m_own, m_far):
    return pl.pallas_call(
        finish_kernel,
        grid=(1,),
        out_shape=(
            jax.ShapeDtypeStruct(m_own.shape, BF16),
            jax.ShapeDtypeStruct((ROWS, HD), BF16),
            jax.ShapeDtypeStruct((TOK, HD), BF16),
            jax.ShapeDtypeStruct((TOK, HD), BF16),
        ),
        in_specs=[pl.BlockSpec((1, ROWS, HD), lambda i: (0, 0, 0))] + [pl.BlockSpec(memory_space=VMEM)] * 4,
        out_specs=(pl.BlockSpec(memory_space=VMEM),) * 4,
        compiler_params=pltpu.CompilerParams(vmem_limit_bytes=24 << 20),
        cost_estimate=pl.CostEstimate(flops=1 << 20, transcendentals=0, bytes_accessed=4 << 20),
        name="finish",
    )(dq, dqa, kvp, m_own, m_far)


def local(queries, keys, values, w_out, d_out, lengths):
    width = w_out.shape[2]
    w_flat = w_out.reshape(GROUP * HD, width)
    qa, ga, kva = gather(
        queries.reshape(ROWS, HD), keys.reshape(NX, SUB, HD), values.reshape(NX, SUB, HD), d_out, w_flat
    )
    ga = ga.reshape(NX, ROWS, HD)
    kva = kva.reshape(2, SHARDS * SUB, HD)
    *ox, st = forward(lengths, qa, ga, kva)
    sta = swap(st)
    ox[1], ox[2], ox[3], _ = lax.optimization_barrier((ox[1], ox[2], ox[3], sta))
    outer = NX * NY
    oxa = [ox[0]] + [
        lax.ppermute(ox[e], "outer", [(i, (i + outer - NY * e) % outer) for i in range(outer)])
        for e in range(1, NX)
    ]
    dq, dkv, share = backward(lengths, qa, ga, kva, st, sta)
    dqa, kvp, m_own, m_far = reduce(dq, dkv.reshape(2, NX, NY, NZ, SUB, HD), share, oxa, w_flat)
    mixed, d_queries, d_keys, d_values = finish(dq, dqa, kvp, m_own, m_far)
    return (
        mixed,
        d_queries.reshape(TOK, GROUP, HD),
        d_keys.reshape(TOK, 1, HD),
        d_values.reshape(TOK, 1, HD),
    )


def solution(mesh):
    tokens = P(("outer", "inner"), "tensor", None)
    rows = P(("outer", "inner", "tensor"), None)
    return jax.shard_map(
        local,
        mesh=mesh,
        in_specs=(tokens, tokens, tokens, P("tensor", None, None), rows, P()),
        out_specs=(rows, tokens, tokens, tokens),
        check_vma=False,
    )
```
